256 devices in a mesh: section: 32 (over z_lo, x, core), tensor: 8 (over y, z_hi).
Axes of the slice: x: 4, y: 4, z: 8 (z_hi: 2, z_lo: 4; z = z_hi * 4 + z_lo), core: 2. Of those that a mesh axis runs over, the one named last changes fastest.
Arguments:
- forward_input: bfloat16 [32, 256, 8192], P('section', None, 'tensor'), may hold values from -6 to 6
- saved_last: bfloat16 [32, 256, 8192], P('section', None, 'tensor'), may hold values from -6 to 6
- saved_first: bfloat16 [32, 256, 8192], P('section', None, 'tensor'), may hold values from -6 to 6
- first_cotangent: bfloat16 [32, 256, 8192], P('section', None, 'tensor'), may hold values from -6 to 6
- section_entry: bfloat16 [256, 8192], P(None, 'tensor'), may hold values from -6 to 6
- last_gain: float32 [32, 8192], P('section'), may hold values from 0.1 to 1.9
- last_up: bfloat16 [32, 8192, 1024], P('section', None, 'tensor'), may hold values from -0.0625 to 0.0625
- last_down: bfloat16 [32, 1024, 8192], P('section', 'tensor'), may hold values from -0.1875 to 0.1875
- first_gain: float32 [32, 8192], P('section'), may hold values from 0.1 to 1.9
- first_up: bfloat16 [32, 8192, 1024], P('section', None, 'tensor'), may hold values from -0.0625 to 0.0625
- first_down: bfloat16 [32, 1024, 8192], P('section', 'tensor'), may hold values from -0.1875 to 0.1875
- head_gain: float32 [8192], replicated, may hold values from 0.1 to 1.9
- head_weight: float32 [8192, 4], P('tensor'), may hold values from -0.0625 to 0.0625
- head_bias: float32 [4], replicated, may hold values from -3 to 3
- prompt_length: int32 [1], replicated, may hold values from 8 to 248
- keep_mask: int32 [1, 256], replicated, may hold values 0 or 1
- target_box: int32 [1, 4], replicated, may hold values from 0 to 1000, as said below
Outputs:
- layer_output: bfloat16 [32, 256, 8192], P('section', None, 'tensor')
- input_gradient: bfloat16 [32, 256, 8192], P('section', None, 'tensor')
The draws below stay inside these ranges and needn't reach their ends.
Inputs may be any that keep to these rules, and one draw needn't show every extreme that they name: `target_box`: each row is a box x1, y1, x2, y2 with x2 - x1 and y2 - y1 at least 100.
All inputs are finite; a program needn't handle non-finite values.
Results may differ from the reference program's by a relative error of at most 0.018.
Values may be sent and summed in bfloat16 or wider, within the bound.
A program may use at most 128 MiB of HBM per device.

```python
import jax
import jax.numpy as jnp
from jax import lax

D = 8192
HID = 1024
SEQ = 256
MB_ROWS = 1
TOKENS = 256
N_SECTION = 32
N_TENSOR = 8


def draw_target_box(key, part):
    key_list = jax.random.split(key, 4)
    corner_x = jnp.maximum(jax.random.randint(key_list[0], (MB_ROWS,), 0, 1000) - 100, 0)
    corner_y = jnp.maximum(jax.random.randint(key_list[1], (MB_ROWS,), 0, 1000) - 100, 0)
    extent_x = jax.random.randint(key_list[2], (MB_ROWS,), 100, 1001)
    extent_y = jax.random.randint(key_list[3], (MB_ROWS,), 100, 1001)
    far_x = jnp.minimum(corner_x + extent_x, 1000)
    far_y = jnp.minimum(corner_y + extent_y, 1000)
    return jnp.stack([corner_x, corner_y, far_x, far_y], axis=1).astype(jnp.int32)


def plant(result, stream_key, smallest, high):
    place = [jax.random.randint(jax.random.fold_in(stream_key, axis), (), 0, length) for axis, length in enumerate(result.shape)]
    longest = result.shape.index(max(result.shape))
    next_to = place[:longest] + [(place[longest] + 1) % result.shape[longest]] + place[longest + 1:]
    return result.at[tuple(place)].set(smallest).at[tuple(next_to)].set(high)


def steps_of(rng, shape, pieces, smallest, top_value):
    loudness, own = 1.0, jax.random.fold_in(rng, 6)
    for axis_at, blocks in pieces:
        heights = jnp.exp(jax.random.uniform(jax.random.fold_in(own, axis_at), (blocks,), jnp.float32, smallest / len(pieces), top_value / len(pieces)))
        loudness = loudness * jnp.repeat(heights, shape[axis_at] // blocks).reshape([-1 if axis == axis_at else 1 for axis in range(len(shape))])
    return loudness


def scatter_about(key, shape, scale, reach, cuts=(), kind=jnp.bfloat16):
    entries = scale * jax.random.normal(key, shape, jnp.float32)
    if cuts:
        entries = entries * steps_of(key, shape, cuts, -0.22, 0.18)
    return jnp.clip(entries, -reach, reach).astype(kind)


def setup_inputs(seed: int = 0) -> dict:
    key_of = jax.random.split(jax.random.key(seed), 18)
    forward_input = scatter_about(key_of[0], (N_SECTION, TOKENS, D), 1.0, 6.0, ((0, 32), (2, 8)))
    saved_last = scatter_about(key_of[1], (N_SECTION, TOKENS, D), 1.0, 6.0, ((0, 32), (2, 8)))
    saved_first = scatter_about(key_of[2], (N_SECTION, TOKENS, D), 1.0, 6.0, ((0, 32), (2, 8)))
    first_cotangent = scatter_about(key_of[3], (N_SECTION, TOKENS, D), 1.0, 6.0, ((0, 32), (2, 8)))
    section_entry = scatter_about(key_of[4], (TOKENS, D), 1.0, 6.0, ((1, 8),))
    last_gain = jnp.clip(1.0 + 0.18 * jax.random.normal(key_of[5], (N_SECTION, D), jnp.float32), 0.1, 1.9)
    last_up = scatter_about(key_of[6], (N_SECTION, D, HID), D ** -0.5, 0.0625, ((0, 32), (2, 8)))
    last_down = scatter_about(key_of[7], (N_SECTION, HID, D), HID ** -0.5, 0.1875, ((0, 32), (1, 8)))
    first_gain = jnp.clip(1.0 + 0.18 * jax.random.normal(key_of[8], (N_SECTION, D), jnp.float32), 0.1, 1.9)
    first_up = scatter_about(key_of[9], (N_SECTION, D, HID), D ** -0.5, 0.0625, ((0, 32), (2, 8)))
    first_down = scatter_about(key_of[10], (N_SECTION, HID, D), HID ** -0.5, 0.1875, ((0, 32), (1, 8)))
    head_gain = jnp.clip(1.0 + 0.18 * jax.random.normal(key_of[11], (D,), jnp.float32), 0.1, 1.9)
    head_weight = scatter_about(key_of[12], (D, 4), D ** -0.5, 0.0625, ((0, 8),), jnp.float32)
    head_bias = scatter_about(key_of[13], (4,), 1.0, 3.0, (), jnp.float32)
    prompt_length = jax.random.randint(key_of[14], (MB_ROWS,), 8, SEQ - 7).astype(jnp.int32)
    keep_mask = plant((jax.random.randint(key_of[15], (MB_ROWS, SEQ), 0, 4) < 1).astype(jnp.int32), jax.random.fold_in(key_of[15], 1), 0, 1)
    target_box = draw_target_box(jax.random.fold_in(key_of[17], 71), 0)
    return {"forward_input": forward_input, "saved_last": saved_last, "saved_first": saved_first, "first_cotangent": first_cotangent, "section_entry": section_entry, "last_gain": last_gain, "last_up": last_up, "last_down": last_down, "first_gain": first_gain, "first_up": first_up, "first_down": first_down, "head_gain": head_gain, "head_weight": head_weight, "head_bias": head_bias, "prompt_length": prompt_length, "keep_mask": keep_mask, "target_box": target_box}


epsilon = 1e-06
softness = 4.0
loss_scale = 4096.0

def unit_rows(values):
    values = values.astype(jnp.float32)
    inverse = lax.rsqrt(lax.optimization_barrier(jnp.mean(values * values, axis=-1, keepdims=True)) + epsilon)
    return (values * inverse, inverse)

def grouped_product(left, right, transpose_right):
    group_width = left.shape[1] // N_TENSOR
    out_width = right.shape[0] if transpose_right else right.shape[1]
    total_sum = jnp.zeros((left.shape[0], out_width), jnp.float32)
    for group in range(N_TENSOR):
        piece_left = left[:, group * group_width:(group + 1) * group_width]
        if transpose_right:
            piece_right = right[:, group * group_width:(group + 1) * group_width].T
        else:
            piece_right = right[group * group_width:(group + 1) * group_width, :]
        term = jnp.dot(piece_left, piece_right, preferred_element_type=jnp.float32).astype(jnp.bfloat16)
        total_sum = total_sum + lax.optimization_barrier(term).astype(jnp.float32)
    return total_sum

def layer_apply(values, gain_row, up_matrix, down_matrix):
    scaled, inverse = unit_rows(values)
    normed = (scaled * gain_row).astype(jnp.bfloat16)
    activated = jax.nn.silu(jnp.dot(normed, up_matrix, preferred_element_type=jnp.float32)).astype(jnp.bfloat16)
    return (values.astype(jnp.float32) + grouped_product(activated, down_matrix, False)).astype(jnp.bfloat16)

def layer_grad(values, cotangent, gain_row, up_matrix, down_matrix):
    scaled, inverse = unit_rows(values)
    normed = (scaled * gain_row).astype(jnp.bfloat16)
    pre_act = jnp.dot(normed, up_matrix, preferred_element_type=jnp.float32)
    act_grad = jnp.dot(cotangent, down_matrix.T, preferred_element_type=jnp.float32)
    sigmoid_pre = jax.nn.sigmoid(pre_act)
    pre_grad = (act_grad * sigmoid_pre * (1.0 + pre_act * (1.0 - sigmoid_pre))).astype(jnp.bfloat16)
    norm_grad = grouped_product(pre_grad, up_matrix, True)
    projection = lax.optimization_barrier(jnp.mean(scaled * gain_row * norm_grad, axis=-1, keepdims=True))
    return (cotangent.astype(jnp.float32) + inverse * (gain_row * norm_grad - scaled * projection)).astype(jnp.bfloat16)

def soft_min(first, second):
    return 0.5 * (first + second - jnp.sqrt((first - second) * (first - second) + softness * softness))

def soft_max(first, second):
    return 0.5 * (first + second + jnp.sqrt((first - second) * (first - second) + softness * softness))

def soft_relu(difference):
    return 0.5 * (difference + jnp.sqrt(difference * difference + softness * softness))

def box_loss(logits, target_box):
    scaled_box = jax.nn.sigmoid(logits) * 1000.0
    centre_x = scaled_box[:, 0]
    centre_y = scaled_box[:, 1]
    box_width = scaled_box[:, 2]
    box_height = scaled_box[:, 3]
    left_pred = centre_x - 0.5 * box_width
    right_pred = centre_x + 0.5 * box_width
    lower_pred = centre_y - 0.5 * box_height
    upper_pred = centre_y + 0.5 * box_height
    target = target_box.astype(jnp.float32)
    inner_width = soft_relu(soft_min(right_pred, target[:, 2]) - soft_max(left_pred, target[:, 0]))
    inner_height = soft_relu(soft_min(upper_pred, target[:, 3]) - soft_max(lower_pred, target[:, 1]))
    intersection_area = inner_width * inner_height
    target_area = (target[:, 2] - target[:, 0]) * (target[:, 3] - target[:, 1])
    union_area = box_width * box_height + target_area - intersection_area
    outer_width = soft_max(right_pred, target[:, 2]) - soft_min(left_pred, target[:, 0])
    outer_height = soft_max(upper_pred, target[:, 3]) - soft_min(lower_pred, target[:, 1])
    enclosing = outer_width * outer_height
    return loss_scale * jnp.mean(1.0 - intersection_area / union_area + (enclosing - union_area) / enclosing)

def pool_table(prompt_length, keep_mask):
    positions = jnp.arange(keep_mask.shape[1], dtype=jnp.int32)[None, :]
    starts = prompt_length[:, None]
    weights = (positions == starts - 1).astype(jnp.float32) + (positions >= starts).astype(jnp.float32) * keep_mask.astype(jnp.float32)
    return (weights, lax.optimization_barrier(jnp.sum(weights, axis=1)))

def head_value(final_hidden, head_gain, head_weight, head_bias, weights, counts, target_box):
    tokens = final_hidden.reshape(weights.shape[0], weights.shape[1], final_hidden.shape[1])
    pooled = jnp.einsum('rt,rtd->rd', weights, tokens, precision=lax.Precision.HIGHEST) / counts[:, None]
    scaled, inverse = unit_rows(pooled)
    logits = jnp.dot(scaled * head_gain, head_weight, precision=lax.Precision.HIGHEST) + head_bias
    return box_loss(logits, target_box)

def reference(forward_input, saved_last, saved_first, first_cotangent, section_entry, last_gain, last_up, last_down, first_gain, first_up, first_down, head_gain, head_weight, head_bias, prompt_length, keep_mask, target_box):
    section_count = forward_input.shape[0]
    hidden = [layer_apply(forward_input[section], last_gain[section], last_up[section], last_down[section]) for section in range(section_count)]
    outputs = []
    for section in range(section_count):
        entry = section_entry if section == 0 else hidden[section - 1]
        outputs.append(layer_apply(entry, first_gain[section], first_up[section], first_down[section]))
    weights, counts = pool_table(prompt_length, keep_mask)
    closing = section_count - 1

    def loss_of(final_hidden):
        return head_value(final_hidden, head_gain, head_weight, head_bias, weights, counts, target_box)
    loss_value, pullback = jax.vjp(loss_of, hidden[closing].astype(jnp.float32))
    head_cotangent = pullback(jnp.ones((), jnp.float32))[0].astype(jnp.bfloat16)
    gradients = []
    for section in range(section_count):
        if section == closing:
            saved = forward_input[section]
            cotangent = head_cotangent
        else:
            saved = saved_last[section]
            cotangent = layer_grad(saved_first[section + 1], first_cotangent[section + 1], first_gain[section + 1], first_up[section + 1], first_down[section + 1])
        gradients.append(layer_grad(saved, cotangent, last_gain[section], last_up[section], last_down[section]))
    return (jnp.stack(outputs), jnp.stack(gradients))
```

```python
import functools

import jax
import jax.numpy as jnp
from jax import lax
from jax.experimental import pallas as pl
from jax.experimental.pallas import tpu as pltpu
from jax.sharding import Mesh
from jax.sharding import PartitionSpec as P

epsilon = 1e-06
softness = 4.0
loss_scale = 4096.0
TENSOR = ("ty", "tz")


def shifted(value, axis, steps):
    count = lax.axis_size(axis)
    initial, last = (max(0, -steps), min(count, count - steps))
    return lax.ppermute(value, axis, [(source, source + steps) for source in range(initial, last)])


def tensor_size():
    return lax.axis_size("ty") * lax.axis_size("tz")


def tensor_index():
    return lax.axis_index("ty") * lax.axis_size("tz") + lax.axis_index("tz")


def unit_rows(values):
    values = values.astype(jnp.float32)
    inverse = lax.rsqrt(jnp.mean(values * values, axis=-1, keepdims=True) + epsilon)
    return (values * inverse, inverse)


def column_start(local_width):
    return tensor_index() * local_width


def column_slice(full_rows, local_width):
    return lax.dynamic_slice_in_dim(full_rows, column_start(local_width), local_width, 1)


MESH_ID = pl.DeviceIdType.MESH


def gather_kernel(ny, nz, x_ref, out_ref, send_sems, recv_sems):
    width = x_ref.shape[2]
    ty, tz = lax.axis_index("ty"), lax.axis_index("tz")
    me = ty * nz + tz
    partner_z = 1 - tz
    partner = ty * nz + partner_z
    y_peers = [lax.rem(ty + step, ny) for step in range(1, ny)]
    section = lax.axis_index("section")

    def device(y, z):
        return (section, y, z)

    def cols(index):
        return pl.ds(pl.multiple_of(index * width, width), width)

    barrier = pltpu.get_barrier_semaphore()
    pl.semaphore_signal(barrier, inc=1, device_id=device(ty, partner_z), device_id_type=MESH_ID)
    for y in y_peers:
        pl.semaphore_signal(barrier, inc=1, device_id=device(y, tz), device_id_type=MESH_ID)
    pl.semaphore_wait(barrier, ny)

    sends = [
        pltpu.make_async_remote_copy(
            src_ref=x_ref,
            dst_ref=out_ref.at[:, :, cols(me)],
            send_sem=send_sems.at[0],
            recv_sem=recv_sems.at[me],
            device_id=device(ty, partner_z),
            device_id_type=MESH_ID,
        )
    ]
    for number, y in enumerate(y_peers):
        sends.append(
            pltpu.make_async_remote_copy(
                src_ref=x_ref,
                dst_ref=out_ref.at[:, :, cols(me)],
                send_sem=send_sems.at[1 + number],
                recv_sem=recv_sems.at[me],
                device_id=device(y, tz),
                device_id_type=MESH_ID,
            )
        )
    for copy in sends:
        copy.start()
    out_ref[:, :, cols(me)] = x_ref[...]
    pltpu.make_async_remote_copy(
        src_ref=x_ref,
        dst_ref=out_ref.at[:, :, cols(partner)],
        send_sem=send_sems.at[0],
        recv_sem=recv_sems.at[partner],
        device_id=device(ty, partner_z),
        device_id_type=MESH_ID,
    ).wait_recv()
    forwards = []
    for number, y in enumerate(y_peers):
        forwards.append(
            pltpu.make_async_remote_copy(
                src_ref=out_ref.at[:, :, cols(partner)],
                dst_ref=out_ref.at[:, :, cols(partner)],
                send_sem=send_sems.at[ny + number],
                recv_sem=recv_sems.at[partner],
                device_id=device(y, tz),
                device_id_type=MESH_ID,
            )
        )
    for copy in forwards:
        copy.start()
    for y in y_peers:
        for z in range(nz):
            source = y * nz + z
            pltpu.make_async_remote_copy(
                src_ref=x_ref,
                dst_ref=out_ref.at[:, :, cols(source)],
                send_sem=send_sems.at[0],
                recv_sem=recv_sems.at[source],
                device_id=device(y, z),
                device_id_type=MESH_ID,
            ).wait_recv()
    for copy in sends + forwards:
        copy.wait_send()


def gather_columns(local_rows, collective):
    k, rows, width = local_rows.shape
    ny, nz = lax.axis_size("ty"), lax.axis_size("tz")
    full = width * ny * nz
    moved = local_rows.size * local_rows.dtype.itemsize * 7
    return pl.pallas_call(
        functools.partial(gather_kernel, ny, nz),
        out_shape=jax.ShapeDtypeStruct((k, rows, full), local_rows.dtype),
        in_specs=[pl.BlockSpec(memory_space=pltpu.VMEM)],
        out_specs=pl.BlockSpec(memory_space=pltpu.VMEM),
        scratch_shapes=[
            pltpu.SemaphoreType.DMA((2 * ny - 1,)),
            pltpu.SemaphoreType.DMA((ny * nz,)),
        ],
        compiler_params=pltpu.CompilerParams(
            collective_id=collective, has_side_effects=True, vmem_limit_bytes=48 * 1024 * 1024
        ),
        cost_estimate=pl.CostEstimate(flops=0, transcendentals=0, bytes_accessed=moved),
    )(local_rows)


def scatter_kernel(ny, nz, part_ref, out_ref, stage, z_send, z_recv, send_sems, recv_sems, z_sems):
    k, rows, width = out_ref.shape
    pair = nz * width
    ty, tz = lax.axis_index("ty"), lax.axis_index("tz")
    partner_z = 1 - tz
    section = lax.axis_index("section")
    chunk = 32

    def device(y, z):
        return (section, y, z)

    barrier = pltpu.get_barrier_semaphore()
    pl.semaphore_signal(barrier, inc=1, device_id=device(ty, partner_z), device_id_type=MESH_ID)
    for step in range(1, ny):
        pl.semaphore_signal(
            barrier, inc=1, device_id=device(lax.rem(ty + step, ny), tz), device_id_type=MESH_ID
        )
    pl.semaphore_wait(barrier, ny)

    sends = []
    for step in range(1, ny):
        peer = lax.rem(ty + step, ny)
        copy = pltpu.make_async_remote_copy(
            src_ref=part_ref.at[:, :, pl.ds(pl.multiple_of(peer * pair, pair), pair)],
            dst_ref=stage.at[ny - step - 1],
            send_sem=send_sems.at[step - 1],
            recv_sem=recv_sems.at[ny - step - 1],
            device_id=device(peer, tz),
            device_id_type=MESH_ID,
        )
        copy.start()
        sends.append(copy)
    for slot in range(ny - 1):
        pltpu.make_async_remote_copy(
            src_ref=stage.at[slot],
            dst_ref=stage.at[slot],
            send_sem=send_sems.at[0],
            recv_sem=recv_sems.at[slot],
            device_id=device(ty, partner_z),
            device_id_type=MESH_ID,
        ).wait_recv()

    def add_terms(z, target):
        own = pl.multiple_of((ty * nz + z) * width, width)
        inside = pl.multiple_of(z * width, width)

        def body(step, carry):
            plane = step // (rows // chunk)
            row = pl.multiple_of((step % (rows // chunk)) * chunk, chunk)
            total = part_ref[plane, pl.ds(row, chunk), pl.ds(own, width)].astype(jnp.float32)
            for slot in range(ny - 1):
                total += stage[slot, plane, pl.ds(row, chunk), pl.ds(inside, width)].astype(
                    jnp.float32
                )
            target(plane, row, total)
            return carry

        lax.fori_loop(0, k * (rows // chunk), body, 0)

    def to_send(plane, row, total):
        z_send[plane, pl.ds(row, chunk), :] = total

    add_terms(partner_z, to_send)
    z_copy = pltpu.make_async_remote_copy(
        src_ref=z_send,
        dst_ref=z_recv,
        send_sem=z_sems.at[0],
        recv_sem=z_sems.at[1],
        device_id=device(ty, partner_z),
        device_id_type=MESH_ID,
    )
    z_copy.start()

    def to_out(plane, row, total):
        out_ref[plane, pl.ds(row, chunk), :] = total

    add_terms(tz, to_out)
    z_copy.wait_recv()
    out_ref[...] += z_recv[...]
    z_copy.wait_send()
    for copy in sends:
        copy.wait_send()


def reduce_columns(partial_rows, collective):
    k, rows, full = partial_rows.shape
    ny, nz = lax.axis_size("ty"), lax.axis_size("tz")
    width = full // (ny * nz)
    terms = partial_rows.astype(jnp.bfloat16)
    moved = terms.size * 2
    return pl.pallas_call(
        functools.partial(scatter_kernel, ny, nz),
        out_shape=jax.ShapeDtypeStruct((k, rows, width), jnp.float32),
        in_specs=[pl.BlockSpec(memory_space=pltpu.VMEM)],
        out_specs=pl.BlockSpec(memory_space=pltpu.VMEM),
        scratch_shapes=[
            pltpu.VMEM((ny - 1, k, rows, nz * width), jnp.bfloat16),
            pltpu.VMEM((k, rows, width), jnp.float32),
            pltpu.VMEM((k, rows, width), jnp.float32),
            pltpu.SemaphoreType.DMA((ny - 1,)),
            pltpu.SemaphoreType.DMA((ny - 1,)),
            pltpu.SemaphoreType.DMA((2,)),
        ],
        compiler_params=pltpu.CompilerParams(
            collective_id=collective, has_side_effects=True, vmem_limit_bytes=56 * 1024 * 1024
        ),
        cost_estimate=pl.CostEstimate(flops=terms.size, transcendentals=0, bytes_accessed=moved),
    )(terms)


def row_sums(values):
    return lax.psum(values, TENSOR)


def layer_core(full_rows, gain_row, up_matrix, down_matrix):
    scaled, inverse = unit_rows(full_rows)
    normed = (scaled * gain_row).astype(jnp.bfloat16)
    activated = jax.nn.silu(jnp.dot(normed, up_matrix, preferred_element_type=jnp.float32)).astype(
        jnp.bfloat16
    )
    return jnp.dot(activated, down_matrix, preferred_element_type=jnp.float32)


def backward_core(saved_full, cotangent_full, gain_row, up_matrix, down_matrix):
    scaled, inverse = unit_rows(saved_full)
    normed = (scaled * gain_row).astype(jnp.bfloat16)
    pre_act = jnp.dot(normed, up_matrix, preferred_element_type=jnp.float32)
    act_grad = lax.dot_general(
        cotangent_full, down_matrix, (((1,), (1,)), ((), ())), preferred_element_type=jnp.float32
    )
    sigmoid_pre = jax.nn.sigmoid(pre_act)
    pre_grad = (act_grad * sigmoid_pre * (1.0 + pre_act * (1.0 - sigmoid_pre))).astype(jnp.bfloat16)
    norm_partial = lax.dot_general(
        pre_grad, up_matrix, (((1,), (1,)), ((), ())), preferred_element_type=jnp.float32
    )
    return norm_partial, scaled, inverse


def backward_finish(cotangent, norm_grad, scaled, inverse, gain_row):
    local_width = cotangent.shape[1]
    full_width = scaled.shape[1]
    scaled_cols = column_slice(scaled, local_width)
    gain_cols = lax.dynamic_slice_in_dim(gain_row, column_start(local_width), local_width, 0)
    row_total = row_sums(jnp.sum(scaled_cols * gain_cols * norm_grad, axis=1))
    result = cotangent.astype(jnp.float32) + inverse * (
        gain_cols * norm_grad - scaled_cols * row_total[:, None] / full_width
    )
    return result.astype(jnp.bfloat16)

def soft_min(first, second):
    return 0.5 * (
        first + second - jnp.sqrt((first - second) * (first - second) + softness * softness)
    )


def soft_max(first, second):
    return 0.5 * (
        first + second + jnp.sqrt((first - second) * (first - second) + softness * softness)
    )


def soft_relu(difference):
    return 0.5 * (difference + jnp.sqrt(difference * difference + softness * softness))


def box_loss(logits, target_box):
    scaled_box = jax.nn.sigmoid(logits) * 1000.0
    centre_x = scaled_box[:, 0]
    centre_y = scaled_box[:, 1]
    box_width = scaled_box[:, 2]
    box_height = scaled_box[:, 3]
    left_pred = centre_x - 0.5 * box_width
    right_pred = centre_x + 0.5 * box_width
    lower_pred = centre_y - 0.5 * box_height
    upper_pred = centre_y + 0.5 * box_height
    target = target_box.astype(jnp.float32)
    inner_width = soft_relu(soft_min(right_pred, target[:, 2]) - soft_max(left_pred, target[:, 0]))
    inner_height = soft_relu(
        soft_min(upper_pred, target[:, 3]) - soft_max(lower_pred, target[:, 1])
    )
    intersection_area = inner_width * inner_height
    target_area = (target[:, 2] - target[:, 0]) * (target[:, 3] - target[:, 1])
    union_area = box_width * box_height + target_area - intersection_area
    outer_width = soft_max(right_pred, target[:, 2]) - soft_min(left_pred, target[:, 0])
    outer_height = soft_max(upper_pred, target[:, 3]) - soft_min(lower_pred, target[:, 1])
    enclosing = outer_width * outer_height
    return loss_scale * jnp.mean(
        1.0 - intersection_area / union_area + (enclosing - union_area) / enclosing
    )


def head_cotangent(
    final_rows, head_gain, head_weight, head_bias, prompt_length, keep_mask, target_box
):
    row_count = keep_mask.shape[0]
    positions = jnp.arange(keep_mask.shape[1], dtype=jnp.int32)[None, :]
    starts = prompt_length[:, None]
    weights = (positions == starts - 1).astype(jnp.float32) + (positions >= starts).astype(
        jnp.float32
    ) * keep_mask.astype(jnp.float32)
    counts = jnp.sum(weights, axis=1)
    local_width = final_rows.shape[1]
    full_width = local_width * tensor_size()
    tokens = final_rows.astype(jnp.float32).reshape(row_count, keep_mask.shape[1], local_width)
    pooled = (
        jnp.einsum("rt,rtd->rd", weights, tokens, precision=lax.Precision.HIGHEST) / counts[:, None]
    )
    gain_cols = lax.dynamic_slice_in_dim(head_gain, column_start(local_width), local_width, 0)
    logit_part = jnp.dot(pooled * gain_cols, head_weight, precision=lax.Precision.HIGHEST)
    square_part = jnp.sum(pooled * pooled, axis=1, keepdims=True)
    totals = row_sums(jnp.concatenate([logit_part, square_part], axis=1))
    inverse = lax.rsqrt(totals[:, 4] / full_width + epsilon)
    logits = totals[:, :4] * inverse[:, None] + head_bias

    def loss_of(logit_value):
        return box_loss(logit_value, target_box)

    loss_value, pullback = jax.vjp(loss_of, logits)
    logit_grad = pullback(jnp.ones((), jnp.float32))[0]
    scaled_grad = jnp.dot(logit_grad, head_weight.T, precision=lax.Precision.HIGHEST)
    unit_pooled = pooled * inverse[:, None]
    row_total = row_sums(jnp.sum(unit_pooled * gain_cols * scaled_grad, axis=1))
    pooled_grad = inverse[:, None] * (
        gain_cols * scaled_grad - unit_pooled * row_total[:, None] / full_width
    )
    token_grad = (weights / counts[:, None])[:, :, None] * pooled_grad[:, None, :]
    return token_grad.reshape(final_rows.shape[0], local_width).astype(jnp.bfloat16)


def per_device(
    forward_input,
    saved_last,
    saved_first,
    first_cotangent,
    section_entry,
    last_gain,
    last_up,
    last_down,
    first_gain,
    first_up,
    first_down,
    head_gain,
    head_weight,
    head_bias,
    prompt_length,
    keep_mask,
    target_box,
):
    section_index = lax.axis_index("section")
    opening = section_index == 0
    closing = section_index == lax.axis_size("section") - 1
    local_input = forward_input[0]
    closing_saved = jnp.where(closing, local_input, saved_last[0])
    gathered_input = gather_columns(local_input[None], 0)[0]
    stored = gather_columns(jnp.stack([saved_first[0], first_cotangent[0], closing_saved]), 1)
    last_partial = layer_core(gathered_input, last_gain[0], last_up[0], last_down[0])
    first_norm_partial, first_scaled, first_inverse = backward_core(
        stored[0], stored[1], first_gain[0], first_up[0], first_down[0]
    )
    reduced = reduce_columns(jnp.stack([last_partial, first_norm_partial]), 3)
    hidden_local = (local_input.astype(jnp.float32) + reduced[0]).astype(jnp.bfloat16)
    first_grad = backward_finish(
        first_cotangent[0], reduced[1], first_scaled, first_inverse, first_gain[0]
    )
    arrived_local = shifted(hidden_local, "section", 1)
    returned = shifted(first_grad, "section", -1)
    head_grad = head_cotangent(
        hidden_local, head_gain, head_weight, head_bias, prompt_length, keep_mask, target_box
    )
    entry_local = jnp.where(opening, section_entry, arrived_local)
    cotangent = jnp.where(closing, head_grad, returned)
    arrived = gather_columns(jnp.stack([entry_local, cotangent]), 2)
    first_partial = layer_core(arrived[0], first_gain[0], first_up[0], first_down[0])
    last_norm_partial, last_scaled, last_inverse = backward_core(
        stored[2], arrived[1], last_gain[0], last_up[0], last_down[0]
    )
    reduced_late = reduce_columns(jnp.stack([first_partial, last_norm_partial]), 4)
    layer_output = (entry_local.astype(jnp.float32) + reduced_late[0]).astype(jnp.bfloat16)
    input_gradient = backward_finish(
        cotangent, reduced_late[1], last_scaled, last_inverse, last_gain[0]
    )
    return (layer_output[None], input_gradient[None])


def solution(mesh):
    sections = mesh.shape["section"]
    tensors = mesh.shape["tensor"]
    split = Mesh(mesh.devices.reshape(sections, tensors // 2, 2), ("section", "ty", "tz"))
    rows = P("section", None, TENSOR)
    placed = (
        rows,
        rows,
        rows,
        rows,
        P(None, TENSOR),
        P("section", None),
        rows,
        P("section", TENSOR, None),
        P("section", None),
        rows,
        P("section", TENSOR, None),
        P(),
        P(TENSOR, None),
        P(),
        P(),
        P(),
        P(),
    )
    return jax.shard_map(
        per_device,
        mesh=split,
        in_specs=placed,
        out_specs=(rows, rows),
        check_vma=False,
    )
```

```python
import functools

import jax
import jax.numpy as jnp
from jax import lax
from jax.experimental import pallas as pl
from jax.experimental.pallas import tpu as pltpu
from jax.sharding import Mesh
from jax.sharding import PartitionSpec as P

epsilon = 1e-06
softness = 4.0
loss_scale = 4096.0
TENSOR = ("ty", "tz")


def shifted(value, axis, steps):
    count = lax.axis_size(axis)
    initial, last = (max(0, -steps), min(count, count - steps))
    return lax.ppermute(value, axis, [(source, source + steps) for source in range(initial, last)])


def tensor_size():
    return lax.axis_size("ty") * lax.axis_size("tz")


def tensor_index():
    return lax.axis_index("ty") * lax.axis_size("tz") + lax.axis_index("tz")


def unit_rows(values):
    values = values.astype(jnp.float32)
    inverse = lax.rsqrt(jnp.mean(values * values, axis=-1, keepdims=True) + epsilon)
    return (values * inverse, inverse)


def column_start(local_width):
    return tensor_index() * local_width


def column_slice(full_rows, local_width):
    return lax.dynamic_slice_in_dim(full_rows, column_start(local_width), local_width, 1)


MESH_ID = pl.DeviceIdType.MESH


def gather_kernel(ny, nz, x_ref, out_ref, send_sems, recv_sems):
    width = x_ref.shape[2]
    ty, tz = lax.axis_index("ty"), lax.axis_index("tz")
    me = ty * nz + tz
    partner_z = 1 - tz
    partner = ty * nz + partner_z
    y_peers = [lax.rem(ty + step, ny) for step in range(1, ny)]
    section = lax.axis_index("section")

    def device(y, z):
        return (section, y, z)

    def cols(index):
        return pl.ds(pl.multiple_of(index * width, width), width)

    barrier = pltpu.get_barrier_semaphore()
    pl.semaphore_signal(barrier, inc=1, device_id=device(ty, partner_z), device_id_type=MESH_ID)
    for y in y_peers:
        pl.semaphore_signal(barrier, inc=1, device_id=device(y, tz), device_id_type=MESH_ID)
    pl.semaphore_wait(barrier, ny)

    sends = [
        pltpu.make_async_remote_copy(
            src_ref=x_ref,
            dst_ref=out_ref.at[:, :, cols(me)],
            send_sem=send_sems.at[0],
            recv_sem=recv_sems.at[me],
            device_id=device(ty, partner_z),
            device_id_type=MESH_ID,
        )
    ]
    for number, y in enumerate(y_peers):
        sends.append(
            pltpu.make_async_remote_copy(
                src_ref=x_ref,
                dst_ref=out_ref.at[:, :, cols(me)],
                send_sem=send_sems.at[1 + number],
                recv_sem=recv_sems.at[me],
                device_id=device(y, tz),
                device_id_type=MESH_ID,
            )
        )
    for copy in sends:
        copy.start()
    out_ref[:, :, cols(me)] = x_ref[...]
    pltpu.make_async_remote_copy(
        src_ref=x_ref,
        dst_ref=out_ref.at[:, :, cols(partner)],
        send_sem=send_sems.at[0],
        recv_sem=recv_sems.at[partner],
        device_id=device(ty, partner_z),
        device_id_type=MESH_ID,
    ).wait_recv()
    forwards = []
    for number, y in enumerate(y_peers):
        forwards.append(
            pltpu.make_async_remote_copy(
                src_ref=out_ref.at[:, :, cols(partner)],
                dst_ref=out_ref.at[:, :, cols(partner)],
                send_sem=send_sems.at[ny + number],
                recv_sem=recv_sems.at[partner],
                device_id=device(y, tz),
                device_id_type=MESH_ID,
            )
        )
    for copy in forwards:
        copy.start()
    for y in y_peers:
        for z in range(nz):
            source = y * nz + z
            pltpu.make_async_remote_copy(
                src_ref=x_ref,
                dst_ref=out_ref.at[:, :, cols(source)],
                send_sem=send_sems.at[0],
                recv_sem=recv_sems.at[source],
                device_id=device(y, z),
                device_id_type=MESH_ID,
            ).wait_recv()
    for copy in sends + forwards:
        copy.wait_send()


def gather_columns(local_rows, collective):
    k, rows, width = local_rows.shape
    ny, nz = lax.axis_size("ty"), lax.axis_size("tz")
    full = width * ny * nz
    moved = local_rows.size * local_rows.dtype.itemsize * 7
    return pl.pallas_call(
        functools.partial(gather_kernel, ny, nz),
        out_shape=jax.ShapeDtypeStruct((k, rows, full), local_rows.dtype),
        in_specs=[pl.BlockSpec(memory_space=pltpu.VMEM)],
        out_specs=pl.BlockSpec(memory_space=pltpu.VMEM),
        scratch_shapes=[
            pltpu.SemaphoreType.DMA((2 * ny - 1,)),
            pltpu.SemaphoreType.DMA((ny * nz,)),
        ],
        compiler_params=pltpu.CompilerParams(
            collective_id=collective, has_side_effects=True, vmem_limit_bytes=48 * 1024 * 1024
        ),
        cost_estimate=pl.CostEstimate(flops=0, transcendentals=0, bytes_accessed=moved),
    )(local_rows)


def scatter_kernel(ny, nz, part_ref, out_ref, stage, z_send, z_recv, send_sems, recv_sems, z_sems):
    k, rows, width = out_ref.shape
    pair = nz * width
    ty, tz = lax.axis_index("ty"), lax.axis_index("tz")
    partner_z = 1 - tz
    section = lax.axis_index("section")
    chunk = 32

    def device(y, z):
        return (section, y, z)

    barrier = pltpu.get_barrier_semaphore()
    pl.semaphore_signal(barrier, inc=1, device_id=device(ty, partner_z), device_id_type=MESH_ID)
    for step in range(1, ny):
        pl.semaphore_signal(
            barrier, inc=1, device_id=device(lax.rem(ty + step, ny), tz), device_id_type=MESH_ID
        )
    pl.semaphore_wait(barrier, ny)

    sends = []
    for step in range(1, ny):
        peer = lax.rem(ty + step, ny)
        copy = pltpu.make_async_remote_copy(
            src_ref=part_ref.at[:, :, pl.ds(pl.multiple_of(peer * pair, pair), pair)],
            dst_ref=stage.at[ny - step - 1],
            send_sem=send_sems.at[step - 1],
            recv_sem=recv_sems.at[ny - step - 1],
            device_id=device(peer, tz),
            device_id_type=MESH_ID,
        )
        copy.start()
        sends.append(copy)
    for slot in range(ny - 1):
        pltpu.make_async_remote_copy(
            src_ref=stage.at[slot],
            dst_ref=stage.at[slot],
            send_sem=send_sems.at[0],
            recv_sem=recv_sems.at[slot],
            device_id=device(ty, partner_z),
            device_id_type=MESH_ID,
        ).wait_recv()

    def add_terms(z, target):
        own = pl.multiple_of((ty * nz + z) * width, width)
        inside = pl.multiple_of(z * width, width)

        def body(step, carry):
            plane = step // (rows // chunk)
            row = pl.multiple_of((step % (rows // chunk)) * chunk, chunk)
            total = part_ref[plane, pl.ds(row, chunk), pl.ds(own, width)].astype(jnp.float32)
            for slot in range(ny - 1):
                total += stage[slot, plane, pl.ds(row, chunk), pl.ds(inside, width)].astype(
                    jnp.float32
                )
            target(plane, row, total)
            return carry

        lax.fori_loop(0, k * (rows // chunk), body, 0)

    def to_send(plane, row, total):
        z_send[plane, pl.ds(row, chunk), :] = total

    add_terms(partner_z, to_send)
    z_copy = pltpu.make_async_remote_copy(
        src_ref=z_send,
        dst_ref=z_recv,
        send_sem=z_sems.at[0],
        recv_sem=z_sems.at[1],
        device_id=device(ty, partner_z),
        device_id_type=MESH_ID,
    )
    z_copy.start()

    def to_out(plane, row, total):
        out_ref[plane, pl.ds(row, chunk), :] = total

    add_terms(tz, to_out)
    z_copy.wait_recv()
    out_ref[...] += z_recv[...]
    z_copy.wait_send()
    for copy in sends:
        copy.wait_send()


def reduce_columns(partial_rows, collective):
    k, rows, full = partial_rows.shape
    ny, nz = lax.axis_size("ty"), lax.axis_size("tz")
    width = full // (ny * nz)
    terms = partial_rows.astype(jnp.bfloat16)
    moved = terms.size * 2
    return pl.pallas_call(
        functools.partial(scatter_kernel, ny, nz),
        out_shape=jax.ShapeDtypeStruct((k, rows, width), jnp.float32),
        in_specs=[pl.BlockSpec(memory_space=pltpu.VMEM)],
        out_specs=pl.BlockSpec(memory_space=pltpu.VMEM),
        scratch_shapes=[
            pltpu.VMEM((ny - 1, k, rows, nz * width), jnp.bfloat16),
            pltpu.VMEM((k, rows, width), jnp.float32),
            pltpu.VMEM((k, rows, width), jnp.float32),
            pltpu.SemaphoreType.DMA((ny - 1,)),
            pltpu.SemaphoreType.DMA((ny - 1,)),
            pltpu.SemaphoreType.DMA((2,)),
        ],
        compiler_params=pltpu.CompilerParams(
            collective_id=collective, has_side_effects=True, vmem_limit_bytes=56 * 1024 * 1024
        ),
        cost_estimate=pl.CostEstimate(flops=terms.size, transcendentals=0, bytes_accessed=moved),
    )(terms)


def sum_kernel(ny, nz, v_ref, out_ref, slots, send_sems, recv_sems):
    ty, tz = lax.axis_index("ty"), lax.axis_index("tz")
    me = ty * nz + tz
    section = lax.axis_index("section")
    peers = [(lax.rem(ty + dy, ny), lax.rem(tz + dz, nz)) for dy in range(ny) for dz in range(nz)][1:]

    barrier = pltpu.get_barrier_semaphore()
    for y, z in peers:
        pl.semaphore_signal(barrier, inc=1, device_id=(section, y, z), device_id_type=MESH_ID)
    pl.semaphore_wait(barrier, len(peers))
    sends = []
    for number, (y, z) in enumerate(peers):
        copy = pltpu.make_async_remote_copy(
            src_ref=v_ref,
            dst_ref=slots.at[me],
            send_sem=send_sems.at[number],
            recv_sem=recv_sems.at[me],
            device_id=(section, y, z),
            device_id_type=MESH_ID,
        )
        copy.start()
        sends.append(copy)
    slots[me] = v_ref[...]
    for y, z in peers:
        source = y * nz + z
        pltpu.make_async_remote_copy(
            src_ref=v_ref,
            dst_ref=slots.at[source],
            send_sem=send_sems.at[0],
            recv_sem=recv_sems.at[source],
            device_id=(section, y, z),
            device_id_type=MESH_ID,
        ).wait_recv()
    total = slots[0]
    for source in range(1, ny * nz):
        total = total + slots[source]
    out_ref[...] = total
    for copy in sends:
        copy.wait_send()


def row_sums(values, collective):
    shape = values.shape
    flat = values.reshape(-1).astype(jnp.float32)
    lanes = 128
    padded = -(-flat.shape[0] // lanes) * lanes
    rows = jnp.pad(flat, (0, padded - flat.shape[0])).reshape(padded // lanes, lanes)
    ny, nz = lax.axis_size("ty"), lax.axis_size("tz")
    summed = pl.pallas_call(
        functools.partial(sum_kernel, ny, nz),
        out_shape=jax.ShapeDtypeStruct(rows.shape, jnp.float32),
        in_specs=[pl.BlockSpec(memory_space=pltpu.VMEM)],
        out_specs=pl.BlockSpec(memory_space=pltpu.VMEM),
        scratch_shapes=[
            pltpu.VMEM((ny * nz,) + rows.shape, jnp.float32),
            pltpu.SemaphoreType.DMA((ny * nz - 1,)),
            pltpu.SemaphoreType.DMA((ny * nz,)),
        ],
        compiler_params=pltpu.CompilerParams(collective_id=collective, has_side_effects=True),
        cost_estimate=pl.CostEstimate(flops=rows.size * 8, transcendentals=0, bytes_accessed=rows.size * 64),
    )(rows)
    return summed.reshape(-1)[: flat.shape[0]].reshape(shape)


def layer_core(full_rows, gain_row, up_matrix, down_matrix):
    scaled, inverse = unit_rows(full_rows)
    normed = (scaled * gain_row).astype(jnp.bfloat16)
    activated = jax.nn.silu(jnp.dot(normed, up_matrix, preferred_element_type=jnp.float32)).astype(
        jnp.bfloat16
    )
    return jnp.dot(activated, down_matrix, preferred_element_type=jnp.float32)


def backward_core(saved_full, cotangent_full, gain_row, up_matrix, down_matrix):
    scaled, inverse = unit_rows(saved_full)
    normed = (scaled * gain_row).astype(jnp.bfloat16)
    pre_act = jnp.dot(normed, up_matrix, preferred_element_type=jnp.float32)
    act_grad = lax.dot_general(
        cotangent_full, down_matrix, (((1,), (1,)), ((), ())), preferred_element_type=jnp.float32
    )
    sigmoid_pre = jax.nn.sigmoid(pre_act)
    pre_grad = (act_grad * sigmoid_pre * (1.0 + pre_act * (1.0 - sigmoid_pre))).astype(jnp.bfloat16)
    norm_partial = lax.dot_general(
        pre_grad, up_matrix, (((1,), (1,)), ((), ())), preferred_element_type=jnp.float32
    )
    return norm_partial, scaled, inverse


def backward_finish(cotangent, norm_grad, scaled, inverse, gain_row, collective):
    local_width = cotangent.shape[1]
    full_width = scaled.shape[1]
    scaled_cols = column_slice(scaled, local_width)
    gain_cols = lax.dynamic_slice_in_dim(gain_row, column_start(local_width), local_width, 0)
    row_total = row_sums(jnp.sum(scaled_cols * gain_cols * norm_grad, axis=1), collective)
    result = cotangent.astype(jnp.float32) + inverse * (
        gain_cols * norm_grad - scaled_cols * row_total[:, None] / full_width
    )
    return result.astype(jnp.bfloat16)

def soft_min(first, second):
    return 0.5 * (
        first + second - jnp.sqrt((first - second) * (first - second) + softness * softness)
    )


def soft_max(first, second):
    return 0.5 * (
        first + second + jnp.sqrt((first - second) * (first - second) + softness * softness)
    )


def soft_relu(difference):
    return 0.5 * (difference + jnp.sqrt(difference * difference + softness * softness))


def box_loss(logits, target_box):
    scaled_box = jax.nn.sigmoid(logits) * 1000.0
    centre_x = scaled_box[:, 0]
    centre_y = scaled_box[:, 1]
    box_width = scaled_box[:, 2]
    box_height = scaled_box[:, 3]
    left_pred = centre_x - 0.5 * box_width
    right_pred = centre_x + 0.5 * box_width
    lower_pred = centre_y - 0.5 * box_height
    upper_pred = centre_y + 0.5 * box_height
    target = target_box.astype(jnp.float32)
    inner_width = soft_relu(soft_min(right_pred, target[:, 2]) - soft_max(left_pred, target[:, 0]))
    inner_height = soft_relu(
        soft_min(upper_pred, target[:, 3]) - soft_max(lower_pred, target[:, 1])
    )
    intersection_area = inner_width * inner_height
    target_area = (target[:, 2] - target[:, 0]) * (target[:, 3] - target[:, 1])
    union_area = box_width * box_height + target_area - intersection_area
    outer_width = soft_max(right_pred, target[:, 2]) - soft_min(left_pred, target[:, 0])
    outer_height = soft_max(upper_pred, target[:, 3]) - soft_min(lower_pred, target[:, 1])
    enclosing = outer_width * outer_height
    return loss_scale * jnp.mean(
        1.0 - intersection_area / union_area + (enclosing - union_area) / enclosing
    )


def head_cotangent(
    final_rows, head_gain, head_weight, head_bias, prompt_length, keep_mask, target_box
):
    row_count = keep_mask.shape[0]
    positions = jnp.arange(keep_mask.shape[1], dtype=jnp.int32)[None, :]
    starts = prompt_length[:, None]
    weights = (positions == starts - 1).astype(jnp.float32) + (positions >= starts).astype(
        jnp.float32
    ) * keep_mask.astype(jnp.float32)
    counts = jnp.sum(weights, axis=1)
    local_width = final_rows.shape[1]
    full_width = local_width * tensor_size()
    tokens = final_rows.astype(jnp.float32).reshape(row_count, keep_mask.shape[1], local_width)
    pooled = (
        jnp.einsum("rt,rtd->rd", weights, tokens, precision=lax.Precision.HIGHEST) / counts[:, None]
    )
    gain_cols = lax.dynamic_slice_in_dim(head_gain, column_start(local_width), local_width, 0)
    logit_part = jnp.dot(pooled * gain_cols, head_weight, precision=lax.Precision.HIGHEST)
    square_part = jnp.sum(pooled * pooled, axis=1, keepdims=True)
    totals = row_sums(jnp.concatenate([logit_part, square_part], axis=1), 5)
    inverse = lax.rsqrt(totals[:, 4] / full_width + epsilon)
    logits = totals[:, :4] * inverse[:, None] + head_bias

    def loss_of(logit_value):
        return box_loss(logit_value, target_box)

    loss_value, pullback = jax.vjp(loss_of, logits)
    logit_grad = pullback(jnp.ones((), jnp.float32))[0]
    scaled_grad = jnp.dot(logit_grad, head_weight.T, precision=lax.Precision.HIGHEST)
    unit_pooled = pooled * inverse[:, None]
    row_total = row_sums(jnp.sum(unit_pooled * gain_cols * scaled_grad, axis=1), 6)
    pooled_grad = inverse[:, None] * (
        gain_cols * scaled_grad - unit_pooled * row_total[:, None] / full_width
    )
    token_grad = (weights / counts[:, None])[:, :, None] * pooled_grad[:, None, :]
    return token_grad.reshape(final_rows.shape[0], local_width).astype(jnp.bfloat16)


def per_device(
    forward_input,
    saved_last,
    saved_first,
    first_cotangent,
    section_entry,
    last_gain,
    last_up,
    last_down,
    first_gain,
    first_up,
    first_down,
    head_gain,
    head_weight,
    head_bias,
    prompt_length,
    keep_mask,
    target_box,
):
    section_index = lax.axis_index("section")
    opening = section_index == 0
    closing = section_index == lax.axis_size("section") - 1
    local_input = forward_input[0]
    closing_saved = jnp.where(closing, local_input, saved_last[0])
    gathered_input = gather_columns(local_input[None], 0)[0]
    stored = gather_columns(jnp.stack([saved_first[0], first_cotangent[0], closing_saved]), 1)
    last_partial = layer_core(gathered_input, last_gain[0], last_up[0], last_down[0])
    first_norm_partial, first_scaled, first_inverse = backward_core(
        stored[0], stored[1], first_gain[0], first_up[0], first_down[0]
    )
    reduced = reduce_columns(jnp.stack([last_partial, first_norm_partial]), 3)
    hidden_local = (local_input.astype(jnp.float32) + reduced[0]).astype(jnp.bfloat16)
    first_grad = backward_finish(
        first_cotangent[0], reduced[1], first_scaled, first_inverse, first_gain[0], 7
    )
    arrived_local = shifted(hidden_local, "section", 1)
    returned = shifted(first_grad, "section", -1)
    head_grad = head_cotangent(
        hidden_local, head_gain, head_weight, head_bias, prompt_length, keep_mask, target_box
    )
    entry_local = jnp.where(opening, section_entry, arrived_local)
    cotangent = jnp.where(closing, head_grad, returned)
    arrived = gather_columns(jnp.stack([entry_local, cotangent]), 2)
    first_partial = layer_core(arrived[0], first_gain[0], first_up[0], first_down[0])
    last_norm_partial, last_scaled, last_inverse = backward_core(
        stored[2], arrived[1], last_gain[0], last_up[0], last_down[0]
    )
    reduced_late = reduce_columns(jnp.stack([first_partial, last_norm_partial]), 4)
    layer_output = (entry_local.astype(jnp.float32) + reduced_late[0]).astype(jnp.bfloat16)
    input_gradient = backward_finish(
        cotangent, reduced_late[1], last_scaled, last_inverse, last_gain[0], 8
    )
    return (layer_output[None], input_gradient[None])


def solution(mesh):
    sections = mesh.shape["section"]
    tensors = mesh.shape["tensor"]
    split = Mesh(mesh.devices.reshape(sections, tensors // 2, 2), ("section", "ty", "tz"))
    rows = P("section", None, TENSOR)
    placed = (
        rows,
        rows,
        rows,
        rows,
        P(None, TENSOR),
        P("section", None),
        rows,
        P("section", TENSOR, None),
        P("section", None),
        rows,
        P("section", TENSOR, None),
        P(),
        P(TENSOR, None),
        P(),
        P(),
        P(),
        P(),
    )
    return jax.shard_map(
        per_device,
        mesh=split,
        in_specs=placed,
        out_specs=(rows, rows),
        check_vma=False,
    )
```

```python
import functools

import jax
import jax.numpy as jnp
from jax import lax
from jax.experimental import pallas as pl
from jax.experimental.pallas import tpu as pltpu
from jax.sharding import Mesh
from jax.sharding import PartitionSpec as P

epsilon = 1e-06
softness = 4.0
loss_scale = 4096.0
TENSOR = ("ty", "tz")


def shifted(value, axis, steps):
    count = lax.axis_size(axis)
    initial, last = (max(0, -steps), min(count, count - steps))
    return lax.ppermute(value, axis, [(source, source + steps) for source in range(initial, last)])


def tensor_size():
    return lax.axis_size("ty") * lax.axis_size("tz")


def tensor_index():
    return lax.axis_index("ty") * lax.axis_size("tz") + lax.axis_index("tz")


def unit_rows(values):
    values = values.astype(jnp.float32)
    inverse = lax.rsqrt(jnp.mean(values * values, axis=-1, keepdims=True) + epsilon)
    return (values * inverse, inverse)


def column_start(local_width):
    return tensor_index() * local_width


def column_slice(full_rows, local_width):
    return lax.dynamic_slice_in_dim(full_rows, column_start(local_width), local_width, 1)


MESH_ID = pl.DeviceIdType.MESH


def gather_kernel(ny, nz, x_ref, out_ref, send_sems, recv_sems):
    width = x_ref.shape[2]
    ty, tz = lax.axis_index("ty"), lax.axis_index("tz")
    me = ty * nz + tz
    partner_z = 1 - tz
    partner = ty * nz + partner_z
    y_peers = [lax.rem(ty + step, ny) for step in range(1, ny)]
    section = lax.axis_index("section")

    def device(y, z):
        return (section, y, z)

    def cols(index):
        return pl.ds(pl.multiple_of(index * width, width), width)

    barrier = pltpu.get_barrier_semaphore()
    pl.semaphore_signal(barrier, inc=1, device_id=device(ty, partner_z), device_id_type=MESH_ID)
    for y in y_peers:
        pl.semaphore_signal(barrier, inc=1, device_id=device(y, tz), device_id_type=MESH_ID)
    pl.semaphore_wait(barrier, ny)

    sends = [
        pltpu.make_async_remote_copy(
            src_ref=x_ref,
            dst_ref=out_ref.at[:, :, cols(me)],
            send_sem=send_sems.at[0],
            recv_sem=recv_sems.at[me],
            device_id=device(ty, partner_z),
            device_id_type=MESH_ID,
        )
    ]
    for number, y in enumerate(y_peers):
        sends.append(
            pltpu.make_async_remote_copy(
                src_ref=x_ref,
                dst_ref=out_ref.at[:, :, cols(me)],
                send_sem=send_sems.at[1 + number],
                recv_sem=recv_sems.at[me],
                device_id=device(y, tz),
                device_id_type=MESH_ID,
            )
        )
    for copy in sends:
        copy.start()
    out_ref[:, :, cols(me)] = x_ref[...]
    pltpu.make_async_remote_copy(
        src_ref=x_ref,
        dst_ref=out_ref.at[:, :, cols(partner)],
        send_sem=send_sems.at[0],
        recv_sem=recv_sems.at[partner],
        device_id=device(ty, partner_z),
        device_id_type=MESH_ID,
    ).wait_recv()
    forwards = []
    for number, y in enumerate(y_peers):
        forwards.append(
            pltpu.make_async_remote_copy(
                src_ref=out_ref.at[:, :, cols(partner)],
                dst_ref=out_ref.at[:, :, cols(partner)],
                send_sem=send_sems.at[ny + number],
                recv_sem=recv_sems.at[partner],
                device_id=device(y, tz),
                device_id_type=MESH_ID,
            )
        )
    for copy in forwards:
        copy.start()
    for y in y_peers:
        for z in range(nz):
            source = y * nz + z
            pltpu.make_async_remote_copy(
                src_ref=x_ref,
                dst_ref=out_ref.at[:, :, cols(source)],
                send_sem=send_sems.at[0],
                recv_sem=recv_sems.at[source],
                device_id=device(y, z),
                device_id_type=MESH_ID,
            ).wait_recv()
    for copy in sends + forwards:
        copy.wait_send()


def gather_columns(local_rows, collective):
    k, rows, width = local_rows.shape
    ny, nz = lax.axis_size("ty"), lax.axis_size("tz")
    full = width * ny * nz
    moved = local_rows.size * local_rows.dtype.itemsize * 7
    return pl.pallas_call(
        functools.partial(gather_kernel, ny, nz),
        out_shape=jax.ShapeDtypeStruct((k, rows, full), local_rows.dtype),
        in_specs=[pl.BlockSpec(memory_space=pltpu.VMEM)],
        out_specs=pl.BlockSpec(memory_space=pltpu.VMEM),
        scratch_shapes=[
            pltpu.SemaphoreType.DMA((2 * ny - 1,)),
            pltpu.SemaphoreType.DMA((ny * nz,)),
        ],
        compiler_params=pltpu.CompilerParams(
            collective_id=collective, has_side_effects=True, vmem_limit_bytes=48 * 1024 * 1024
        ),
        cost_estimate=pl.CostEstimate(flops=0, transcendentals=0, bytes_accessed=moved),
    )(local_rows)


def scatter_kernel(ny, nz, part_ref, out_ref, stage, z_send, z_recv, send_sems, recv_sems, z_sems):
    k, rows, width = out_ref.shape
    pair = nz * width
    ty, tz = lax.axis_index("ty"), lax.axis_index("tz")
    partner_z = 1 - tz
    section = lax.axis_index("section")
    chunk = 32

    def device(y, z):
        return (section, y, z)

    barrier = pltpu.get_barrier_semaphore()
    pl.semaphore_signal(barrier, inc=1, device_id=device(ty, partner_z), device_id_type=MESH_ID)
    for step in range(1, ny):
        pl.semaphore_signal(
            barrier, inc=1, device_id=device(lax.rem(ty + step, ny), tz), device_id_type=MESH_ID
        )
    pl.semaphore_wait(barrier, ny)

    sends = []
    for step in range(1, ny):
        peer = lax.rem(ty + step, ny)
        copy = pltpu.make_async_remote_copy(
            src_ref=part_ref.at[:, :, pl.ds(pl.multiple_of(peer * pair, pair), pair)],
            dst_ref=stage.at[ny - step - 1],
            send_sem=send_sems.at[step - 1],
            recv_sem=recv_sems.at[ny - step - 1],
            device_id=device(peer, tz),
            device_id_type=MESH_ID,
        )
        copy.start()
        sends.append(copy)
    for slot in range(ny - 1):
        pltpu.make_async_remote_copy(
            src_ref=stage.at[slot],
            dst_ref=stage.at[slot],
            send_sem=send_sems.at[0],
            recv_sem=recv_sems.at[slot],
            device_id=device(ty, partner_z),
            device_id_type=MESH_ID,
        ).wait_recv()

    def add_terms(z, target):
        own = pl.multiple_of((ty * nz + z) * width, width)
        inside = pl.multiple_of(z * width, width)

        def body(step, carry):
            plane = step // (rows // chunk)
            row = pl.multiple_of((step % (rows // chunk)) * chunk, chunk)
            total = part_ref[plane, pl.ds(row, chunk), pl.ds(own, width)].astype(jnp.float32)
            for slot in range(ny - 1):
                total += stage[slot, plane, pl.ds(row, chunk), pl.ds(inside, width)].astype(
                    jnp.float32
                )
            target(plane, row, total)
            return carry

        lax.fori_loop(0, k * (rows // chunk), body, 0)

    def to_send(plane, row, total):
        z_send[plane, pl.ds(row, chunk), :] = total

    add_terms(partner_z, to_send)
    z_copy = pltpu.make_async_remote_copy(
        src_ref=z_send,
        dst_ref=z_recv,
        send_sem=z_sems.at[0],
        recv_sem=z_sems.at[1],
        device_id=device(ty, partner_z),
        device_id_type=MESH_ID,
    )
    z_copy.start()

    def to_out(plane, row, total):
        out_ref[plane, pl.ds(row, chunk), :] = total

    add_terms(tz, to_out)
    z_copy.wait_recv()
    out_ref[...] += z_recv[...]
    z_copy.wait_send()
    for copy in sends:
        copy.wait_send()


def reduce_columns(partial_rows, collective, term_type=jnp.bfloat16):
    k, rows, full = partial_rows.shape
    ny, nz = lax.axis_size("ty"), lax.axis_size("tz")
    width = full // (ny * nz)
    terms = partial_rows.astype(term_type)
    moved = terms.size * terms.dtype.itemsize
    return pl.pallas_call(
        functools.partial(scatter_kernel, ny, nz),
        out_shape=jax.ShapeDtypeStruct((k, rows, width), jnp.float32),
        in_specs=[pl.BlockSpec(memory_space=pltpu.VMEM)],
        out_specs=pl.BlockSpec(memory_space=pltpu.VMEM),
        scratch_shapes=[
            pltpu.VMEM((ny - 1, k, rows, nz * width), term_type),
            pltpu.VMEM((k, rows, width), jnp.float32),
            pltpu.VMEM((k, rows, width), jnp.float32),
            pltpu.SemaphoreType.DMA((ny - 1,)),
            pltpu.SemaphoreType.DMA((ny - 1,)),
            pltpu.SemaphoreType.DMA((2,)),
        ],
        compiler_params=pltpu.CompilerParams(
            collective_id=collective, has_side_effects=True, vmem_limit_bytes=56 * 1024 * 1024
        ),
        cost_estimate=pl.CostEstimate(flops=terms.size, transcendentals=0, bytes_accessed=moved),
    )(terms)


def sum_kernel(ny, nz, v_ref, out_ref, slots, send_sems, recv_sems):
    ty, tz = lax.axis_index("ty"), lax.axis_index("tz")
    me = ty * nz + tz
    section = lax.axis_index("section")
    peers = [(lax.rem(ty + dy, ny), lax.rem(tz + dz, nz)) for dy in range(ny) for dz in range(nz)][1:]

    barrier = pltpu.get_barrier_semaphore()
    for y, z in peers:
        pl.semaphore_signal(barrier, inc=1, device_id=(section, y, z), device_id_type=MESH_ID)
    pl.semaphore_wait(barrier, len(peers))
    sends = []
    for number, (y, z) in enumerate(peers):
        copy = pltpu.make_async_remote_copy(
            src_ref=v_ref,
            dst_ref=slots.at[me],
            send_sem=send_sems.at[number],
            recv_sem=recv_sems.at[me],
            device_id=(section, y, z),
            device_id_type=MESH_ID,
        )
        copy.start()
        sends.append(copy)
    slots[me] = v_ref[...]
    for y, z in peers:
        source = y * nz + z
        pltpu.make_async_remote_copy(
            src_ref=v_ref,
            dst_ref=slots.at[source],
            send_sem=send_sems.at[0],
            recv_sem=recv_sems.at[source],
            device_id=(section, y, z),
            device_id_type=MESH_ID,
        ).wait_recv()
    total = slots[0]
    for source in range(1, ny * nz):
        total = total + slots[source]
    out_ref[...] = total
    for copy in sends:
        copy.wait_send()


def row_sums(values, collective):
    shape = values.shape
    flat = values.reshape(-1).astype(jnp.float32)
    lanes = 128
    padded = -(-flat.shape[0] // lanes) * lanes
    rows = jnp.pad(flat, (0, padded - flat.shape[0])).reshape(padded // lanes, lanes)
    ny, nz = lax.axis_size("ty"), lax.axis_size("tz")
    summed = pl.pallas_call(
        functools.partial(sum_kernel, ny, nz),
        out_shape=jax.ShapeDtypeStruct(rows.shape, jnp.float32),
        in_specs=[pl.BlockSpec(memory_space=pltpu.VMEM)],
        out_specs=pl.BlockSpec(memory_space=pltpu.VMEM),
        scratch_shapes=[
            pltpu.VMEM((ny * nz,) + rows.shape, jnp.float32),
            pltpu.SemaphoreType.DMA((ny * nz - 1,)),
            pltpu.SemaphoreType.DMA((ny * nz,)),
        ],
        compiler_params=pltpu.CompilerParams(collective_id=collective, has_side_effects=True),
        cost_estimate=pl.CostEstimate(flops=rows.size * 8, transcendentals=0, bytes_accessed=rows.size * 64),
    )(rows)
    return summed.reshape(-1)[: flat.shape[0]].reshape(shape)


def spread_weights(up_matrix, down_matrix):
    n = tensor_size()
    full, hidden = up_matrix.shape
    width = full // n
    up_blocks = lax.all_to_all(up_matrix.reshape(n, width, hidden), TENSOR, 0, 0, tiled=True)
    up_local = up_blocks.transpose(1, 0, 2).reshape(width, n * hidden)
    down_blocks = down_matrix.reshape(hidden, n, width).transpose(1, 0, 2)
    down_local = lax.all_to_all(down_blocks, TENSOR, 0, 0, tiled=True).reshape(n * hidden, width)
    return up_local, down_local


def grouped_sum(left, right, contract):
    n = tensor_size()
    rows = left.shape[0]
    hidden = left.shape[1] // n
    left_groups = left.reshape(rows, n, hidden)
    if contract == "rows":
        right_groups = right.reshape(n, hidden, right.shape[1])
        terms = jnp.einsum("tgk,gkf->gtf", left_groups, right_groups, preferred_element_type=jnp.float32)
    else:
        right_groups = right.reshape(right.shape[0], n, hidden)
        terms = jnp.einsum("tgk,fgk->gtf", left_groups, right_groups, preferred_element_type=jnp.float32)
    return jnp.sum(terms.astype(jnp.bfloat16).astype(jnp.float32), axis=0)


def normed_rows(local_rows, total_squares, gain_cols, full_width):
    values = local_rows.astype(jnp.float32)
    inverse = lax.rsqrt(total_squares[:, None] / full_width + epsilon)
    scaled = values * inverse
    return scaled, inverse, (scaled * gain_cols).astype(jnp.bfloat16)


def local_squares(local_rows):
    values = local_rows.astype(jnp.float32)
    return jnp.sum(values * values, axis=-1)


def layer_forward(local_rows, squares, gain_cols, up_local, full_width):
    scaled, inverse, normed = normed_rows(local_rows, squares, gain_cols, full_width)
    return jnp.dot(normed, up_local, preferred_element_type=jnp.float32)


def layer_back_partials(saved_rows, squares, cotangent, gain_cols, up_local, down_local, full_width):
    scaled, inverse, normed = normed_rows(saved_rows, squares, gain_cols, full_width)
    pre_part = jnp.dot(normed, up_local, preferred_element_type=jnp.float32)
    grad_part = lax.dot_general(
        cotangent, down_local, (((1,), (1,)), ((), ())), preferred_element_type=jnp.float32
    )
    return pre_part, grad_part, scaled, inverse


def pre_gradient(pre_act, act_grad):
    sigmoid_pre = jax.nn.sigmoid(pre_act)
    return (act_grad * sigmoid_pre * (1.0 + pre_act * (1.0 - sigmoid_pre))).astype(jnp.bfloat16)


def back_finish(cotangent, norm_grad, scaled, inverse, gain_cols, full_width, collective):
    row_total = row_sums(jnp.sum(scaled * gain_cols * norm_grad, axis=1), collective)
    result = cotangent.astype(jnp.float32) + inverse * (
        gain_cols * norm_grad - scaled * row_total[:, None] / full_width
    )
    return result.astype(jnp.bfloat16)


def soft_min(first, second):
    return 0.5 * (
        first + second - jnp.sqrt((first - second) * (first - second) + softness * softness)
    )


def soft_max(first, second):
    return 0.5 * (
        first + second + jnp.sqrt((first - second) * (first - second) + softness * softness)
    )


def soft_relu(difference):
    return 0.5 * (difference + jnp.sqrt(difference * difference + softness * softness))


def box_loss(logits, target_box):
    scaled_box = jax.nn.sigmoid(logits) * 1000.0
    centre_x = scaled_box[:, 0]
    centre_y = scaled_box[:, 1]
    box_width = scaled_box[:, 2]
    box_height = scaled_box[:, 3]
    left_pred = centre_x - 0.5 * box_width
    right_pred = centre_x + 0.5 * box_width
    lower_pred = centre_y - 0.5 * box_height
    upper_pred = centre_y + 0.5 * box_height
    target = target_box.astype(jnp.float32)
    inner_width = soft_relu(soft_min(right_pred, target[:, 2]) - soft_max(left_pred, target[:, 0]))
    inner_height = soft_relu(
        soft_min(upper_pred, target[:, 3]) - soft_max(lower_pred, target[:, 1])
    )
    intersection_area = inner_width * inner_height
    target_area = (target[:, 2] - target[:, 0]) * (target[:, 3] - target[:, 1])
    union_area = box_width * box_height + target_area - intersection_area
    outer_width = soft_max(right_pred, target[:, 2]) - soft_min(left_pred, target[:, 0])
    outer_height = soft_max(upper_pred, target[:, 3]) - soft_min(lower_pred, target[:, 1])
    enclosing = outer_width * outer_height
    return loss_scale * jnp.mean(
        1.0 - intersection_area / union_area + (enclosing - union_area) / enclosing
    )


def head_cotangent(
    final_rows, head_gain, head_weight, head_bias, prompt_length, keep_mask, target_box
):
    row_count = keep_mask.shape[0]
    positions = jnp.arange(keep_mask.shape[1], dtype=jnp.int32)[None, :]
    starts = prompt_length[:, None]
    weights = (positions == starts - 1).astype(jnp.float32) + (positions >= starts).astype(
        jnp.float32
    ) * keep_mask.astype(jnp.float32)
    counts = jnp.sum(weights, axis=1)
    local_width = final_rows.shape[1]
    full_width = local_width * tensor_size()
    tokens = final_rows.astype(jnp.float32).reshape(row_count, keep_mask.shape[1], local_width)
    pooled = (
        jnp.einsum("rt,rtd->rd", weights, tokens, precision=lax.Precision.HIGHEST) / counts[:, None]
    )
    gain_cols = lax.dynamic_slice_in_dim(head_gain, column_start(local_width), local_width, 0)
    logit_part = jnp.dot(pooled * gain_cols, head_weight, precision=lax.Precision.HIGHEST)
    square_part = jnp.sum(pooled * pooled, axis=1, keepdims=True)
    totals = row_sums(jnp.concatenate([logit_part, square_part], axis=1), 5)
    inverse = lax.rsqrt(totals[:, 4] / full_width + epsilon)
    logits = totals[:, :4] * inverse[:, None] + head_bias

    def loss_of(logit_value):
        return box_loss(logit_value, target_box)

    loss_value, pullback = jax.vjp(loss_of, logits)
    logit_grad = pullback(jnp.ones((), jnp.float32))[0]
    scaled_grad = jnp.dot(logit_grad, head_weight.T, precision=lax.Precision.HIGHEST)
    unit_pooled = pooled * inverse[:, None]
    row_total = row_sums(jnp.sum(unit_pooled * gain_cols * scaled_grad, axis=1), 6)
    pooled_grad = inverse[:, None] * (
        gain_cols * scaled_grad - unit_pooled * row_total[:, None] / full_width
    )
    token_grad = (weights / counts[:, None])[:, :, None] * pooled_grad[:, None, :]
    return token_grad.reshape(final_rows.shape[0], local_width).astype(jnp.bfloat16)


def per_device(
    forward_input,
    saved_last,
    saved_first,
    first_cotangent,
    section_entry,
    last_gain,
    last_up,
    last_down,
    first_gain,
    first_up,
    first_down,
    head_gain,
    head_weight,
    head_bias,
    prompt_length,
    keep_mask,
    target_box,
):
    section_index = lax.axis_index("section")
    opening = section_index == 0
    closing = section_index == lax.axis_size("section") - 1
    local_input = forward_input[0]
    width = local_input.shape[1]
    full_width = width * tensor_size()
    last_gain_cols = lax.dynamic_slice_in_dim(last_gain[0], column_start(width), width, 0)
    first_gain_cols = lax.dynamic_slice_in_dim(first_gain[0], column_start(width), width, 0)
    last_up_local, last_down_local = spread_weights(last_up[0], last_down[0])
    first_up_local, first_down_local = spread_weights(first_up[0], first_down[0])
    closing_saved = jnp.where(closing, local_input, saved_last[0])
    squares = row_sums(
        jnp.stack(
            [local_squares(local_input), local_squares(saved_first[0]), local_squares(closing_saved)]
        ),
        9,
    )
    last_pre = layer_forward(local_input, squares[0], last_gain_cols, last_up_local, full_width)
    first_pre, first_grad_part, first_scaled, first_inverse = layer_back_partials(
        saved_first[0], squares[1], first_cotangent[0], first_gain_cols, first_up_local,
        first_down_local, full_width,
    )
    reduced = reduce_columns(jnp.stack([last_pre, first_pre, first_grad_part]), 3, jnp.float32)
    last_act = jax.nn.silu(reduced[0]).astype(jnp.bfloat16)
    first_pre_grad = pre_gradient(reduced[1], reduced[2])
    spread = gather_columns(jnp.stack([last_act, first_pre_grad]), 0)
    last_out = grouped_sum(spread[0], last_down_local, "rows")
    hidden_local = (local_input.astype(jnp.float32) + last_out).astype(jnp.bfloat16)
    first_norm_grad = grouped_sum(spread[1], first_up_local, "cols")
    first_grad = back_finish(
        first_cotangent[0], first_norm_grad, first_scaled, first_inverse, first_gain_cols,
        full_width, 7,
    )
    arrived_local = shifted(hidden_local, "section", 1)
    returned = shifted(first_grad, "section", -1)
    head_grad = head_cotangent(
        hidden_local, head_gain, head_weight, head_bias, prompt_length, keep_mask, target_box
    )
    entry_local = jnp.where(opening, section_entry, arrived_local)
    cotangent = jnp.where(closing, head_grad, returned)
    entry_squares = row_sums(local_squares(entry_local), 10)
    first_pre_late = layer_forward(entry_local, entry_squares, first_gain_cols, first_up_local, full_width)
    last_pre_late, last_grad_part, last_scaled, last_inverse = layer_back_partials(
        closing_saved, squares[2], cotangent, last_gain_cols, last_up_local, last_down_local,
        full_width,
    )
    reduced_late = reduce_columns(
        jnp.stack([first_pre_late, last_pre_late, last_grad_part]), 4, jnp.float32
    )
    first_act = jax.nn.silu(reduced_late[0]).astype(jnp.bfloat16)
    last_pre_grad = pre_gradient(reduced_late[1], reduced_late[2])
    spread_late = gather_columns(jnp.stack([first_act, last_pre_grad]), 1)
    first_out = grouped_sum(spread_late[0], first_down_local, "rows")
    layer_output = (entry_local.astype(jnp.float32) + first_out).astype(jnp.bfloat16)
    last_norm_grad = grouped_sum(spread_late[1], last_up_local, "cols")
    input_gradient = back_finish(
        cotangent, last_norm_grad, last_scaled, last_inverse, last_gain_cols, full_width, 8
    )
    return (layer_output[None], input_gradient[None])


def solution(mesh):
    sections = mesh.shape["section"]
    tensors = mesh.shape["tensor"]
    split = Mesh(mesh.devices.reshape(sections, tensors // 2, 2), ("section", "ty", "tz"))
    rows = P("section", None, TENSOR)
    placed = (
        rows,
        rows,
        rows,
        rows,
        P(None, TENSOR),
        P("section", None),
        rows,
        P("section", TENSOR, None),
        P("section", None),
        rows,
        P("section", TENSOR, None),
        P(),
        P(TENSOR, None),
        P(),
        P(),
        P(),
        P(),
    )
    return jax.shard_map(
        per_device,
        mesh=split,
        in_specs=placed,
        out_specs=(rows, rows),
        check_vma=False,
    )
```

```python
import functools

import jax
import jax.numpy as jnp
from jax import lax
from jax.experimental import pallas as pl
from jax.experimental.pallas import tpu as pltpu
from jax.sharding import Mesh
from jax.sharding import PartitionSpec as P

epsilon = 1e-06
softness = 4.0
loss_scale = 4096.0
TENSOR = ("ty", "tz")


def shifted(value, axis, steps):
    count = lax.axis_size(axis)
    initial, last = (max(0, -steps), min(count, count - steps))
    return lax.ppermute(value, axis, [(source, source + steps) for source in range(initial, last)])


def tensor_size():
    return lax.axis_size("ty") * lax.axis_size("tz")


def tensor_index():
    return lax.axis_index("ty") * lax.axis_size("tz") + lax.axis_index("tz")


def unit_rows(values):
    values = values.astype(jnp.float32)
    inverse = lax.rsqrt(jnp.mean(values * values, axis=-1, keepdims=True) + epsilon)
    return (values * inverse, inverse)


def column_start(local_width):
    return tensor_index() * local_width


def column_slice(full_rows, local_width):
    return lax.dynamic_slice_in_dim(full_rows, column_start(local_width), local_width, 1)


MESH_ID = pl.DeviceIdType.MESH


def gather_kernel(ny, nz, x_ref, out_ref, send_sems, recv_sems):
    width = x_ref.shape[2]
    ty, tz = lax.axis_index("ty"), lax.axis_index("tz")
    me = ty * nz + tz
    partner_z = 1 - tz
    partner = ty * nz + partner_z
    y_peers = [lax.rem(ty + step, ny) for step in range(1, ny)]
    section = lax.axis_index("section")

    def device(y, z):
        return (section, y, z)

    def cols(index):
        return pl.ds(pl.multiple_of(index * width, width), width)

    barrier = pltpu.get_barrier_semaphore()
    pl.semaphore_signal(barrier, inc=1, device_id=device(ty, partner_z), device_id_type=MESH_ID)
    for y in y_peers:
        pl.semaphore_signal(barrier, inc=1, device_id=device(y, tz), device_id_type=MESH_ID)
    pl.semaphore_wait(barrier, ny)

    sends = [
        pltpu.make_async_remote_copy(
            src_ref=x_ref,
            dst_ref=out_ref.at[:, :, cols(me)],
            send_sem=send_sems.at[0],
            recv_sem=recv_sems.at[me],
            device_id=device(ty, partner_z),
            device_id_type=MESH_ID,
        )
    ]
    for number, y in enumerate(y_peers):
        sends.append(
            pltpu.make_async_remote_copy(
                src_ref=x_ref,
                dst_ref=out_ref.at[:, :, cols(me)],
                send_sem=send_sems.at[1 + number],
                recv_sem=recv_sems.at[me],
                device_id=device(y, tz),
                device_id_type=MESH_ID,
            )
        )
    for copy in sends:
        copy.start()
    out_ref[:, :, cols(me)] = x_ref[...]
    pltpu.make_async_remote_copy(
        src_ref=x_ref,
        dst_ref=out_ref.at[:, :, cols(partner)],
        send_sem=send_sems.at[0],
        recv_sem=recv_sems.at[partner],
        device_id=device(ty, partner_z),
        device_id_type=MESH_ID,
    ).wait_recv()
    forwards = []
    for number, y in enumerate(y_peers):
        forwards.append(
            pltpu.make_async_remote_copy(
                src_ref=out_ref.at[:, :, cols(partner)],
                dst_ref=out_ref.at[:, :, cols(partner)],
                send_sem=send_sems.at[ny + number],
                recv_sem=recv_sems.at[partner],
                device_id=device(y, tz),
                device_id_type=MESH_ID,
            )
        )
    for copy in forwards:
        copy.start()
    for y in y_peers:
        for z in range(nz):
            source = y * nz + z
            pltpu.make_async_remote_copy(
                src_ref=x_ref,
                dst_ref=out_ref.at[:, :, cols(source)],
                send_sem=send_sems.at[0],
                recv_sem=recv_sems.at[source],
                device_id=device(y, z),
                device_id_type=MESH_ID,
            ).wait_recv()
    for copy in sends + forwards:
        copy.wait_send()


def gather_columns(local_rows, collective):
    k, rows, width = local_rows.shape
    ny, nz = lax.axis_size("ty"), lax.axis_size("tz")
    full = width * ny * nz
    moved = local_rows.size * local_rows.dtype.itemsize * 7
    return pl.pallas_call(
        functools.partial(gather_kernel, ny, nz),
        out_shape=jax.ShapeDtypeStruct((k, rows, full), local_rows.dtype),
        in_specs=[pl.BlockSpec(memory_space=pltpu.VMEM)],
        out_specs=pl.BlockSpec(memory_space=pltpu.VMEM),
        scratch_shapes=[
            pltpu.SemaphoreType.DMA((2 * ny - 1,)),
            pltpu.SemaphoreType.DMA((ny * nz,)),
        ],
        compiler_params=pltpu.CompilerParams(
            collective_id=collective, has_side_effects=True, vmem_limit_bytes=48 * 1024 * 1024
        ),
        cost_estimate=pl.CostEstimate(flops=0, transcendentals=0, bytes_accessed=moved),
    )(local_rows)


def scatter_kernel(ny, nz, part_ref, out_ref, stage, z_send, z_recv, send_sems, recv_sems, z_sems):
    k, rows, width = out_ref.shape
    pair = nz * width
    ty, tz = lax.axis_index("ty"), lax.axis_index("tz")
    partner_z = 1 - tz
    section = lax.axis_index("section")
    chunk = 32

    def device(y, z):
        return (section, y, z)

    barrier = pltpu.get_barrier_semaphore()
    pl.semaphore_signal(barrier, inc=1, device_id=device(ty, partner_z), device_id_type=MESH_ID)
    for step in range(1, ny):
        pl.semaphore_signal(
            barrier, inc=1, device_id=device(lax.rem(ty + step, ny), tz), device_id_type=MESH_ID
        )
    pl.semaphore_wait(barrier, ny)

    sends = []
    for step in range(1, ny):
        peer = lax.rem(ty + step, ny)
        copy = pltpu.make_async_remote_copy(
            src_ref=part_ref.at[:, :, pl.ds(pl.multiple_of(peer * pair, pair), pair)],
            dst_ref=stage.at[ny - step - 1],
            send_sem=send_sems.at[step - 1],
            recv_sem=recv_sems.at[ny - step - 1],
            device_id=device(peer, tz),
            device_id_type=MESH_ID,
        )
        copy.start()
        sends.append(copy)
    for slot in range(ny - 1):
        pltpu.make_async_remote_copy(
            src_ref=stage.at[slot],
            dst_ref=stage.at[slot],
            send_sem=send_sems.at[0],
            recv_sem=recv_sems.at[slot],
            device_id=device(ty, partner_z),
            device_id_type=MESH_ID,
        ).wait_recv()

    def add_terms(z, target):
        own = pl.multiple_of((ty * nz + z) * width, width)
        inside = pl.multiple_of(z * width, width)

        def body(step, carry):
            plane = step // (rows // chunk)
            row = pl.multiple_of((step % (rows // chunk)) * chunk, chunk)
            total = part_ref[plane, pl.ds(row, chunk), pl.ds(own, width)].astype(jnp.float32)
            for slot in range(ny - 1):
                total += stage[slot, plane, pl.ds(row, chunk), pl.ds(inside, width)].astype(
                    jnp.float32
                )
            target(plane, row, total)
            return carry

        lax.fori_loop(0, k * (rows // chunk), body, 0)

    def to_send(plane, row, total):
        z_send[plane, pl.ds(row, chunk), :] = total

    add_terms(partner_z, to_send)
    z_copy = pltpu.make_async_remote_copy(
        src_ref=z_send,
        dst_ref=z_recv,
        send_sem=z_sems.at[0],
        recv_sem=z_sems.at[1],
        device_id=device(ty, partner_z),
        device_id_type=MESH_ID,
    )
    z_copy.start()

    def to_out(plane, row, total):
        out_ref[plane, pl.ds(row, chunk), :] = total

    add_terms(tz, to_out)
    z_copy.wait_recv()
    out_ref[...] += z_recv[...]
    z_copy.wait_send()
    for copy in sends:
        copy.wait_send()


def reduce_columns(partial_rows, collective, term_type=jnp.bfloat16):
    k, rows, full = partial_rows.shape
    ny, nz = lax.axis_size("ty"), lax.axis_size("tz")
    width = full // (ny * nz)
    terms = partial_rows.astype(term_type)
    moved = terms.size * terms.dtype.itemsize
    return pl.pallas_call(
        functools.partial(scatter_kernel, ny, nz),
        out_shape=jax.ShapeDtypeStruct((k, rows, width), jnp.float32),
        in_specs=[pl.BlockSpec(memory_space=pltpu.VMEM)],
        out_specs=pl.BlockSpec(memory_space=pltpu.VMEM),
        scratch_shapes=[
            pltpu.VMEM((ny - 1, k, rows, nz * width), term_type),
            pltpu.VMEM((k, rows, width), jnp.float32),
            pltpu.VMEM((k, rows, width), jnp.float32),
            pltpu.SemaphoreType.DMA((ny - 1,)),
            pltpu.SemaphoreType.DMA((ny - 1,)),
            pltpu.SemaphoreType.DMA((2,)),
        ],
        compiler_params=pltpu.CompilerParams(
            collective_id=collective, has_side_effects=True, vmem_limit_bytes=56 * 1024 * 1024
        ),
        cost_estimate=pl.CostEstimate(flops=terms.size, transcendentals=0, bytes_accessed=moved),
    )(terms)


def sum_kernel(ny, nz, v_ref, out_ref, slots, send_sems, recv_sems):
    ty, tz = lax.axis_index("ty"), lax.axis_index("tz")
    me = ty * nz + tz
    section = lax.axis_index("section")
    peers = [(lax.rem(ty + dy, ny), lax.rem(tz + dz, nz)) for dy in range(ny) for dz in range(nz)][1:]

    barrier = pltpu.get_barrier_semaphore()
    for y, z in peers:
        pl.semaphore_signal(barrier, inc=1, device_id=(section, y, z), device_id_type=MESH_ID)
    pl.semaphore_wait(barrier, len(peers))
    sends = []
    for number, (y, z) in enumerate(peers):
        copy = pltpu.make_async_remote_copy(
            src_ref=v_ref,
            dst_ref=slots.at[me],
            send_sem=send_sems.at[number],
            recv_sem=recv_sems.at[me],
            device_id=(section, y, z),
            device_id_type=MESH_ID,
        )
        copy.start()
        sends.append(copy)
    slots[me] = v_ref[...]
    for y, z in peers:
        source = y * nz + z
        pltpu.make_async_remote_copy(
            src_ref=v_ref,
            dst_ref=slots.at[source],
            send_sem=send_sems.at[0],
            recv_sem=recv_sems.at[source],
            device_id=(section, y, z),
            device_id_type=MESH_ID,
        ).wait_recv()
    total = slots[0]
    for source in range(1, ny * nz):
        total = total + slots[source]
    out_ref[...] = total
    for copy in sends:
        copy.wait_send()


def row_sums(values, collective):
    shape = values.shape
    flat = values.reshape(-1).astype(jnp.float32)
    lanes = 128
    padded = -(-flat.shape[0] // lanes) * lanes
    rows = jnp.pad(flat, (0, padded - flat.shape[0])).reshape(padded // lanes, lanes)
    ny, nz = lax.axis_size("ty"), lax.axis_size("tz")
    summed = pl.pallas_call(
        functools.partial(sum_kernel, ny, nz),
        out_shape=jax.ShapeDtypeStruct(rows.shape, jnp.float32),
        in_specs=[pl.BlockSpec(memory_space=pltpu.VMEM)],
        out_specs=pl.BlockSpec(memory_space=pltpu.VMEM),
        scratch_shapes=[
            pltpu.VMEM((ny * nz,) + rows.shape, jnp.float32),
            pltpu.SemaphoreType.DMA((ny * nz - 1,)),
            pltpu.SemaphoreType.DMA((ny * nz,)),
        ],
        compiler_params=pltpu.CompilerParams(collective_id=collective, has_side_effects=True),
        cost_estimate=pl.CostEstimate(flops=rows.size * 8, transcendentals=0, bytes_accessed=rows.size * 64),
    )(rows)
    return summed.reshape(-1)[: flat.shape[0]].reshape(shape)


def spread_weights(up_matrix, down_matrix):
    n = tensor_size()
    full, hidden = up_matrix.shape
    width = full // n
    up_blocks = lax.all_to_all(up_matrix.reshape(n, width, hidden), TENSOR, 0, 0, tiled=True)
    up_local = up_blocks.transpose(1, 0, 2).reshape(width, n * hidden)
    down_blocks = down_matrix.reshape(hidden, n, width).transpose(1, 0, 2)
    down_local = lax.all_to_all(down_blocks, TENSOR, 0, 0, tiled=True).reshape(n * hidden, width)
    return up_local, down_local


def grouped_sum(left, right, contract):
    n = tensor_size()
    rows = left.shape[0]
    hidden = left.shape[1] // n
    left_groups = left.reshape(rows, n, hidden)
    if contract == "rows":
        right_groups = right.reshape(n, hidden, right.shape[1])
        terms = jnp.einsum("tgk,gkf->gtf", left_groups, right_groups, preferred_element_type=jnp.float32)
    else:
        right_groups = right.reshape(right.shape[0], n, hidden)
        terms = jnp.einsum("tgk,fgk->gtf", left_groups, right_groups, preferred_element_type=jnp.float32)
    return jnp.sum(terms.astype(jnp.bfloat16).astype(jnp.float32), axis=0)


def normed_rows(local_rows, total_squares, gain_cols, full_width):
    values = local_rows.astype(jnp.float32)
    inverse = lax.rsqrt(total_squares[:, None] / full_width + epsilon)
    scaled = values * inverse
    return scaled, inverse, (scaled * gain_cols).astype(jnp.bfloat16)


def local_squares(local_rows):
    values = local_rows.astype(jnp.float32)
    return jnp.sum(values * values, axis=-1)


def layer_forward(local_rows, squares, gain_cols, up_local, full_width):
    scaled, inverse, normed = normed_rows(local_rows, squares, gain_cols, full_width)
    return jnp.dot(normed, up_local, preferred_element_type=jnp.float32)


def layer_back_partials(saved_rows, squares, cotangent, gain_cols, up_local, down_local, full_width):
    scaled, inverse, normed = normed_rows(saved_rows, squares, gain_cols, full_width)
    pre_part = jnp.dot(normed, up_local, preferred_element_type=jnp.float32)
    grad_part = lax.dot_general(
        cotangent, down_local, (((1,), (1,)), ((), ())), preferred_element_type=jnp.float32
    )
    return pre_part, grad_part, scaled, inverse


def pre_gradient(pre_act, act_grad):
    sigmoid_pre = jax.nn.sigmoid(pre_act)
    return (act_grad * sigmoid_pre * (1.0 + pre_act * (1.0 - sigmoid_pre))).astype(jnp.bfloat16)


def back_projection(scaled, gain_cols, norm_grad):
    return jnp.sum(scaled * gain_cols * norm_grad, axis=1)


def back_finish(cotangent, norm_grad, scaled, inverse, gain_cols, full_width, row_total):
    result = cotangent.astype(jnp.float32) + inverse * (
        gain_cols * norm_grad - scaled * row_total[:, None] / full_width
    )
    return result.astype(jnp.bfloat16)


def soft_min(first, second):
    return 0.5 * (
        first + second - jnp.sqrt((first - second) * (first - second) + softness * softness)
    )


def soft_max(first, second):
    return 0.5 * (
        first + second + jnp.sqrt((first - second) * (first - second) + softness * softness)
    )


def soft_relu(difference):
    return 0.5 * (difference + jnp.sqrt(difference * difference + softness * softness))


def box_loss(logits, target_box):
    scaled_box = jax.nn.sigmoid(logits) * 1000.0
    centre_x = scaled_box[:, 0]
    centre_y = scaled_box[:, 1]
    box_width = scaled_box[:, 2]
    box_height = scaled_box[:, 3]
    left_pred = centre_x - 0.5 * box_width
    right_pred = centre_x + 0.5 * box_width
    lower_pred = centre_y - 0.5 * box_height
    upper_pred = centre_y + 0.5 * box_height
    target = target_box.astype(jnp.float32)
    inner_width = soft_relu(soft_min(right_pred, target[:, 2]) - soft_max(left_pred, target[:, 0]))
    inner_height = soft_relu(
        soft_min(upper_pred, target[:, 3]) - soft_max(lower_pred, target[:, 1])
    )
    intersection_area = inner_width * inner_height
    target_area = (target[:, 2] - target[:, 0]) * (target[:, 3] - target[:, 1])
    union_area = box_width * box_height + target_area - intersection_area
    outer_width = soft_max(right_pred, target[:, 2]) - soft_min(left_pred, target[:, 0])
    outer_height = soft_max(upper_pred, target[:, 3]) - soft_min(lower_pred, target[:, 1])
    enclosing = outer_width * outer_height
    return loss_scale * jnp.mean(
        1.0 - intersection_area / union_area + (enclosing - union_area) / enclosing
    )


def head_pool(final_rows, head_gain, head_weight, prompt_length, keep_mask):
    row_count = keep_mask.shape[0]
    positions = jnp.arange(keep_mask.shape[1], dtype=jnp.int32)[None, :]
    starts = prompt_length[:, None]
    weights = (positions == starts - 1).astype(jnp.float32) + (positions >= starts).astype(
        jnp.float32
    ) * keep_mask.astype(jnp.float32)
    counts = jnp.sum(weights, axis=1)
    local_width = final_rows.shape[1]
    tokens = final_rows.astype(jnp.float32).reshape(row_count, keep_mask.shape[1], local_width)
    pooled = (
        jnp.einsum("rt,rtd->rd", weights, tokens, precision=lax.Precision.HIGHEST) / counts[:, None]
    )
    gain_cols = lax.dynamic_slice_in_dim(head_gain, column_start(local_width), local_width, 0)
    logit_part = jnp.dot(pooled * gain_cols, head_weight, precision=lax.Precision.HIGHEST)
    square_part = jnp.sum(pooled * pooled, axis=1, keepdims=True)
    return (weights, counts, pooled, gain_cols), jnp.concatenate([logit_part, square_part], axis=1)


def head_middle(pooled_state, totals, head_weight, head_bias, target_box):
    weights, counts, pooled, gain_cols = pooled_state
    full_width = pooled.shape[1] * tensor_size()
    inverse = lax.rsqrt(totals[:, 4] / full_width + epsilon)
    logits = totals[:, :4] * inverse[:, None] + head_bias

    def loss_of(logit_value):
        return box_loss(logit_value, target_box)

    loss_value, pullback = jax.vjp(loss_of, logits)
    logit_grad = pullback(jnp.ones((), jnp.float32))[0]
    scaled_grad = jnp.dot(logit_grad, head_weight.T, precision=lax.Precision.HIGHEST)
    unit_pooled = pooled * inverse[:, None]
    return (inverse, scaled_grad, unit_pooled), jnp.sum(unit_pooled * gain_cols * scaled_grad, axis=1)


def head_finish(pooled_state, middle_state, row_total, row_shape):
    weights, counts, pooled, gain_cols = pooled_state
    inverse, scaled_grad, unit_pooled = middle_state
    full_width = pooled.shape[1] * tensor_size()
    pooled_grad = inverse[:, None] * (
        gain_cols * scaled_grad - unit_pooled * row_total[:, None] / full_width
    )
    token_grad = (weights / counts[:, None])[:, :, None] * pooled_grad[:, None, :]
    return token_grad.reshape(row_shape).astype(jnp.bfloat16)


def per_device(
    forward_input,
    saved_last,
    saved_first,
    first_cotangent,
    section_entry,
    last_gain,
    last_up,
    last_down,
    first_gain,
    first_up,
    first_down,
    head_gain,
    head_weight,
    head_bias,
    prompt_length,
    keep_mask,
    target_box,
):
    section_index = lax.axis_index("section")
    opening = section_index == 0
    closing = section_index == lax.axis_size("section") - 1
    local_input = forward_input[0]
    width = local_input.shape[1]
    full_width = width * tensor_size()
    last_gain_cols = lax.dynamic_slice_in_dim(last_gain[0], column_start(width), width, 0)
    first_gain_cols = lax.dynamic_slice_in_dim(first_gain[0], column_start(width), width, 0)
    closing_saved = jnp.where(closing, local_input, saved_last[0])
    squares = row_sums(
        jnp.stack(
            [local_squares(local_input), local_squares(saved_first[0]), local_squares(closing_saved)]
        ),
        9,
    )
    last_up_local, last_down_local = spread_weights(last_up[0], last_down[0])
    first_up_local, first_down_local = spread_weights(first_up[0], first_down[0])
    last_pre = layer_forward(local_input, squares[0], last_gain_cols, last_up_local, full_width)
    first_pre, first_grad_part, first_scaled, first_inverse = layer_back_partials(
        saved_first[0], squares[1], first_cotangent[0], first_gain_cols, first_up_local,
        first_down_local, full_width,
    )
    reduced = reduce_columns(jnp.stack([last_pre, first_pre, first_grad_part]), 3, jnp.float32)
    last_act = jax.nn.silu(reduced[0]).astype(jnp.bfloat16)
    first_pre_grad = pre_gradient(reduced[1], reduced[2])
    spread = gather_columns(jnp.stack([last_act, first_pre_grad]), 0)
    last_out = grouped_sum(spread[0], last_down_local, "rows")
    hidden_local = (local_input.astype(jnp.float32) + last_out).astype(jnp.bfloat16)
    first_norm_grad = grouped_sum(spread[1], first_up_local, "cols")
    rows = first_norm_grad.shape[0]
    pooled_state, head_part = head_pool(
        hidden_local, head_gain, head_weight, prompt_length, keep_mask
    )
    first_projection = back_projection(first_scaled, first_gain_cols, first_norm_grad)
    joined = row_sums(jnp.concatenate([first_projection, head_part.reshape(-1)]), 7)
    first_grad = back_finish(
        first_cotangent[0], first_norm_grad, first_scaled, first_inverse, first_gain_cols,
        full_width, joined[:rows],
    )
    arrived_local = shifted(hidden_local, "section", 1)
    returned = shifted(first_grad, "section", -1)
    middle_state, head_row = head_middle(
        pooled_state, joined[rows:].reshape(head_part.shape), head_weight, head_bias, target_box
    )
    entry_local = jnp.where(opening, section_entry, arrived_local)
    late_joined = row_sums(jnp.concatenate([local_squares(entry_local), head_row]), 10)
    entry_squares = late_joined[:rows]
    head_grad = head_finish(pooled_state, middle_state, late_joined[rows:], hidden_local.shape)
    cotangent = jnp.where(closing, head_grad, returned)
    first_pre_late = layer_forward(entry_local, entry_squares, first_gain_cols, first_up_local, full_width)
    last_pre_late, last_grad_part, last_scaled, last_inverse = layer_back_partials(
        closing_saved, squares[2], cotangent, last_gain_cols, last_up_local, last_down_local,
        full_width,
    )
    reduced_late = reduce_columns(
        jnp.stack([first_pre_late, last_pre_late, last_grad_part]), 4, jnp.float32
    )
    first_act = jax.nn.silu(reduced_late[0]).astype(jnp.bfloat16)
    last_pre_grad = pre_gradient(reduced_late[1], reduced_late[2])
    spread_late = gather_columns(jnp.stack([first_act, last_pre_grad]), 1)
    first_out = grouped_sum(spread_late[0], first_down_local, "rows")
    layer_output = (entry_local.astype(jnp.float32) + first_out).astype(jnp.bfloat16)
    last_norm_grad = grouped_sum(spread_late[1], last_up_local, "cols")
    last_total = row_sums(back_projection(last_scaled, last_gain_cols, last_norm_grad), 8)
    input_gradient = back_finish(
        cotangent, last_norm_grad, last_scaled, last_inverse, last_gain_cols, full_width, last_total
    )
    return (layer_output[None], input_gradient[None])


def solution(mesh):
    sections = mesh.shape["section"]
    tensors = mesh.shape["tensor"]
    split = Mesh(mesh.devices.reshape(sections, tensors // 2, 2), ("section", "ty", "tz"))
    rows = P("section", None, TENSOR)
    placed = (
        rows,
        rows,
        rows,
        rows,
        P(None, TENSOR),
        P("section", None),
        rows,
        P("section", TENSOR, None),
        P("section", None),
        rows,
        P("section", TENSOR, None),
        P(),
        P(TENSOR, None),
        P(),
        P(),
        P(),
        P(),
    )
    return jax.shard_map(
        per_device,
        mesh=split,
        in_specs=placed,
        out_specs=(rows, rows),
        check_vma=False,
    )
```

```python
import functools

import jax
import jax.numpy as jnp
from jax import lax
from jax.experimental import pallas as pl
from jax.experimental.pallas import tpu as pltpu
from jax.sharding import Mesh
from jax.sharding import PartitionSpec as P

epsilon = 1e-06
softness = 4.0
loss_scale = 4096.0
TENSOR = ("ty", "tz")


def shifted(value, axis, steps):
    count = lax.axis_size(axis)
    initial, last = (max(0, -steps), min(count, count - steps))
    return lax.ppermute(value, axis, [(source, source + steps) for source in range(initial, last)])


def tensor_size():
    return lax.axis_size("ty") * lax.axis_size("tz")


def tensor_index():
    return lax.axis_index("ty") * lax.axis_size("tz") + lax.axis_index("tz")


def unit_rows(values):
    values = values.astype(jnp.float32)
    inverse = lax.rsqrt(jnp.mean(values * values, axis=-1, keepdims=True) + epsilon)
    return (values * inverse, inverse)


def column_start(local_width):
    return tensor_index() * local_width


def column_slice(full_rows, local_width):
    return lax.dynamic_slice_in_dim(full_rows, column_start(local_width), local_width, 1)


MESH_ID = pl.DeviceIdType.MESH


def gather_kernel(ny, nz, x_ref, out_ref, send_sems, recv_sems):
    width = x_ref.shape[2]
    ty, tz = lax.axis_index("ty"), lax.axis_index("tz")
    me = ty * nz + tz
    partner_z = 1 - tz
    partner = ty * nz + partner_z
    y_peers = [lax.rem(ty + step, ny) for step in range(1, ny)]
    section = lax.axis_index("section")

    def device(y, z):
        return (section, y, z)

    def cols(index):
        return pl.ds(pl.multiple_of(index * width, width), width)

    barrier = pltpu.get_barrier_semaphore()
    pl.semaphore_signal(barrier, inc=1, device_id=device(ty, partner_z), device_id_type=MESH_ID)
    for y in y_peers:
        pl.semaphore_signal(barrier, inc=1, device_id=device(y, tz), device_id_type=MESH_ID)
    pl.semaphore_wait(barrier, ny)

    sends = [
        pltpu.make_async_remote_copy(
            src_ref=x_ref,
            dst_ref=out_ref.at[:, :, cols(me)],
            send_sem=send_sems.at[0],
            recv_sem=recv_sems.at[me],
            device_id=device(ty, partner_z),
            device_id_type=MESH_ID,
        )
    ]
    for number, y in enumerate(y_peers):
        sends.append(
            pltpu.make_async_remote_copy(
                src_ref=x_ref,
                dst_ref=out_ref.at[:, :, cols(me)],
                send_sem=send_sems.at[1 + number],
                recv_sem=recv_sems.at[me],
                device_id=device(y, tz),
                device_id_type=MESH_ID,
            )
        )
    for copy in sends:
        copy.start()
    out_ref[:, :, cols(me)] = x_ref[...]
    pltpu.make_async_remote_copy(
        src_ref=x_ref,
        dst_ref=out_ref.at[:, :, cols(partner)],
        send_sem=send_sems.at[0],
        recv_sem=recv_sems.at[partner],
        device_id=device(ty, partner_z),
        device_id_type=MESH_ID,
    ).wait_recv()
    forwards = []
    for number, y in enumerate(y_peers):
        forwards.append(
            pltpu.make_async_remote_copy(
                src_ref=out_ref.at[:, :, cols(partner)],
                dst_ref=out_ref.at[:, :, cols(partner)],
                send_sem=send_sems.at[ny + number],
                recv_sem=recv_sems.at[partner],
                device_id=device(y, tz),
                device_id_type=MESH_ID,
            )
        )
    for copy in forwards:
        copy.start()
    for y in y_peers:
        for z in range(nz):
            source = y * nz + z
            pltpu.make_async_remote_copy(
                src_ref=x_ref,
                dst_ref=out_ref.at[:, :, cols(source)],
                send_sem=send_sems.at[0],
                recv_sem=recv_sems.at[source],
                device_id=device(y, z),
                device_id_type=MESH_ID,
            ).wait_recv()
    for copy in sends + forwards:
        copy.wait_send()


def gather_columns(local_rows, collective):
    k, rows, width = local_rows.shape
    ny, nz = lax.axis_size("ty"), lax.axis_size("tz")
    full = width * ny * nz
    moved = local_rows.size * local_rows.dtype.itemsize * 7
    return pl.pallas_call(
        functools.partial(gather_kernel, ny, nz),
        out_shape=jax.ShapeDtypeStruct((k, rows, full), local_rows.dtype),
        in_specs=[pl.BlockSpec(memory_space=pltpu.VMEM)],
        out_specs=pl.BlockSpec(memory_space=pltpu.VMEM),
        scratch_shapes=[
            pltpu.SemaphoreType.DMA((2 * ny - 1,)),
            pltpu.SemaphoreType.DMA((ny * nz,)),
        ],
        compiler_params=pltpu.CompilerParams(
            collective_id=collective, has_side_effects=True, vmem_limit_bytes=48 * 1024 * 1024
        ),
        cost_estimate=pl.CostEstimate(flops=0, transcendentals=0, bytes_accessed=moved),
    )(local_rows)


def scatter_kernel(ny, nz, part_ref, out_ref, stage, z_send, z_recv, send_sems, recv_sems, z_sems):
    k, rows, width = out_ref.shape
    pair = nz * width
    ty, tz = lax.axis_index("ty"), lax.axis_index("tz")
    partner_z = 1 - tz
    section = lax.axis_index("section")
    chunk = 32

    def device(y, z):
        return (section, y, z)

    barrier = pltpu.get_barrier_semaphore()
    pl.semaphore_signal(barrier, inc=1, device_id=device(ty, partner_z), device_id_type=MESH_ID)
    for step in range(1, ny):
        pl.semaphore_signal(
            barrier, inc=1, device_id=device(lax.rem(ty + step, ny), tz), device_id_type=MESH_ID
        )
    pl.semaphore_wait(barrier, ny)

    sends = []
    for step in range(1, ny):
        peer = lax.rem(ty + step, ny)
        copy = pltpu.make_async_remote_copy(
            src_ref=part_ref.at[:, :, pl.ds(pl.multiple_of(peer * pair, pair), pair)],
            dst_ref=stage.at[ny - step - 1],
            send_sem=send_sems.at[step - 1],
            recv_sem=recv_sems.at[ny - step - 1],
            device_id=device(peer, tz),
            device_id_type=MESH_ID,
        )
        copy.start()
        sends.append(copy)
    for slot in range(ny - 1):
        pltpu.make_async_remote_copy(
            src_ref=stage.at[slot],
            dst_ref=stage.at[slot],
            send_sem=send_sems.at[0],
            recv_sem=recv_sems.at[slot],
            device_id=device(ty, partner_z),
            device_id_type=MESH_ID,
        ).wait_recv()

    def add_terms(z, target):
        own = pl.multiple_of((ty * nz + z) * width, width)
        inside = pl.multiple_of(z * width, width)

        def body(step, carry):
            plane = step // (rows // chunk)
            row = pl.multiple_of((step % (rows // chunk)) * chunk, chunk)
            total = part_ref[plane, pl.ds(row, chunk), pl.ds(own, width)].astype(jnp.float32)
            for slot in range(ny - 1):
                total += stage[slot, plane, pl.ds(row, chunk), pl.ds(inside, width)].astype(
                    jnp.float32
                )
            target(plane, row, total)
            return carry

        lax.fori_loop(0, k * (rows // chunk), body, 0)

    def to_send(plane, row, total):
        z_send[plane, pl.ds(row, chunk), :] = total

    add_terms(partner_z, to_send)
    z_copy = pltpu.make_async_remote_copy(
        src_ref=z_send,
        dst_ref=z_recv,
        send_sem=z_sems.at[0],
        recv_sem=z_sems.at[1],
        device_id=device(ty, partner_z),
        device_id_type=MESH_ID,
    )
    z_copy.start()

    def to_out(plane, row, total):
        out_ref[plane, pl.ds(row, chunk), :] = total

    add_terms(tz, to_out)
    z_copy.wait_recv()
    out_ref[...] += z_recv[...]
    z_copy.wait_send()
    for copy in sends:
        copy.wait_send()


def reduce_columns(partial_rows, collective, term_type=jnp.bfloat16):
    k, rows, full = partial_rows.shape
    ny, nz = lax.axis_size("ty"), lax.axis_size("tz")
    width = full // (ny * nz)
    terms = partial_rows.astype(term_type)
    moved = terms.size * terms.dtype.itemsize
    return pl.pallas_call(
        functools.partial(scatter_kernel, ny, nz),
        out_shape=jax.ShapeDtypeStruct((k, rows, width), jnp.float32),
        in_specs=[pl.BlockSpec(memory_space=pltpu.VMEM)],
        out_specs=pl.BlockSpec(memory_space=pltpu.VMEM),
        scratch_shapes=[
            pltpu.VMEM((ny - 1, k, rows, nz * width), term_type),
            pltpu.VMEM((k, rows, width), jnp.float32),
            pltpu.VMEM((k, rows, width), jnp.float32),
            pltpu.SemaphoreType.DMA((ny - 1,)),
            pltpu.SemaphoreType.DMA((ny - 1,)),
            pltpu.SemaphoreType.DMA((2,)),
        ],
        compiler_params=pltpu.CompilerParams(
            collective_id=collective, has_side_effects=True, vmem_limit_bytes=56 * 1024 * 1024
        ),
        cost_estimate=pl.CostEstimate(flops=terms.size, transcendentals=0, bytes_accessed=moved),
    )(terms)


def sum_kernel(ny, nz, v_ref, out_ref, slots, send_sems, recv_sems):
    ty, tz = lax.axis_index("ty"), lax.axis_index("tz")
    me = ty * nz + tz
    section = lax.axis_index("section")
    peers = [(lax.rem(ty + dy, ny), lax.rem(tz + dz, nz)) for dy in range(ny) for dz in range(nz)][1:]

    barrier = pltpu.get_barrier_semaphore()
    for y, z in peers:
        pl.semaphore_signal(barrier, inc=1, device_id=(section, y, z), device_id_type=MESH_ID)
    pl.semaphore_wait(barrier, len(peers))
    sends = []
    for number, (y, z) in enumerate(peers):
        copy = pltpu.make_async_remote_copy(
            src_ref=v_ref,
            dst_ref=slots.at[me],
            send_sem=send_sems.at[number],
            recv_sem=recv_sems.at[me],
            device_id=(section, y, z),
            device_id_type=MESH_ID,
        )
        copy.start()
        sends.append(copy)
    slots[me] = v_ref[...]
    for y, z in peers:
        source = y * nz + z
        pltpu.make_async_remote_copy(
            src_ref=v_ref,
            dst_ref=slots.at[source],
            send_sem=send_sems.at[0],
            recv_sem=recv_sems.at[source],
            device_id=(section, y, z),
            device_id_type=MESH_ID,
        ).wait_recv()
    total = slots[0]
    for source in range(1, ny * nz):
        total = total + slots[source]
    out_ref[...] = total
    for copy in sends:
        copy.wait_send()


def row_sums(values, collective):
    shape = values.shape
    flat = values.reshape(-1).astype(jnp.float32)
    lanes = 128
    padded = -(-flat.shape[0] // lanes) * lanes
    rows = jnp.pad(flat, (0, padded - flat.shape[0])).reshape(padded // lanes, lanes)
    ny, nz = lax.axis_size("ty"), lax.axis_size("tz")
    summed = pl.pallas_call(
        functools.partial(sum_kernel, ny, nz),
        out_shape=jax.ShapeDtypeStruct(rows.shape, jnp.float32),
        in_specs=[pl.BlockSpec(memory_space=pltpu.VMEM)],
        out_specs=pl.BlockSpec(memory_space=pltpu.VMEM),
        scratch_shapes=[
            pltpu.VMEM((ny * nz,) + rows.shape, jnp.float32),
            pltpu.SemaphoreType.DMA((ny * nz - 1,)),
            pltpu.SemaphoreType.DMA((ny * nz,)),
        ],
        compiler_params=pltpu.CompilerParams(collective_id=collective, has_side_effects=True),
        cost_estimate=pl.CostEstimate(flops=rows.size * 8, transcendentals=0, bytes_accessed=rows.size * 64),
    )(rows)
    return summed.reshape(-1)[: flat.shape[0]].reshape(shape)


def spread_weights(up_matrix, down_matrix):
    n = tensor_size()
    full, hidden = up_matrix.shape
    width = full // n
    up_blocks = lax.all_to_all(up_matrix.reshape(n, width, hidden), TENSOR, 0, 0, tiled=True)
    up_local = up_blocks.transpose(1, 0, 2).reshape(width, n * hidden)
    down_blocks = down_matrix.reshape(hidden, n, width).transpose(1, 0, 2)
    down_local = lax.all_to_all(down_blocks, TENSOR, 0, 0, tiled=True).reshape(n * hidden, width)
    return up_local, down_local


def grouped_sum(left, right, contract):
    n = tensor_size()
    rows = left.shape[0]
    hidden = left.shape[1] // n
    left_groups = left.reshape(rows, n, hidden)
    if contract == "rows":
        right_groups = right.reshape(n, hidden, right.shape[1])
        terms = jnp.einsum("tgk,gkf->gtf", left_groups, right_groups, preferred_element_type=jnp.float32)
    else:
        right_groups = right.reshape(right.shape[0], n, hidden)
        terms = jnp.einsum("tgk,fgk->gtf", left_groups, right_groups, preferred_element_type=jnp.float32)
    return jnp.sum(terms.astype(jnp.bfloat16).astype(jnp.float32), axis=0)


def normed_rows(local_rows, total_squares, gain_cols, full_width):
    values = local_rows.astype(jnp.float32)
    inverse = lax.rsqrt(total_squares[:, None] / full_width + epsilon)
    scaled = values * inverse
    return scaled, inverse, (scaled * gain_cols).astype(jnp.bfloat16)


def local_squares(local_rows):
    values = local_rows.astype(jnp.float32)
    return jnp.sum(values * values, axis=-1)


def layer_forward(local_rows, squares, gain_cols, up_local, full_width):
    scaled, inverse, normed = normed_rows(local_rows, squares, gain_cols, full_width)
    return jnp.dot(normed, up_local, preferred_element_type=jnp.float32)


def layer_back_partials(saved_rows, squares, cotangent, gain_cols, up_local, down_local, full_width):
    scaled, inverse, normed = normed_rows(saved_rows, squares, gain_cols, full_width)
    pre_part = jnp.dot(normed, up_local, preferred_element_type=jnp.float32)
    grad_part = lax.dot_general(
        cotangent, down_local, (((1,), (1,)), ((), ())), preferred_element_type=jnp.float32
    )
    return pre_part, grad_part, scaled, inverse


def pre_gradient(pre_act, act_grad):
    sigmoid_pre = jax.nn.sigmoid(pre_act)
    return (act_grad * sigmoid_pre * (1.0 + pre_act * (1.0 - sigmoid_pre))).astype(jnp.bfloat16)


def back_projection(scaled, gain_cols, norm_grad):
    return jnp.sum(scaled * gain_cols * norm_grad, axis=1)


def back_finish(cotangent, norm_grad, scaled, inverse, gain_cols, full_width, row_total):
    result = cotangent.astype(jnp.float32) + inverse * (
        gain_cols * norm_grad - scaled * row_total[:, None] / full_width
    )
    return result.astype(jnp.bfloat16)


def soft_min(first, second):
    return 0.5 * (
        first + second - jnp.sqrt((first - second) * (first - second) + softness * softness)
    )


def soft_max(first, second):
    return 0.5 * (
        first + second + jnp.sqrt((first - second) * (first - second) + softness * softness)
    )


def soft_relu(difference):
    return 0.5 * (difference + jnp.sqrt(difference * difference + softness * softness))


def box_loss(logits, target_box):
    scaled_box = jax.nn.sigmoid(logits) * 1000.0
    centre_x = scaled_box[:, 0]
    centre_y = scaled_box[:, 1]
    box_width = scaled_box[:, 2]
    box_height = scaled_box[:, 3]
    left_pred = centre_x - 0.5 * box_width
    right_pred = centre_x + 0.5 * box_width
    lower_pred = centre_y - 0.5 * box_height
    upper_pred = centre_y + 0.5 * box_height
    target = target_box.astype(jnp.float32)
    inner_width = soft_relu(soft_min(right_pred, target[:, 2]) - soft_max(left_pred, target[:, 0]))
    inner_height = soft_relu(
        soft_min(upper_pred, target[:, 3]) - soft_max(lower_pred, target[:, 1])
    )
    intersection_area = inner_width * inner_height
    target_area = (target[:, 2] - target[:, 0]) * (target[:, 3] - target[:, 1])
    union_area = box_width * box_height + target_area - intersection_area
    outer_width = soft_max(right_pred, target[:, 2]) - soft_min(left_pred, target[:, 0])
    outer_height = soft_max(upper_pred, target[:, 3]) - soft_min(lower_pred, target[:, 1])
    enclosing = outer_width * outer_height
    return loss_scale * jnp.mean(
        1.0 - intersection_area / union_area + (enclosing - union_area) / enclosing
    )


def head_pool(final_rows, head_gain, head_weight, prompt_length, keep_mask):
    row_count = keep_mask.shape[0]
    positions = jnp.arange(keep_mask.shape[1], dtype=jnp.int32)[None, :]
    starts = prompt_length[:, None]
    weights = (positions == starts - 1).astype(jnp.float32) + (positions >= starts).astype(
        jnp.float32
    ) * keep_mask.astype(jnp.float32)
    counts = jnp.sum(weights, axis=1)
    local_width = final_rows.shape[1]
    tokens = final_rows.astype(jnp.float32).reshape(row_count, keep_mask.shape[1], local_width)
    pooled = (
        jnp.einsum("rt,rtd->rd", weights, tokens, precision=lax.Precision.HIGHEST) / counts[:, None]
    )
    gain_cols = lax.dynamic_slice_in_dim(head_gain, column_start(local_width), local_width, 0)
    logit_part = jnp.dot(pooled * gain_cols, head_weight, precision=lax.Precision.HIGHEST)
    square_part = jnp.sum(pooled * pooled, axis=1, keepdims=True)
    return (weights, counts, pooled, gain_cols), jnp.concatenate([logit_part, square_part], axis=1)


def head_middle(pooled_state, totals, head_weight, head_bias, target_box):
    weights, counts, pooled, gain_cols = pooled_state
    full_width = pooled.shape[1] * tensor_size()
    inverse = lax.rsqrt(totals[:, 4] / full_width + epsilon)
    logits = totals[:, :4] * inverse[:, None] + head_bias

    def loss_of(logit_value):
        return box_loss(logit_value, target_box)

    loss_value, pullback = jax.vjp(loss_of, logits)
    logit_grad = pullback(jnp.ones((), jnp.float32))[0]
    scaled_grad = jnp.dot(logit_grad, head_weight.T, precision=lax.Precision.HIGHEST)
    unit_pooled = pooled * inverse[:, None]
    return (inverse, scaled_grad, unit_pooled), jnp.sum(unit_pooled * gain_cols * scaled_grad, axis=1)


def head_finish(pooled_state, middle_state, row_total, row_shape):
    weights, counts, pooled, gain_cols = pooled_state
    inverse, scaled_grad, unit_pooled = middle_state
    full_width = pooled.shape[1] * tensor_size()
    pooled_grad = inverse[:, None] * (
        gain_cols * scaled_grad - unit_pooled * row_total[:, None] / full_width
    )
    token_grad = (weights / counts[:, None])[:, :, None] * pooled_grad[:, None, :]
    return token_grad.reshape(row_shape).astype(jnp.bfloat16)


def per_device(
    forward_input,
    saved_last,
    saved_first,
    first_cotangent,
    section_entry,
    last_gain,
    last_up,
    last_down,
    first_gain,
    first_up,
    first_down,
    head_gain,
    head_weight,
    head_bias,
    prompt_length,
    keep_mask,
    target_box,
):
    section_index = lax.axis_index("section")
    opening = section_index == 0
    closing = section_index == lax.axis_size("section") - 1
    local_input = forward_input[0]
    width = local_input.shape[1]
    full_width = width * tensor_size()
    last_gain_cols = lax.dynamic_slice_in_dim(last_gain[0], column_start(width), width, 0)
    first_gain_cols = lax.dynamic_slice_in_dim(first_gain[0], column_start(width), width, 0)
    closing_saved = jnp.where(closing, local_input, saved_last[0])
    squares = row_sums(
        jnp.stack(
            [local_squares(local_input), local_squares(saved_first[0]), local_squares(closing_saved)]
        ),
        9,
    )
    squares, up_last, down_last, up_first, down_first = lax.optimization_barrier(
        (squares, last_up[0], last_down[0], first_up[0], first_down[0])
    )
    last_up_local, last_down_local = spread_weights(up_last, down_last)
    first_up_local, first_down_local = spread_weights(up_first, down_first)
    last_pre = layer_forward(local_input, squares[0], last_gain_cols, last_up_local, full_width)
    first_pre, first_grad_part, first_scaled, first_inverse = layer_back_partials(
        saved_first[0], squares[1], first_cotangent[0], first_gain_cols, first_up_local,
        first_down_local, full_width,
    )
    reduced = reduce_columns(jnp.stack([last_pre, first_pre, first_grad_part]), 3, jnp.float32)
    last_act = jax.nn.silu(reduced[0]).astype(jnp.bfloat16)
    first_pre_grad = pre_gradient(reduced[1], reduced[2])
    spread = gather_columns(jnp.stack([last_act, first_pre_grad]), 0)
    last_out = grouped_sum(spread[0], last_down_local, "rows")
    hidden_local = (local_input.astype(jnp.float32) + last_out).astype(jnp.bfloat16)
    first_norm_grad = grouped_sum(spread[1], first_up_local, "cols")
    rows = first_norm_grad.shape[0]
    pooled_state, head_part = head_pool(
        hidden_local, head_gain, head_weight, prompt_length, keep_mask
    )
    first_projection = back_projection(first_scaled, first_gain_cols, first_norm_grad)
    joined = row_sums(jnp.concatenate([first_projection, head_part.reshape(-1)]), 7)
    first_grad = back_finish(
        first_cotangent[0], first_norm_grad, first_scaled, first_inverse, first_gain_cols,
        full_width, joined[:rows],
    )
    arrived_local = shifted(hidden_local, "section", 1)
    returned = shifted(first_grad, "section", -1)
    middle_state, head_row = head_middle(
        pooled_state, joined[rows:].reshape(head_part.shape), head_weight, head_bias, target_box
    )
    entry_local = jnp.where(opening, section_entry, arrived_local)
    late_joined = row_sums(jnp.concatenate([local_squares(entry_local), head_row]), 10)
    entry_squares = late_joined[:rows]
    head_grad = head_finish(pooled_state, middle_state, late_joined[rows:], hidden_local.shape)
    cotangent = jnp.where(closing, head_grad, returned)
    first_pre_late = layer_forward(entry_local, entry_squares, first_gain_cols, first_up_local, full_width)
    last_pre_late, last_grad_part, last_scaled, last_inverse = layer_back_partials(
        closing_saved, squares[2], cotangent, last_gain_cols, last_up_local, last_down_local,
        full_width,
    )
    reduced_late = reduce_columns(
        jnp.stack([first_pre_late, last_pre_late, last_grad_part]), 4, jnp.float32
    )
    first_act = jax.nn.silu(reduced_late[0]).astype(jnp.bfloat16)
    last_pre_grad = pre_gradient(reduced_late[1], reduced_late[2])
    spread_late = gather_columns(jnp.stack([first_act, last_pre_grad]), 1)
    first_out = grouped_sum(spread_late[0], first_down_local, "rows")
    layer_output = (entry_local.astype(jnp.float32) + first_out).astype(jnp.bfloat16)
    last_norm_grad = grouped_sum(spread_late[1], last_up_local, "cols")
    last_total = row_sums(back_projection(last_scaled, last_gain_cols, last_norm_grad), 8)
    input_gradient = back_finish(
        cotangent, last_norm_grad, last_scaled, last_inverse, last_gain_cols, full_width, last_total
    )
    return (layer_output[None], input_gradient[None])


def solution(mesh):
    sections = mesh.shape["section"]
    tensors = mesh.shape["tensor"]
    split = Mesh(mesh.devices.reshape(sections, tensors // 2, 2), ("section", "ty", "tz"))
    rows = P("section", None, TENSOR)
    placed = (
        rows,
        rows,
        rows,
        rows,
        P(None, TENSOR),
        P("section", None),
        rows,
        P("section", TENSOR, None),
        P("section", None),
        rows,
        P("section", TENSOR, None),
        P(),
        P(TENSOR, None),
        P(),
        P(),
        P(),
        P(),
    )
    return jax.shard_map(
        per_device,
        mesh=split,
        in_specs=placed,
        out_specs=(rows, rows),
        check_vma=False,
    )
```

```python
import functools

import jax
import jax.numpy as jnp
from jax import lax
from jax.experimental import pallas as pl
from jax.experimental.pallas import tpu as pltpu
from jax.sharding import Mesh
from jax.sharding import PartitionSpec as P

epsilon = 1e-06
softness = 4.0
loss_scale = 4096.0
TENSOR = ("ty", "tz")


def shifted(value, axis, steps):
    count = lax.axis_size(axis)
    initial, last = (max(0, -steps), min(count, count - steps))
    return lax.ppermute(value, axis, [(source, source + steps) for source in range(initial, last)])


def tensor_size():
    return lax.axis_size("ty") * lax.axis_size("tz")


def tensor_index():
    return lax.axis_index("ty") * lax.axis_size("tz") + lax.axis_index("tz")


def unit_rows(values):
    values = values.astype(jnp.float32)
    inverse = lax.rsqrt(jnp.mean(values * values, axis=-1, keepdims=True) + epsilon)
    return (values * inverse, inverse)


def column_start(local_width):
    return tensor_index() * local_width


def column_slice(full_rows, local_width):
    return lax.dynamic_slice_in_dim(full_rows, column_start(local_width), local_width, 1)


MESH_ID = pl.DeviceIdType.MESH


def gather_kernel(ny, nz, x_ref, out_ref, send_sems, recv_sems):
    width = x_ref.shape[2]
    ty, tz = lax.axis_index("ty"), lax.axis_index("tz")
    me = ty * nz + tz
    partner_z = 1 - tz
    partner = ty * nz + partner_z
    y_peers = [lax.rem(ty + step, ny) for step in range(1, ny)]
    section = lax.axis_index("section")

    def device(y, z):
        return (section, y, z)

    def cols(index):
        return pl.ds(pl.multiple_of(index * width, width), width)

    barrier = pltpu.get_barrier_semaphore()
    pl.semaphore_signal(barrier, inc=1, device_id=device(ty, partner_z), device_id_type=MESH_ID)
    for y in y_peers:
        pl.semaphore_signal(barrier, inc=1, device_id=device(y, tz), device_id_type=MESH_ID)
    pl.semaphore_wait(barrier, ny)

    sends = [
        pltpu.make_async_remote_copy(
            src_ref=x_ref,
            dst_ref=out_ref.at[:, :, cols(me)],
            send_sem=send_sems.at[0],
            recv_sem=recv_sems.at[me],
            device_id=device(ty, partner_z),
            device_id_type=MESH_ID,
        )
    ]
    for number, y in enumerate(y_peers):
        sends.append(
            pltpu.make_async_remote_copy(
                src_ref=x_ref,
                dst_ref=out_ref.at[:, :, cols(me)],
                send_sem=send_sems.at[1 + number],
                recv_sem=recv_sems.at[me],
                device_id=device(y, tz),
                device_id_type=MESH_ID,
            )
        )
    for copy in sends:
        copy.start()
    out_ref[:, :, cols(me)] = x_ref[...]
    pltpu.make_async_remote_copy(
        src_ref=x_ref,
        dst_ref=out_ref.at[:, :, cols(partner)],
        send_sem=send_sems.at[0],
        recv_sem=recv_sems.at[partner],
        device_id=device(ty, partner_z),
        device_id_type=MESH_ID,
    ).wait_recv()
    forwards = []
    for number, y in enumerate(y_peers):
        forwards.append(
            pltpu.make_async_remote_copy(
                src_ref=out_ref.at[:, :, cols(partner)],
                dst_ref=out_ref.at[:, :, cols(partner)],
                send_sem=send_sems.at[ny + number],
                recv_sem=recv_sems.at[partner],
                device_id=device(y, tz),
                device_id_type=MESH_ID,
            )
        )
    for copy in forwards:
        copy.start()
    for y in y_peers:
        for z in range(nz):
            source = y * nz + z
            pltpu.make_async_remote_copy(
                src_ref=x_ref,
                dst_ref=out_ref.at[:, :, cols(source)],
                send_sem=send_sems.at[0],
                recv_sem=recv_sems.at[source],
                device_id=device(y, z),
                device_id_type=MESH_ID,
            ).wait_recv()
    for copy in sends + forwards:
        copy.wait_send()


def gather_columns(local_rows, collective):
    k, rows, width = local_rows.shape
    ny, nz = lax.axis_size("ty"), lax.axis_size("tz")
    full = width * ny * nz
    moved = local_rows.size * local_rows.dtype.itemsize * 7
    return pl.pallas_call(
        functools.partial(gather_kernel, ny, nz),
        out_shape=jax.ShapeDtypeStruct((k, rows, full), local_rows.dtype),
        in_specs=[pl.BlockSpec(memory_space=pltpu.VMEM)],
        out_specs=pl.BlockSpec(memory_space=pltpu.VMEM),
        scratch_shapes=[
            pltpu.SemaphoreType.DMA((2 * ny - 1,)),
            pltpu.SemaphoreType.DMA((ny * nz,)),
        ],
        compiler_params=pltpu.CompilerParams(
            collective_id=collective, has_side_effects=True, vmem_limit_bytes=48 * 1024 * 1024
        ),
        cost_estimate=pl.CostEstimate(flops=0, transcendentals=0, bytes_accessed=moved),
    )(local_rows)


def scatter_kernel(ny, nz, part_ref, out_ref, stage, z_send, z_recv, send_sems, recv_sems, z_sems):
    k, rows, width = out_ref.shape
    pair = nz * width
    ty, tz = lax.axis_index("ty"), lax.axis_index("tz")
    partner_z = 1 - tz
    section = lax.axis_index("section")
    chunk = 32

    def device(y, z):
        return (section, y, z)

    barrier = pltpu.get_barrier_semaphore()
    pl.semaphore_signal(barrier, inc=1, device_id=device(ty, partner_z), device_id_type=MESH_ID)
    for step in range(1, ny):
        pl.semaphore_signal(
            barrier, inc=1, device_id=device(lax.rem(ty + step, ny), tz), device_id_type=MESH_ID
        )
    pl.semaphore_wait(barrier, ny)

    sends = []
    for step in range(1, ny):
        peer = lax.rem(ty + step, ny)
        copy = pltpu.make_async_remote_copy(
            src_ref=part_ref.at[:, :, pl.ds(pl.multiple_of(peer * pair, pair), pair)],
            dst_ref=stage.at[ny - step - 1],
            send_sem=send_sems.at[step - 1],
            recv_sem=recv_sems.at[ny - step - 1],
            device_id=device(peer, tz),
            device_id_type=MESH_ID,
        )
        copy.start()
        sends.append(copy)
    for slot in range(ny - 1):
        pltpu.make_async_remote_copy(
            src_ref=stage.at[slot],
            dst_ref=stage.at[slot],
            send_sem=send_sems.at[0],
            recv_sem=recv_sems.at[slot],
            device_id=device(ty, partner_z),
            device_id_type=MESH_ID,
        ).wait_recv()

    def add_terms(z, target):
        own = pl.multiple_of((ty * nz + z) * width, width)
        inside = pl.multiple_of(z * width, width)

        def body(step, carry):
            plane = step // (rows // chunk)
            row = pl.multiple_of((step % (rows // chunk)) * chunk, chunk)
            total = part_ref[plane, pl.ds(row, chunk), pl.ds(own, width)].astype(jnp.float32)
            for slot in range(ny - 1):
                total += stage[slot, plane, pl.ds(row, chunk), pl.ds(inside, width)].astype(
                    jnp.float32
                )
            target(plane, row, total)
            return carry

        lax.fori_loop(0, k * (rows // chunk), body, 0)

    def to_send(plane, row, total):
        z_send[plane, pl.ds(row, chunk), :] = total

    add_terms(partner_z, to_send)
    z_copy = pltpu.make_async_remote_copy(
        src_ref=z_send,
        dst_ref=z_recv,
        send_sem=z_sems.at[0],
        recv_sem=z_sems.at[1],
        device_id=device(ty, partner_z),
        device_id_type=MESH_ID,
    )
    z_copy.start()

    def to_out(plane, row, total):
        out_ref[plane, pl.ds(row, chunk), :] = total

    add_terms(tz, to_out)
    z_copy.wait_recv()
    out_ref[...] += z_recv[...]
    z_copy.wait_send()
    for copy in sends:
        copy.wait_send()


def reduce_columns(partial_rows, collective, term_type=jnp.bfloat16):
    k, rows, full = partial_rows.shape
    ny, nz = lax.axis_size("ty"), lax.axis_size("tz")
    width = full // (ny * nz)
    terms = partial_rows.astype(term_type)
    moved = terms.size * terms.dtype.itemsize
    return pl.pallas_call(
        functools.partial(scatter_kernel, ny, nz),
        out_shape=jax.ShapeDtypeStruct((k, rows, width), jnp.float32),
        in_specs=[pl.BlockSpec(memory_space=pltpu.VMEM)],
        out_specs=pl.BlockSpec(memory_space=pltpu.VMEM),
        scratch_shapes=[
            pltpu.VMEM((ny - 1, k, rows, nz * width), term_type),
            pltpu.VMEM((k, rows, width), jnp.float32),
            pltpu.VMEM((k, rows, width), jnp.float32),
            pltpu.SemaphoreType.DMA((ny - 1,)),
            pltpu.SemaphoreType.DMA((ny - 1,)),
            pltpu.SemaphoreType.DMA((2,)),
        ],
        compiler_params=pltpu.CompilerParams(
            collective_id=collective, has_side_effects=True, vmem_limit_bytes=56 * 1024 * 1024
        ),
        cost_estimate=pl.CostEstimate(flops=terms.size, transcendentals=0, bytes_accessed=moved),
    )(terms)


def sum_kernel(ny, nz, v_ref, out_ref, slots, send_sems, recv_sems):
    ty, tz = lax.axis_index("ty"), lax.axis_index("tz")
    me = ty * nz + tz
    section = lax.axis_index("section")
    peers = [(lax.rem(ty + dy, ny), lax.rem(tz + dz, nz)) for dy in range(ny) for dz in range(nz)][1:]

    barrier = pltpu.get_barrier_semaphore()
    for y, z in peers:
        pl.semaphore_signal(barrier, inc=1, device_id=(section, y, z), device_id_type=MESH_ID)
    pl.semaphore_wait(barrier, len(peers))
    sends = []
    for number, (y, z) in enumerate(peers):
        copy = pltpu.make_async_remote_copy(
            src_ref=v_ref,
            dst_ref=slots.at[me],
            send_sem=send_sems.at[number],
            recv_sem=recv_sems.at[me],
            device_id=(section, y, z),
            device_id_type=MESH_ID,
        )
        copy.start()
        sends.append(copy)
    slots[me] = v_ref[...]
    for y, z in peers:
        source = y * nz + z
        pltpu.make_async_remote_copy(
            src_ref=v_ref,
            dst_ref=slots.at[source],
            send_sem=send_sems.at[0],
            recv_sem=recv_sems.at[source],
            device_id=(section, y, z),
            device_id_type=MESH_ID,
        ).wait_recv()
    total = slots[0]
    for source in range(1, ny * nz):
        total = total + slots[source]
    out_ref[...] = total
    for copy in sends:
        copy.wait_send()


def row_sums(values, collective):
    shape = values.shape
    flat = values.reshape(-1).astype(jnp.float32)
    lanes = 128
    padded = -(-flat.shape[0] // lanes) * lanes
    rows = jnp.pad(flat, (0, padded - flat.shape[0])).reshape(padded // lanes, lanes)
    ny, nz = lax.axis_size("ty"), lax.axis_size("tz")
    summed = pl.pallas_call(
        functools.partial(sum_kernel, ny, nz),
        out_shape=jax.ShapeDtypeStruct(rows.shape, jnp.float32),
        in_specs=[pl.BlockSpec(memory_space=pltpu.VMEM)],
        out_specs=pl.BlockSpec(memory_space=pltpu.VMEM),
        scratch_shapes=[
            pltpu.VMEM((ny * nz,) + rows.shape, jnp.float32),
            pltpu.SemaphoreType.DMA((ny * nz - 1,)),
            pltpu.SemaphoreType.DMA((ny * nz,)),
        ],
        compiler_params=pltpu.CompilerParams(collective_id=collective, has_side_effects=True),
        cost_estimate=pl.CostEstimate(flops=rows.size * 8, transcendentals=0, bytes_accessed=rows.size * 64),
    )(rows)
    return summed.reshape(-1)[: flat.shape[0]].reshape(shape)


def spread_kernel(ny, nz, *refs):
    ups_in, downs_in = refs[0:4:2], refs[1:4:2]
    ups_out, downs_out = refs[4:8:2], refs[5:8:2]
    send_sems, recv_sems, local_sems = refs[8:]
    n = ny * nz
    ty, tz = lax.axis_index("ty"), lax.axis_index("tz")
    me = ty * nz + tz
    section = lax.axis_index("section")
    width, hidden = ups_in[0].shape[0] // n, ups_in[0].shape[1]
    peers = [(lax.rem(ty + dy, ny), lax.rem(tz + dz, nz)) for dy in range(ny) for dz in range(nz)][1:]

    def up_rows(index):
        return pl.ds(pl.multiple_of(index * width, width), width)

    def hidden_part(index):
        return pl.ds(pl.multiple_of(index * hidden, hidden), hidden)

    pieces = []
    for layer in range(2):
        up_in, down_in, up_out, down_out = ups_in[layer], downs_in[layer], ups_out[layer], downs_out[layer]
        pieces.append(
            (lambda i, r=up_in: r.at[up_rows(i), :], lambda i, r=up_out: r.at[:, hidden_part(i)])
        )
        pieces.append(
            (lambda i, r=down_in: r.at[:, up_rows(i)], lambda i, r=down_out: r.at[hidden_part(i), :])
        )

    barrier = pltpu.get_barrier_semaphore()
    for y, z in peers:
        pl.semaphore_signal(barrier, inc=1, device_id=(section, y, z), device_id_type=MESH_ID)
    pl.semaphore_wait(barrier, len(peers))
    started, own_copies = [], []
    for piece, (source, target) in enumerate(pieces):
        for number, (y, z) in enumerate(peers):
            copy = pltpu.make_async_remote_copy(
                src_ref=source(y * nz + z),
                dst_ref=target(me),
                send_sem=send_sems.at[piece, number],
                recv_sem=recv_sems.at[piece, me],
                device_id=(section, y, z),
                device_id_type=MESH_ID,
            )
            copy.start()
            started.append(copy)
        own = pltpu.make_async_copy(source(me), target(me), local_sems.at[piece])
        own.start()
        own_copies.append(own)
    for piece, (source, target) in enumerate(pieces):
        for y, z in peers:
            index = y * nz + z
            pltpu.make_async_remote_copy(
                src_ref=source(index),
                dst_ref=target(index),
                send_sem=send_sems.at[piece, 0],
                recv_sem=recv_sems.at[piece, index],
                device_id=(section, y, z),
                device_id_type=MESH_ID,
            ).wait_recv()
    for copy in own_copies:
        copy.wait()
    for copy in started:
        copy.wait_send()


def spread_weights(last_up, last_down, first_up, first_down):
    ny, nz = lax.axis_size("ty"), lax.axis_size("tz")
    n = ny * nz
    full, hidden = last_up.shape
    up_shape = jax.ShapeDtypeStruct((full // n, n * hidden), last_up.dtype)
    down_shape = jax.ShapeDtypeStruct((n * hidden, full // n), last_down.dtype)
    moved = 4 * last_up.size * last_up.dtype.itemsize
    return pl.pallas_call(
        functools.partial(spread_kernel, ny, nz),
        out_shape=(up_shape, down_shape, up_shape, down_shape),
        in_specs=[pl.BlockSpec(memory_space=pl.ANY)] * 4,
        out_specs=(pl.BlockSpec(memory_space=pl.ANY),) * 4,
        scratch_shapes=[
            pltpu.SemaphoreType.DMA((4, n - 1)),
            pltpu.SemaphoreType.DMA((4, n)),
            pltpu.SemaphoreType.DMA((4,)),
        ],
        compiler_params=pltpu.CompilerParams(collective_id=11, has_side_effects=True),
        cost_estimate=pl.CostEstimate(flops=0, transcendentals=0, bytes_accessed=moved),
    )(last_up, last_down, first_up, first_down)


def grouped_sum(left, right, contract):
    n = tensor_size()
    rows = left.shape[0]
    hidden = left.shape[1] // n
    left_groups = left.reshape(rows, n, hidden)
    if contract == "rows":
        right_groups = right.reshape(n, hidden, right.shape[1])
        terms = jnp.einsum("tgk,gkf->gtf", left_groups, right_groups, preferred_element_type=jnp.float32)
    else:
        right_groups = right.reshape(right.shape[0], n, hidden)
        terms = jnp.einsum("tgk,fgk->gtf", left_groups, right_groups, preferred_element_type=jnp.float32)
    return jnp.sum(terms.astype(jnp.bfloat16).astype(jnp.float32), axis=0)


def normed_rows(local_rows, total_squares, gain_cols, full_width):
    values = local_rows.astype(jnp.float32)
    inverse = lax.rsqrt(total_squares[:, None] / full_width + epsilon)
    scaled = values * inverse
    return scaled, inverse, (scaled * gain_cols).astype(jnp.bfloat16)


def local_squares(local_rows):
    values = local_rows.astype(jnp.float32)
    return jnp.sum(values * values, axis=-1)


def layer_forward(local_rows, squares, gain_cols, up_local, full_width):
    scaled, inverse, normed = normed_rows(local_rows, squares, gain_cols, full_width)
    return jnp.dot(normed, up_local, preferred_element_type=jnp.float32)


def layer_back_partials(saved_rows, squares, cotangent, gain_cols, up_local, down_local, full_width):
    scaled, inverse, normed = normed_rows(saved_rows, squares, gain_cols, full_width)
    pre_part = jnp.dot(normed, up_local, preferred_element_type=jnp.float32)
    grad_part = lax.dot_general(
        cotangent, down_local, (((1,), (1,)), ((), ())), preferred_element_type=jnp.float32
    )
    return pre_part, grad_part, scaled, inverse


def pre_gradient(pre_act, act_grad):
    sigmoid_pre = jax.nn.sigmoid(pre_act)
    return (act_grad * sigmoid_pre * (1.0 + pre_act * (1.0 - sigmoid_pre))).astype(jnp.bfloat16)


def back_projection(scaled, gain_cols, norm_grad):
    return jnp.sum(scaled * gain_cols * norm_grad, axis=1)


def back_finish(cotangent, norm_grad, scaled, inverse, gain_cols, full_width, row_total):
    result = cotangent.astype(jnp.float32) + inverse * (
        gain_cols * norm_grad - scaled * row_total[:, None] / full_width
    )
    return result.astype(jnp.bfloat16)


def soft_min(first, second):
    return 0.5 * (
        first + second - jnp.sqrt((first - second) * (first - second) + softness * softness)
    )


def soft_max(first, second):
    return 0.5 * (
        first + second + jnp.sqrt((first - second) * (first - second) + softness * softness)
    )


def soft_relu(difference):
    return 0.5 * (difference + jnp.sqrt(difference * difference + softness * softness))


def box_loss(logits, target_box):
    scaled_box = jax.nn.sigmoid(logits) * 1000.0
    centre_x = scaled_box[:, 0]
    centre_y = scaled_box[:, 1]
    box_width = scaled_box[:, 2]
    box_height = scaled_box[:, 3]
    left_pred = centre_x - 0.5 * box_width
    right_pred = centre_x + 0.5 * box_width
    lower_pred = centre_y - 0.5 * box_height
    upper_pred = centre_y + 0.5 * box_height
    target = target_box.astype(jnp.float32)
    inner_width = soft_relu(soft_min(right_pred, target[:, 2]) - soft_max(left_pred, target[:, 0]))
    inner_height = soft_relu(
        soft_min(upper_pred, target[:, 3]) - soft_max(lower_pred, target[:, 1])
    )
    intersection_area = inner_width * inner_height
    target_area = (target[:, 2] - target[:, 0]) * (target[:, 3] - target[:, 1])
    union_area = box_width * box_height + target_area - intersection_area
    outer_width = soft_max(right_pred, target[:, 2]) - soft_min(left_pred, target[:, 0])
    outer_height = soft_max(upper_pred, target[:, 3]) - soft_min(lower_pred, target[:, 1])
    enclosing = outer_width * outer_height
    return loss_scale * jnp.mean(
        1.0 - intersection_area / union_area + (enclosing - union_area) / enclosing
    )


def head_pool(final_rows, head_gain, head_weight, prompt_length, keep_mask):
    row_count = keep_mask.shape[0]
    positions = jnp.arange(keep_mask.shape[1], dtype=jnp.int32)[None, :]
    starts = prompt_length[:, None]
    weights = (positions == starts - 1).astype(jnp.float32) + (positions >= starts).astype(
        jnp.float32
    ) * keep_mask.astype(jnp.float32)
    counts = jnp.sum(weights, axis=1)
    local_width = final_rows.shape[1]
    tokens = final_rows.astype(jnp.float32).reshape(row_count, keep_mask.shape[1], local_width)
    pooled = (
        jnp.einsum("rt,rtd->rd", weights, tokens, precision=lax.Precision.HIGHEST) / counts[:, None]
    )
    gain_cols = lax.dynamic_slice_in_dim(head_gain, column_start(local_width), local_width, 0)
    logit_part = jnp.dot(pooled * gain_cols, head_weight, precision=lax.Precision.HIGHEST)
    square_part = jnp.sum(pooled * pooled, axis=1, keepdims=True)
    return (weights, counts, pooled, gain_cols), jnp.concatenate([logit_part, square_part], axis=1)


def head_middle(pooled_state, totals, head_weight, head_bias, target_box):
    weights, counts, pooled, gain_cols = pooled_state
    full_width = pooled.shape[1] * tensor_size()
    inverse = lax.rsqrt(totals[:, 4] / full_width + epsilon)
    logits = totals[:, :4] * inverse[:, None] + head_bias

    def loss_of(logit_value):
        return box_loss(logit_value, target_box)

    loss_value, pullback = jax.vjp(loss_of, logits)
    logit_grad = pullback(jnp.ones((), jnp.float32))[0]
    scaled_grad = jnp.dot(logit_grad, head_weight.T, precision=lax.Precision.HIGHEST)
    unit_pooled = pooled * inverse[:, None]
    return (inverse, scaled_grad, unit_pooled), jnp.sum(unit_pooled * gain_cols * scaled_grad, axis=1)


def head_finish(pooled_state, middle_state, row_total, row_shape):
    weights, counts, pooled, gain_cols = pooled_state
    inverse, scaled_grad, unit_pooled = middle_state
    full_width = pooled.shape[1] * tensor_size()
    pooled_grad = inverse[:, None] * (
        gain_cols * scaled_grad - unit_pooled * row_total[:, None] / full_width
    )
    token_grad = (weights / counts[:, None])[:, :, None] * pooled_grad[:, None, :]
    return token_grad.reshape(row_shape).astype(jnp.bfloat16)


def per_device(
    forward_input,
    saved_last,
    saved_first,
    first_cotangent,
    section_entry,
    last_gain,
    last_up,
    last_down,
    first_gain,
    first_up,
    first_down,
    head_gain,
    head_weight,
    head_bias,
    prompt_length,
    keep_mask,
    target_box,
):
    section_index = lax.axis_index("section")
    opening = section_index == 0
    closing = section_index == lax.axis_size("section") - 1
    local_input = forward_input[0]
    width = local_input.shape[1]
    full_width = width * tensor_size()
    last_gain_cols = lax.dynamic_slice_in_dim(last_gain[0], column_start(width), width, 0)
    first_gain_cols = lax.dynamic_slice_in_dim(first_gain[0], column_start(width), width, 0)
    closing_saved = jnp.where(closing, local_input, saved_last[0])
    squares = row_sums(
        jnp.stack(
            [local_squares(local_input), local_squares(saved_first[0]), local_squares(closing_saved)]
        ),
        9,
    )
    squares, up_last, down_last, up_first, down_first = lax.optimization_barrier(
        (squares, last_up[0], last_down[0], first_up[0], first_down[0])
    )
    last_up_local, last_down_local, first_up_local, first_down_local = spread_weights(
        up_last, down_last, up_first, down_first
    )
    last_pre = layer_forward(local_input, squares[0], last_gain_cols, last_up_local, full_width)
    first_pre, first_grad_part, first_scaled, first_inverse = layer_back_partials(
        saved_first[0], squares[1], first_cotangent[0], first_gain_cols, first_up_local,
        first_down_local, full_width,
    )
    reduced = reduce_columns(jnp.stack([last_pre, first_pre, first_grad_part]), 3, jnp.float32)
    last_act = jax.nn.silu(reduced[0]).astype(jnp.bfloat16)
    first_pre_grad = pre_gradient(reduced[1], reduced[2])
    spread = gather_columns(jnp.stack([last_act, first_pre_grad]), 0)
    last_out = grouped_sum(spread[0], last_down_local, "rows")
    hidden_local = (local_input.astype(jnp.float32) + last_out).astype(jnp.bfloat16)
    first_norm_grad = grouped_sum(spread[1], first_up_local, "cols")
    rows = first_norm_grad.shape[0]
    pooled_state, head_part = head_pool(
        hidden_local, head_gain, head_weight, prompt_length, keep_mask
    )
    first_projection = back_projection(first_scaled, first_gain_cols, first_norm_grad)
    joined = row_sums(jnp.concatenate([first_projection, head_part.reshape(-1)]), 7)
    first_grad = back_finish(
        first_cotangent[0], first_norm_grad, first_scaled, first_inverse, first_gain_cols,
        full_width, joined[:rows],
    )
    arrived_local = shifted(hidden_local, "section", 1)
    returned = shifted(first_grad, "section", -1)
    middle_state, head_row = head_middle(
        pooled_state, joined[rows:].reshape(head_part.shape), head_weight, head_bias, target_box
    )
    entry_local = jnp.where(opening, section_entry, arrived_local)
    late_joined = row_sums(jnp.concatenate([local_squares(entry_local), head_row]), 10)
    entry_squares = late_joined[:rows]
    head_grad = head_finish(pooled_state, middle_state, late_joined[rows:], hidden_local.shape)
    cotangent = jnp.where(closing, head_grad, returned)
    first_pre_late = layer_forward(entry_local, entry_squares, first_gain_cols, first_up_local, full_width)
    last_pre_late, last_grad_part, last_scaled, last_inverse = layer_back_partials(
        closing_saved, squares[2], cotangent, last_gain_cols, last_up_local, last_down_local,
        full_width,
    )
    reduced_late = reduce_columns(
        jnp.stack([first_pre_late, last_pre_late, last_grad_part]), 4, jnp.float32
    )
    first_act = jax.nn.silu(reduced_late[0]).astype(jnp.bfloat16)
    last_pre_grad = pre_gradient(reduced_late[1], reduced_late[2])
    spread_late = gather_columns(jnp.stack([first_act, last_pre_grad]), 1)
    first_out = grouped_sum(spread_late[0], first_down_local, "rows")
    layer_output = (entry_local.astype(jnp.float32) + first_out).astype(jnp.bfloat16)
    last_norm_grad = grouped_sum(spread_late[1], last_up_local, "cols")
    last_total = row_sums(back_projection(last_scaled, last_gain_cols, last_norm_grad), 8)
    input_gradient = back_finish(
        cotangent, last_norm_grad, last_scaled, last_inverse, last_gain_cols, full_width, last_total
    )
    return (layer_output[None], input_gradient[None])


def solution(mesh):
    sections = mesh.shape["section"]
    tensors = mesh.shape["tensor"]
    split = Mesh(mesh.devices.reshape(sections, tensors // 2, 2), ("section", "ty", "tz"))
    rows = P("section", None, TENSOR)
    placed = (
        rows,
        rows,
        rows,
        rows,
        P(None, TENSOR),
        P("section", None),
        rows,
        P("section", TENSOR, None),
        P("section", None),
        rows,
        P("section", TENSOR, None),
        P(),
        P(TENSOR, None),
        P(),
        P(),
        P(),
        P(),
    )
    return jax.shard_map(
        per_device,
        mesh=split,
        in_specs=placed,
        out_specs=(rows, rows),
        check_vma=False,
    )
```

```python
import functools

import jax
import jax.numpy as jnp
from jax import lax
from jax.experimental import pallas as pl
from jax.experimental.pallas import tpu as pltpu
from jax.sharding import Mesh
from jax.sharding import PartitionSpec as P

epsilon = 1e-06
softness = 4.0
loss_scale = 4096.0
TENSOR = ("ty", "tz")


def shifted(value, axis, steps):
    count = lax.axis_size(axis)
    initial, last = (max(0, -steps), min(count, count - steps))
    return lax.ppermute(value, axis, [(source, source + steps) for source in range(initial, last)])


def tensor_size():
    return lax.axis_size("ty") * lax.axis_size("tz")


def tensor_index():
    return lax.axis_index("ty") * lax.axis_size("tz") + lax.axis_index("tz")


def unit_rows(values):
    values = values.astype(jnp.float32)
    inverse = lax.rsqrt(jnp.mean(values * values, axis=-1, keepdims=True) + epsilon)
    return (values * inverse, inverse)


def column_start(local_width):
    return tensor_index() * local_width


def column_slice(full_rows, local_width):
    return lax.dynamic_slice_in_dim(full_rows, column_start(local_width), local_width, 1)


MESH_ID = pl.DeviceIdType.MESH


def gather_kernel(ny, nz, x_ref, out_ref, send_sems, recv_sems):
    width = x_ref.shape[2]
    ty, tz = lax.axis_index("ty"), lax.axis_index("tz")
    me = ty * nz + tz
    partner_z = 1 - tz
    partner = ty * nz + partner_z
    y_peers = [lax.rem(ty + step, ny) for step in range(1, ny)]
    section = lax.axis_index("section")

    def device(y, z):
        return (section, y, z)

    def cols(index):
        return pl.ds(pl.multiple_of(index * width, width), width)

    barrier = pltpu.get_barrier_semaphore()
    pl.semaphore_signal(barrier, inc=1, device_id=device(ty, partner_z), device_id_type=MESH_ID)
    for y in y_peers:
        pl.semaphore_signal(barrier, inc=1, device_id=device(y, tz), device_id_type=MESH_ID)
    pl.semaphore_wait(barrier, ny)

    sends = [
        pltpu.make_async_remote_copy(
            src_ref=x_ref,
            dst_ref=out_ref.at[:, :, cols(me)],
            send_sem=send_sems.at[0],
            recv_sem=recv_sems.at[me],
            device_id=device(ty, partner_z),
            device_id_type=MESH_ID,
        )
    ]
    for number, y in enumerate(y_peers):
        sends.append(
            pltpu.make_async_remote_copy(
                src_ref=x_ref,
                dst_ref=out_ref.at[:, :, cols(me)],
                send_sem=send_sems.at[1 + number],
                recv_sem=recv_sems.at[me],
                device_id=device(y, tz),
                device_id_type=MESH_ID,
            )
        )
    for copy in sends:
        copy.start()
    out_ref[:, :, cols(me)] = x_ref[...]
    pltpu.make_async_remote_copy(
        src_ref=x_ref,
        dst_ref=out_ref.at[:, :, cols(partner)],
        send_sem=send_sems.at[0],
        recv_sem=recv_sems.at[partner],
        device_id=device(ty, partner_z),
        device_id_type=MESH_ID,
    ).wait_recv()
    forwards = []
    for number, y in enumerate(y_peers):
        forwards.append(
            pltpu.make_async_remote_copy(
                src_ref=out_ref.at[:, :, cols(partner)],
                dst_ref=out_ref.at[:, :, cols(partner)],
                send_sem=send_sems.at[ny + number],
                recv_sem=recv_sems.at[partner],
                device_id=device(y, tz),
                device_id_type=MESH_ID,
            )
        )
    for copy in forwards:
        copy.start()
    for y in y_peers:
        for z in range(nz):
            source = y * nz + z
            pltpu.make_async_remote_copy(
                src_ref=x_ref,
                dst_ref=out_ref.at[:, :, cols(source)],
                send_sem=send_sems.at[0],
                recv_sem=recv_sems.at[source],
                device_id=device(y, z),
                device_id_type=MESH_ID,
            ).wait_recv()
    for copy in sends + forwards:
        copy.wait_send()


def gather_columns(local_rows, collective):
    k, rows, width = local_rows.shape
    ny, nz = lax.axis_size("ty"), lax.axis_size("tz")
    full = width * ny * nz
    moved = local_rows.size * local_rows.dtype.itemsize * 7
    return pl.pallas_call(
        functools.partial(gather_kernel, ny, nz),
        out_shape=jax.ShapeDtypeStruct((k, rows, full), local_rows.dtype),
        in_specs=[pl.BlockSpec(memory_space=pltpu.VMEM)],
        out_specs=pl.BlockSpec(memory_space=pltpu.VMEM),
        scratch_shapes=[
            pltpu.SemaphoreType.DMA((2 * ny - 1,)),
            pltpu.SemaphoreType.DMA((ny * nz,)),
        ],
        compiler_params=pltpu.CompilerParams(
            collective_id=collective, has_side_effects=True, vmem_limit_bytes=48 * 1024 * 1024
        ),
        cost_estimate=pl.CostEstimate(flops=0, transcendentals=0, bytes_accessed=moved),
    )(local_rows)


def scatter_kernel(ny, nz, part_ref, out_ref, stage, z_send, z_recv, send_sems, recv_sems, z_sems):
    k, rows, width = out_ref.shape
    pair = nz * width
    ty, tz = lax.axis_index("ty"), lax.axis_index("tz")
    partner_z = 1 - tz
    section = lax.axis_index("section")
    chunk = 32

    def device(y, z):
        return (section, y, z)

    barrier = pltpu.get_barrier_semaphore()
    pl.semaphore_signal(barrier, inc=1, device_id=device(ty, partner_z), device_id_type=MESH_ID)
    for step in range(1, ny):
        pl.semaphore_signal(
            barrier, inc=1, device_id=device(lax.rem(ty + step, ny), tz), device_id_type=MESH_ID
        )
    pl.semaphore_wait(barrier, ny)

    sends = []
    for step in range(1, ny):
        peer = lax.rem(ty + step, ny)
        copy = pltpu.make_async_remote_copy(
            src_ref=part_ref.at[:, :, pl.ds(pl.multiple_of(peer * pair, pair), pair)],
            dst_ref=stage.at[ny - step - 1],
            send_sem=send_sems.at[step - 1],
            recv_sem=recv_sems.at[ny - step - 1],
            device_id=device(peer, tz),
            device_id_type=MESH_ID,
        )
        copy.start()
        sends.append(copy)
    for slot in range(ny - 1):
        pltpu.make_async_remote_copy(
            src_ref=stage.at[slot],
            dst_ref=stage.at[slot],
            send_sem=send_sems.at[0],
            recv_sem=recv_sems.at[slot],
            device_id=device(ty, partner_z),
            device_id_type=MESH_ID,
        ).wait_recv()

    def add_terms(z, target):
        own = pl.multiple_of((ty * nz + z) * width, width)
        inside = pl.multiple_of(z * width, width)

        def body(step, carry):
            plane = step // (rows // chunk)
            row = pl.multiple_of((step % (rows // chunk)) * chunk, chunk)
            total = part_ref[plane, pl.ds(row, chunk), pl.ds(own, width)].astype(jnp.float32)
            for slot in range(ny - 1):
                total += stage[slot, plane, pl.ds(row, chunk), pl.ds(inside, width)].astype(
                    jnp.float32
                )
            target(plane, row, total)
            return carry

        lax.fori_loop(0, k * (rows // chunk), body, 0)

    def to_send(plane, row, total):
        z_send[plane, pl.ds(row, chunk), :] = total

    add_terms(partner_z, to_send)
    z_copy = pltpu.make_async_remote_copy(
        src_ref=z_send,
        dst_ref=z_recv,
        send_sem=z_sems.at[0],
        recv_sem=z_sems.at[1],
        device_id=device(ty, partner_z),
        device_id_type=MESH_ID,
    )
    z_copy.start()

    def to_out(plane, row, total):
        out_ref[plane, pl.ds(row, chunk), :] = total

    add_terms(tz, to_out)
    z_copy.wait_recv()
    out_ref[...] += z_recv[...]
    z_copy.wait_send()
    for copy in sends:
        copy.wait_send()


def reduce_columns(partial_rows, collective, term_type=jnp.bfloat16):
    k, rows, full = partial_rows.shape
    ny, nz = lax.axis_size("ty"), lax.axis_size("tz")
    width = full // (ny * nz)
    terms = partial_rows.astype(term_type)
    moved = terms.size * terms.dtype.itemsize
    return pl.pallas_call(
        functools.partial(scatter_kernel, ny, nz),
        out_shape=jax.ShapeDtypeStruct((k, rows, width), jnp.float32),
        in_specs=[pl.BlockSpec(memory_space=pltpu.VMEM)],
        out_specs=pl.BlockSpec(memory_space=pltpu.VMEM),
        scratch_shapes=[
            pltpu.VMEM((ny - 1, k, rows, nz * width), term_type),
            pltpu.VMEM((k, rows, width), jnp.float32),
            pltpu.VMEM((k, rows, width), jnp.float32),
            pltpu.SemaphoreType.DMA((ny - 1,)),
            pltpu.SemaphoreType.DMA((ny - 1,)),
            pltpu.SemaphoreType.DMA((2,)),
        ],
        compiler_params=pltpu.CompilerParams(
            collective_id=collective, has_side_effects=True, vmem_limit_bytes=56 * 1024 * 1024
        ),
        cost_estimate=pl.CostEstimate(flops=terms.size, transcendentals=0, bytes_accessed=moved),
    )(terms)


def sum_kernel(ny, nz, v_ref, out_ref, slots, send_sems, recv_sems):
    ty, tz = lax.axis_index("ty"), lax.axis_index("tz")
    me = ty * nz + tz
    section = lax.axis_index("section")
    peers = [(lax.rem(ty + dy, ny), lax.rem(tz + dz, nz)) for dy in range(ny) for dz in range(nz)][1:]

    barrier = pltpu.get_barrier_semaphore()
    for y, z in peers:
        pl.semaphore_signal(barrier, inc=1, device_id=(section, y, z), device_id_type=MESH_ID)
    pl.semaphore_wait(barrier, len(peers))
    sends = []
    for number, (y, z) in enumerate(peers):
        copy = pltpu.make_async_remote_copy(
            src_ref=v_ref,
            dst_ref=slots.at[me],
            send_sem=send_sems.at[number],
            recv_sem=recv_sems.at[me],
            device_id=(section, y, z),
            device_id_type=MESH_ID,
        )
        copy.start()
        sends.append(copy)
    slots[me] = v_ref[...]
    for y, z in peers:
        source = y * nz + z
        pltpu.make_async_remote_copy(
            src_ref=v_ref,
            dst_ref=slots.at[source],
            send_sem=send_sems.at[0],
            recv_sem=recv_sems.at[source],
            device_id=(section, y, z),
            device_id_type=MESH_ID,
        ).wait_recv()
    total = slots[0]
    for source in range(1, ny * nz):
        total = total + slots[source]
    out_ref[...] = total
    for copy in sends:
        copy.wait_send()


def row_sums(values, collective):
    shape = values.shape
    flat = values.reshape(-1).astype(jnp.float32)
    lanes = 128
    padded = -(-flat.shape[0] // lanes) * lanes
    rows = jnp.pad(flat, (0, padded - flat.shape[0])).reshape(padded // lanes, lanes)
    ny, nz = lax.axis_size("ty"), lax.axis_size("tz")
    summed = pl.pallas_call(
        functools.partial(sum_kernel, ny, nz),
        out_shape=jax.ShapeDtypeStruct(rows.shape, jnp.float32),
        in_specs=[pl.BlockSpec(memory_space=pltpu.VMEM)],
        out_specs=pl.BlockSpec(memory_space=pltpu.VMEM),
        scratch_shapes=[
            pltpu.VMEM((ny * nz,) + rows.shape, jnp.float32),
            pltpu.SemaphoreType.DMA((ny * nz - 1,)),
            pltpu.SemaphoreType.DMA((ny * nz,)),
        ],
        compiler_params=pltpu.CompilerParams(collective_id=collective, has_side_effects=True),
        cost_estimate=pl.CostEstimate(flops=rows.size * 8, transcendentals=0, bytes_accessed=rows.size * 64),
    )(rows)
    return summed.reshape(-1)[: flat.shape[0]].reshape(shape)


def spread_kernel(ny, nz, *refs):
    ups_in, downs_in = refs[0:4:2], refs[1:4:2]
    ups_out, downs_out = refs[4:8:2], refs[5:8:2]
    send_sems, recv_sems, local_sems = refs[8:]
    n = ny * nz
    ty, tz = lax.axis_index("ty"), lax.axis_index("tz")
    me = ty * nz + tz
    section = lax.axis_index("section")
    width, hidden = ups_in[0].shape[0] // n, ups_in[0].shape[1]
    peers = [(lax.rem(ty + dy, ny), lax.rem(tz + dz, nz)) for dy in range(ny) for dz in range(nz)][1:]

    def up_rows(index):
        return pl.ds(pl.multiple_of(index * width, width), width)

    def hidden_part(index):
        return pl.ds(pl.multiple_of(index * hidden, hidden), hidden)

    pieces = []
    for layer in range(2):
        up_in, down_in, up_out, down_out = ups_in[layer], downs_in[layer], ups_out[layer], downs_out[layer]
        pieces.append(
            (lambda i, r=up_in: r.at[up_rows(i), :], lambda i, r=up_out: r.at[:, hidden_part(i)])
        )
        pieces.append(
            (lambda i, r=down_in: r.at[:, up_rows(i)], lambda i, r=down_out: r.at[hidden_part(i), :])
        )

    barrier = pltpu.get_barrier_semaphore()
    for y, z in peers:
        pl.semaphore_signal(barrier, inc=1, device_id=(section, y, z), device_id_type=MESH_ID)
    pl.semaphore_wait(barrier, len(peers))
    started, own_copies = [], []
    for piece, (source, target) in enumerate(pieces):
        for number, (y, z) in enumerate(peers):
            copy = pltpu.make_async_remote_copy(
                src_ref=source(y * nz + z),
                dst_ref=target(me),
                send_sem=send_sems.at[piece, number],
                recv_sem=recv_sems.at[piece, me],
                device_id=(section, y, z),
                device_id_type=MESH_ID,
            )
            copy.start()
            started.append(copy)
        own = pltpu.make_async_copy(source(me), target(me), local_sems.at[piece])
        own.start()
        own_copies.append(own)
        for copy in started[-len(peers):]:
            copy.wait_send()
    for piece, (source, target) in enumerate(pieces):
        for y, z in peers:
            index = y * nz + z
            pltpu.make_async_remote_copy(
                src_ref=source(index),
                dst_ref=target(index),
                send_sem=send_sems.at[piece, 0],
                recv_sem=recv_sems.at[piece, index],
                device_id=(section, y, z),
                device_id_type=MESH_ID,
            ).wait_recv()
    for copy in own_copies:
        copy.wait()


def spread_weights(last_up, last_down, first_up, first_down):
    ny, nz = lax.axis_size("ty"), lax.axis_size("tz")
    n = ny * nz
    full, hidden = last_up.shape
    up_shape = jax.ShapeDtypeStruct((full // n, n * hidden), last_up.dtype)
    down_shape = jax.ShapeDtypeStruct((n * hidden, full // n), last_down.dtype)
    moved = 4 * last_up.size * last_up.dtype.itemsize
    return pl.pallas_call(
        functools.partial(spread_kernel, ny, nz),
        out_shape=(up_shape, down_shape, up_shape, down_shape),
        in_specs=[pl.BlockSpec(memory_space=pl.ANY)] * 4,
        out_specs=(pl.BlockSpec(memory_space=pl.ANY),) * 4,
        scratch_shapes=[
            pltpu.SemaphoreType.DMA((4, n - 1)),
            pltpu.SemaphoreType.DMA((4, n)),
            pltpu.SemaphoreType.DMA((4,)),
        ],
        compiler_params=pltpu.CompilerParams(collective_id=11, has_side_effects=True),
        cost_estimate=pl.CostEstimate(flops=0, transcendentals=0, bytes_accessed=moved),
    )(last_up, last_down, first_up, first_down)


def grouped_sum(left, right, contract):
    n = tensor_size()
    rows = left.shape[0]
    hidden = left.shape[1] // n
    left_groups = left.reshape(rows, n, hidden)
    if contract == "rows":
        right_groups = right.reshape(n, hidden, right.shape[1])
        terms = jnp.einsum("tgk,gkf->gtf", left_groups, right_groups, preferred_element_type=jnp.float32)
    else:
        right_groups = right.reshape(right.shape[0], n, hidden)
        terms = jnp.einsum("tgk,fgk->gtf", left_groups, right_groups, preferred_element_type=jnp.float32)
    return jnp.sum(terms.astype(jnp.bfloat16).astype(jnp.float32), axis=0)


def normed_rows(local_rows, total_squares, gain_cols, full_width):
    values = local_rows.astype(jnp.float32)
    inverse = lax.rsqrt(total_squares[:, None] / full_width + epsilon)
    scaled = values * inverse
    return scaled, inverse, (scaled * gain_cols).astype(jnp.bfloat16)


def local_squares(local_rows):
    values = local_rows.astype(jnp.float32)
    return jnp.sum(values * values, axis=-1)


def layer_forward(local_rows, squares, gain_cols, up_local, full_width):
    scaled, inverse, normed = normed_rows(local_rows, squares, gain_cols, full_width)
    return jnp.dot(normed, up_local, preferred_element_type=jnp.float32)


def layer_back_partials(saved_rows, squares, cotangent, gain_cols, up_local, down_local, full_width):
    scaled, inverse, normed = normed_rows(saved_rows, squares, gain_cols, full_width)
    pre_part = jnp.dot(normed, up_local, preferred_element_type=jnp.float32)
    grad_part = lax.dot_general(
        cotangent, down_local, (((1,), (1,)), ((), ())), preferred_element_type=jnp.float32
    )
    return pre_part, grad_part, scaled, inverse


def pre_gradient(pre_act, act_grad):
    sigmoid_pre = jax.nn.sigmoid(pre_act)
    return (act_grad * sigmoid_pre * (1.0 + pre_act * (1.0 - sigmoid_pre))).astype(jnp.bfloat16)


def back_projection(scaled, gain_cols, norm_grad):
    return jnp.sum(scaled * gain_cols * norm_grad, axis=1)


def back_finish(cotangent, norm_grad, scaled, inverse, gain_cols, full_width, row_total):
    result = cotangent.astype(jnp.float32) + inverse * (
        gain_cols * norm_grad - scaled * row_total[:, None] / full_width
    )
    return result.astype(jnp.bfloat16)


def soft_min(first, second):
    return 0.5 * (
        first + second - jnp.sqrt((first - second) * (first - second) + softness * softness)
    )


def soft_max(first, second):
    return 0.5 * (
        first + second + jnp.sqrt((first - second) * (first - second) + softness * softness)
    )


def soft_relu(difference):
    return 0.5 * (difference + jnp.sqrt(difference * difference + softness * softness))


def box_loss(logits, target_box):
    scaled_box = jax.nn.sigmoid(logits) * 1000.0
    centre_x = scaled_box[:, 0]
    centre_y = scaled_box[:, 1]
    box_width = scaled_box[:, 2]
    box_height = scaled_box[:, 3]
    left_pred = centre_x - 0.5 * box_width
    right_pred = centre_x + 0.5 * box_width
    lower_pred = centre_y - 0.5 * box_height
    upper_pred = centre_y + 0.5 * box_height
    target = target_box.astype(jnp.float32)
    inner_width = soft_relu(soft_min(right_pred, target[:, 2]) - soft_max(left_pred, target[:, 0]))
    inner_height = soft_relu(
        soft_min(upper_pred, target[:, 3]) - soft_max(lower_pred, target[:, 1])
    )
    intersection_area = inner_width * inner_height
    target_area = (target[:, 2] - target[:, 0]) * (target[:, 3] - target[:, 1])
    union_area = box_width * box_height + target_area - intersection_area
    outer_width = soft_max(right_pred, target[:, 2]) - soft_min(left_pred, target[:, 0])
    outer_height = soft_max(upper_pred, target[:, 3]) - soft_min(lower_pred, target[:, 1])
    enclosing = outer_width * outer_height
    return loss_scale * jnp.mean(
        1.0 - intersection_area / union_area + (enclosing - union_area) / enclosing
    )


def head_pool(final_rows, head_gain, head_weight, prompt_length, keep_mask):
    row_count = keep_mask.shape[0]
    positions = jnp.arange(keep_mask.shape[1], dtype=jnp.int32)[None, :]
    starts = prompt_length[:, None]
    weights = (positions == starts - 1).astype(jnp.float32) + (positions >= starts).astype(
        jnp.float32
    ) * keep_mask.astype(jnp.float32)
    counts = jnp.sum(weights, axis=1)
    local_width = final_rows.shape[1]
    tokens = final_rows.astype(jnp.float32).reshape(row_count, keep_mask.shape[1], local_width)
    pooled = (
        jnp.einsum("rt,rtd->rd", weights, tokens, precision=lax.Precision.HIGHEST) / counts[:, None]
    )
    gain_cols = lax.dynamic_slice_in_dim(head_gain, column_start(local_width), local_width, 0)
    logit_part = jnp.dot(pooled * gain_cols, head_weight, precision=lax.Precision.HIGHEST)
    square_part = jnp.sum(pooled * pooled, axis=1, keepdims=True)
    return (weights, counts, pooled, gain_cols), jnp.concatenate([logit_part, square_part], axis=1)


def head_middle(pooled_state, totals, head_weight, head_bias, target_box):
    weights, counts, pooled, gain_cols = pooled_state
    full_width = pooled.shape[1] * tensor_size()
    inverse = lax.rsqrt(totals[:, 4] / full_width + epsilon)
    logits = totals[:, :4] * inverse[:, None] + head_bias

    def loss_of(logit_value):
        return box_loss(logit_value, target_box)

    loss_value, pullback = jax.vjp(loss_of, logits)
    logit_grad = pullback(jnp.ones((), jnp.float32))[0]
    scaled_grad = jnp.dot(logit_grad, head_weight.T, precision=lax.Precision.HIGHEST)
    unit_pooled = pooled * inverse[:, None]
    return (inverse, scaled_grad, unit_pooled), jnp.sum(unit_pooled * gain_cols * scaled_grad, axis=1)


def head_finish(pooled_state, middle_state, row_total, row_shape):
    weights, counts, pooled, gain_cols = pooled_state
    inverse, scaled_grad, unit_pooled = middle_state
    full_width = pooled.shape[1] * tensor_size()
    pooled_grad = inverse[:, None] * (
        gain_cols * scaled_grad - unit_pooled * row_total[:, None] / full_width
    )
    token_grad = (weights / counts[:, None])[:, :, None] * pooled_grad[:, None, :]
    return token_grad.reshape(row_shape).astype(jnp.bfloat16)


def per_device(
    forward_input,
    saved_last,
    saved_first,
    first_cotangent,
    section_entry,
    last_gain,
    last_up,
    last_down,
    first_gain,
    first_up,
    first_down,
    head_gain,
    head_weight,
    head_bias,
    prompt_length,
    keep_mask,
    target_box,
):
    section_index = lax.axis_index("section")
    opening = section_index == 0
    closing = section_index == lax.axis_size("section") - 1
    local_input = forward_input[0]
    width = local_input.shape[1]
    full_width = width * tensor_size()
    last_gain_cols = lax.dynamic_slice_in_dim(last_gain[0], column_start(width), width, 0)
    first_gain_cols = lax.dynamic_slice_in_dim(first_gain[0], column_start(width), width, 0)
    closing_saved = jnp.where(closing, local_input, saved_last[0])
    squares = row_sums(
        jnp.stack(
            [local_squares(local_input), local_squares(saved_first[0]), local_squares(closing_saved)]
        ),
        9,
    )
    squares, up_last, down_last, up_first, down_first = lax.optimization_barrier(
        (squares, last_up[0], last_down[0], first_up[0], first_down[0])
    )
    last_up_local, last_down_local, first_up_local, first_down_local = spread_weights(
        up_last, down_last, up_first, down_first
    )
    last_pre = layer_forward(local_input, squares[0], last_gain_cols, last_up_local, full_width)
    first_pre, first_grad_part, first_scaled, first_inverse = layer_back_partials(
        saved_first[0], squares[1], first_cotangent[0], first_gain_cols, first_up_local,
        first_down_local, full_width,
    )
    reduced = reduce_columns(jnp.stack([last_pre, first_pre, first_grad_part]), 3, jnp.float32)
    last_act = jax.nn.silu(reduced[0]).astype(jnp.bfloat16)
    first_pre_grad = pre_gradient(reduced[1], reduced[2])
    spread = gather_columns(jnp.stack([last_act, first_pre_grad]), 0)
    last_out = grouped_sum(spread[0], last_down_local, "rows")
    hidden_local = (local_input.astype(jnp.float32) + last_out).astype(jnp.bfloat16)
    first_norm_grad = grouped_sum(spread[1], first_up_local, "cols")
    rows = first_norm_grad.shape[0]
    pooled_state, head_part = head_pool(
        hidden_local, head_gain, head_weight, prompt_length, keep_mask
    )
    first_projection = back_projection(first_scaled, first_gain_cols, first_norm_grad)
    joined = row_sums(jnp.concatenate([first_projection, head_part.reshape(-1)]), 7)
    first_grad = back_finish(
        first_cotangent[0], first_norm_grad, first_scaled, first_inverse, first_gain_cols,
        full_width, joined[:rows],
    )
    arrived_local = shifted(hidden_local, "section", 1)
    returned = shifted(first_grad, "section", -1)
    middle_state, head_row = head_middle(
        pooled_state, joined[rows:].reshape(head_part.shape), head_weight, head_bias, target_box
    )
    entry_local = jnp.where(opening, section_entry, arrived_local)
    late_joined = row_sums(jnp.concatenate([local_squares(entry_local), head_row]), 10)
    entry_squares = late_joined[:rows]
    head_grad = head_finish(pooled_state, middle_state, late_joined[rows:], hidden_local.shape)
    cotangent = jnp.where(closing, head_grad, returned)
    first_pre_late = layer_forward(entry_local, entry_squares, first_gain_cols, first_up_local, full_width)
    last_pre_late, last_grad_part, last_scaled, last_inverse = layer_back_partials(
        closing_saved, squares[2], cotangent, last_gain_cols, last_up_local, last_down_local,
        full_width,
    )
    reduced_late = reduce_columns(
        jnp.stack([first_pre_late, last_pre_late, last_grad_part]), 4, jnp.float32
    )
    first_act = jax.nn.silu(reduced_late[0]).astype(jnp.bfloat16)
    last_pre_grad = pre_gradient(reduced_late[1], reduced_late[2])
    spread_late = gather_columns(jnp.stack([first_act, last_pre_grad]), 1)
    first_out = grouped_sum(spread_late[0], first_down_local, "rows")
    layer_output = (entry_local.astype(jnp.float32) + first_out).astype(jnp.bfloat16)
    last_norm_grad = grouped_sum(spread_late[1], last_up_local, "cols")
    last_total = row_sums(back_projection(last_scaled, last_gain_cols, last_norm_grad), 8)
    input_gradient = back_finish(
        cotangent, last_norm_grad, last_scaled, last_inverse, last_gain_cols, full_width, last_total
    )
    return (layer_output[None], input_gradient[None])


def solution(mesh):
    sections = mesh.shape["section"]
    tensors = mesh.shape["tensor"]
    split = Mesh(mesh.devices.reshape(sections, tensors // 2, 2), ("section", "ty", "tz"))
    rows = P("section", None, TENSOR)
    placed = (
        rows,
        rows,
        rows,
        rows,
        P(None, TENSOR),
        P("section", None),
        rows,
        P("section", TENSOR, None),
        P("section", None),
        rows,
        P("section", TENSOR, None),
        P(),
        P(TENSOR, None),
        P(),
        P(),
        P(),
        P(),
    )
    return jax.shard_map(
        per_device,
        mesh=split,
        in_specs=placed,
        out_specs=(rows, rows),
        check_vma=False,
    )
```

```python
import functools

import jax
import jax.numpy as jnp
from jax import lax
from jax.experimental import pallas as pl
from jax.experimental.pallas import tpu as pltpu
from jax.sharding import Mesh
from jax.sharding import PartitionSpec as P

epsilon = 1e-06
softness = 4.0
loss_scale = 4096.0
TENSOR = ("ty", "tz")


def shifted(value, axis, steps):
    count = lax.axis_size(axis)
    initial, last = (max(0, -steps), min(count, count - steps))
    return lax.ppermute(value, axis, [(source, source + steps) for source in range(initial, last)])


def tensor_size():
    return lax.axis_size("ty") * lax.axis_size("tz")


def tensor_index():
    return lax.axis_index("ty") * lax.axis_size("tz") + lax.axis_index("tz")


def unit_rows(values):
    values = values.astype(jnp.float32)
    inverse = lax.rsqrt(jnp.mean(values * values, axis=-1, keepdims=True) + epsilon)
    return (values * inverse, inverse)


def column_start(local_width):
    return tensor_index() * local_width


def column_slice(full_rows, local_width):
    return lax.dynamic_slice_in_dim(full_rows, column_start(local_width), local_width, 1)


MESH_ID = pl.DeviceIdType.MESH


def gather_kernel(ny, nz, x_ref, out_ref, send_sems, recv_sems):
    width = x_ref.shape[2]
    ty, tz = lax.axis_index("ty"), lax.axis_index("tz")
    me = ty * nz + tz
    partner_z = 1 - tz
    partner = ty * nz + partner_z
    y_peers = [lax.rem(ty + step, ny) for step in range(1, ny)]
    section = lax.axis_index("section")

    def device(y, z):
        return (section, y, z)

    def cols(index):
        return pl.ds(pl.multiple_of(index * width, width), width)

    barrier = pltpu.get_barrier_semaphore()
    pl.semaphore_signal(barrier, inc=1, device_id=device(ty, partner_z), device_id_type=MESH_ID)
    for y in y_peers:
        pl.semaphore_signal(barrier, inc=1, device_id=device(y, tz), device_id_type=MESH_ID)
    pl.semaphore_wait(barrier, ny)

    sends = [
        pltpu.make_async_remote_copy(
            src_ref=x_ref,
            dst_ref=out_ref.at[:, :, cols(me)],
            send_sem=send_sems.at[0],
            recv_sem=recv_sems.at[me],
            device_id=device(ty, partner_z),
            device_id_type=MESH_ID,
        )
    ]
    for number, y in enumerate(y_peers):
        sends.append(
            pltpu.make_async_remote_copy(
                src_ref=x_ref,
                dst_ref=out_ref.at[:, :, cols(me)],
                send_sem=send_sems.at[1 + number],
                recv_sem=recv_sems.at[me],
                device_id=device(y, tz),
                device_id_type=MESH_ID,
            )
        )
    for copy in sends:
        copy.start()
    out_ref[:, :, cols(me)] = x_ref[...]
    pltpu.make_async_remote_copy(
        src_ref=x_ref,
        dst_ref=out_ref.at[:, :, cols(partner)],
        send_sem=send_sems.at[0],
        recv_sem=recv_sems.at[partner],
        device_id=device(ty, partner_z),
        device_id_type=MESH_ID,
    ).wait_recv()
    forwards = []
    for number, y in enumerate(y_peers):
        forwards.append(
            pltpu.make_async_remote_copy(
                src_ref=out_ref.at[:, :, cols(partner)],
                dst_ref=out_ref.at[:, :, cols(partner)],
                send_sem=send_sems.at[ny + number],
                recv_sem=recv_sems.at[partner],
                device_id=device(y, tz),
                device_id_type=MESH_ID,
            )
        )
    for copy in forwards:
        copy.start()
    for y in y_peers:
        for z in range(nz):
            source = y * nz + z
            pltpu.make_async_remote_copy(
                src_ref=x_ref,
                dst_ref=out_ref.at[:, :, cols(source)],
                send_sem=send_sems.at[0],
                recv_sem=recv_sems.at[source],
                device_id=device(y, z),
                device_id_type=MESH_ID,
            ).wait_recv()
    for copy in sends + forwards:
        copy.wait_send()


def gather_columns(local_rows, collective):
    k, rows, width = local_rows.shape
    ny, nz = lax.axis_size("ty"), lax.axis_size("tz")
    full = width * ny * nz
    moved = local_rows.size * local_rows.dtype.itemsize * 7
    return pl.pallas_call(
        functools.partial(gather_kernel, ny, nz),
        out_shape=jax.ShapeDtypeStruct((k, rows, full), local_rows.dtype),
        in_specs=[pl.BlockSpec(memory_space=pltpu.VMEM)],
        out_specs=pl.BlockSpec(memory_space=pltpu.VMEM),
        scratch_shapes=[
            pltpu.SemaphoreType.DMA((2 * ny - 1,)),
            pltpu.SemaphoreType.DMA((ny * nz,)),
        ],
        compiler_params=pltpu.CompilerParams(
            collective_id=collective, has_side_effects=True, vmem_limit_bytes=48 * 1024 * 1024
        ),
        cost_estimate=pl.CostEstimate(flops=0, transcendentals=0, bytes_accessed=moved),
    )(local_rows)


def scatter_kernel(ny, nz, part_ref, out_ref, stage, z_send, z_recv, send_sems, recv_sems, z_sems):
    k, rows, width = out_ref.shape
    pair = nz * width
    ty, tz = lax.axis_index("ty"), lax.axis_index("tz")
    partner_z = 1 - tz
    section = lax.axis_index("section")
    chunk = 32

    def device(y, z):
        return (section, y, z)

    barrier = pltpu.get_barrier_semaphore()
    pl.semaphore_signal(barrier, inc=1, device_id=device(ty, partner_z), device_id_type=MESH_ID)
    for step in range(1, ny):
        pl.semaphore_signal(
            barrier, inc=1, device_id=device(lax.rem(ty + step, ny), tz), device_id_type=MESH_ID
        )
    pl.semaphore_wait(barrier, ny)

    sends = []
    for step in sorted(range(1, ny), key=lambda s: -min(s, ny - s)):
        peer = lax.rem(ty + step, ny)
        copy = pltpu.make_async_remote_copy(
            src_ref=part_ref.at[:, :, pl.ds(pl.multiple_of(peer * pair, pair), pair)],
            dst_ref=stage.at[ny - step - 1],
            send_sem=send_sems.at[step - 1],
            recv_sem=recv_sems.at[ny - step - 1],
            device_id=device(peer, tz),
            device_id_type=MESH_ID,
        )
        copy.start()
        sends.append(copy)
    for slot in range(ny - 1):
        pltpu.make_async_remote_copy(
            src_ref=stage.at[slot],
            dst_ref=stage.at[slot],
            send_sem=send_sems.at[0],
            recv_sem=recv_sems.at[slot],
            device_id=device(ty, partner_z),
            device_id_type=MESH_ID,
        ).wait_recv()

    def add_terms(z, target):
        own = pl.multiple_of((ty * nz + z) * width, width)
        inside = pl.multiple_of(z * width, width)

        def body(step, carry):
            plane = step // (rows // chunk)
            row = pl.multiple_of((step % (rows // chunk)) * chunk, chunk)
            total = part_ref[plane, pl.ds(row, chunk), pl.ds(own, width)].astype(jnp.float32)
            for slot in range(ny - 1):
                total += stage[slot, plane, pl.ds(row, chunk), pl.ds(inside, width)].astype(
                    jnp.float32
                )
            target(plane, row, total)
            return carry

        lax.fori_loop(0, k * (rows // chunk), body, 0)

    def to_send(plane, row, total):
        z_send[plane, pl.ds(row, chunk), :] = total

    add_terms(partner_z, to_send)
    z_copy = pltpu.make_async_remote_copy(
        src_ref=z_send,
        dst_ref=z_recv,
        send_sem=z_sems.at[0],
        recv_sem=z_sems.at[1],
        device_id=device(ty, partner_z),
        device_id_type=MESH_ID,
    )
    z_copy.start()

    def to_out(plane, row, total):
        out_ref[plane, pl.ds(row, chunk), :] = total

    add_terms(tz, to_out)
    z_copy.wait_recv()
    out_ref[...] += z_recv[...]
    z_copy.wait_send()
    for copy in sends:
        copy.wait_send()


def reduce_columns(partial_rows, collective, term_type=jnp.bfloat16):
    k, rows, full = partial_rows.shape
    ny, nz = lax.axis_size("ty"), lax.axis_size("tz")
    width = full // (ny * nz)
    terms = partial_rows.astype(term_type)
    moved = terms.size * terms.dtype.itemsize
    return pl.pallas_call(
        functools.partial(scatter_kernel, ny, nz),
        out_shape=jax.ShapeDtypeStruct((k, rows, width), jnp.float32),
        in_specs=[pl.BlockSpec(memory_space=pltpu.VMEM)],
        out_specs=pl.BlockSpec(memory_space=pltpu.VMEM),
        scratch_shapes=[
            pltpu.VMEM((ny - 1, k, rows, nz * width), term_type),
            pltpu.VMEM((k, rows, width), jnp.float32),
            pltpu.VMEM((k, rows, width), jnp.float32),
            pltpu.SemaphoreType.DMA((ny - 1,)),
            pltpu.SemaphoreType.DMA((ny - 1,)),
            pltpu.SemaphoreType.DMA((2,)),
        ],
        compiler_params=pltpu.CompilerParams(
            collective_id=collective, has_side_effects=True, vmem_limit_bytes=56 * 1024 * 1024
        ),
        cost_estimate=pl.CostEstimate(flops=terms.size, transcendentals=0, bytes_accessed=moved),
    )(terms)


def sum_kernel(ny, nz, v_ref, out_ref, slots, send_sems, recv_sems):
    ty, tz = lax.axis_index("ty"), lax.axis_index("tz")
    me = ty * nz + tz
    section = lax.axis_index("section")
    peers = [(lax.rem(ty + dy, ny), lax.rem(tz + dz, nz)) for dy in range(ny) for dz in range(nz)][1:]

    barrier = pltpu.get_barrier_semaphore()
    for y, z in peers:
        pl.semaphore_signal(barrier, inc=1, device_id=(section, y, z), device_id_type=MESH_ID)
    pl.semaphore_wait(barrier, len(peers))
    sends = []
    for number, (y, z) in enumerate(peers):
        copy = pltpu.make_async_remote_copy(
            src_ref=v_ref,
            dst_ref=slots.at[me],
            send_sem=send_sems.at[number],
            recv_sem=recv_sems.at[me],
            device_id=(section, y, z),
            device_id_type=MESH_ID,
        )
        copy.start()
        sends.append(copy)
    slots[me] = v_ref[...]
    for y, z in peers:
        source = y * nz + z
        pltpu.make_async_remote_copy(
            src_ref=v_ref,
            dst_ref=slots.at[source],
            send_sem=send_sems.at[0],
            recv_sem=recv_sems.at[source],
            device_id=(section, y, z),
            device_id_type=MESH_ID,
        ).wait_recv()
    total = slots[0]
    for source in range(1, ny * nz):
        total = total + slots[source]
    out_ref[...] = total
    for copy in sends:
        copy.wait_send()


def row_sums(values, collective):
    shape = values.shape
    flat = values.reshape(-1).astype(jnp.float32)
    lanes = 128
    padded = -(-flat.shape[0] // lanes) * lanes
    rows = jnp.pad(flat, (0, padded - flat.shape[0])).reshape(padded // lanes, lanes)
    ny, nz = lax.axis_size("ty"), lax.axis_size("tz")
    summed = pl.pallas_call(
        functools.partial(sum_kernel, ny, nz),
        out_shape=jax.ShapeDtypeStruct(rows.shape, jnp.float32),
        in_specs=[pl.BlockSpec(memory_space=pltpu.VMEM)],
        out_specs=pl.BlockSpec(memory_space=pltpu.VMEM),
        scratch_shapes=[
            pltpu.VMEM((ny * nz,) + rows.shape, jnp.float32),
            pltpu.SemaphoreType.DMA((ny * nz - 1,)),
            pltpu.SemaphoreType.DMA((ny * nz,)),
        ],
        compiler_params=pltpu.CompilerParams(collective_id=collective, has_side_effects=True),
        cost_estimate=pl.CostEstimate(flops=rows.size * 8, transcendentals=0, bytes_accessed=rows.size * 64),
    )(rows)
    return summed.reshape(-1)[: flat.shape[0]].reshape(shape)


def spread_weights(up_matrix, down_matrix):
    n = tensor_size()
    full, hidden = up_matrix.shape
    width = full // n
    up_blocks = lax.all_to_all(up_matrix.reshape(n, width, hidden), TENSOR, 0, 0, tiled=True)
    up_local = up_blocks.transpose(1, 0, 2).reshape(width, n * hidden)
    down_blocks = down_matrix.reshape(hidden, n, width).transpose(1, 0, 2)
    down_local = lax.all_to_all(down_blocks, TENSOR, 0, 0, tiled=True).reshape(n * hidden, width)
    return up_local, down_local


def grouped_sum(left, right, contract):
    n = tensor_size()
    rows = left.shape[0]
    hidden = left.shape[1] // n
    left_groups = left.reshape(rows, n, hidden)
    if contract == "rows":
        right_groups = right.reshape(n, hidden, right.shape[1])
        terms = jnp.einsum("tgk,gkf->gtf", left_groups, right_groups, preferred_element_type=jnp.float32)
    else:
        right_groups = right.reshape(right.shape[0], n, hidden)
        terms = jnp.einsum("tgk,fgk->gtf", left_groups, right_groups, preferred_element_type=jnp.float32)
    return jnp.sum(terms.astype(jnp.bfloat16).astype(jnp.float32), axis=0)


def normed_rows(local_rows, total_squares, gain_cols, full_width):
    values = local_rows.astype(jnp.float32)
    inverse = lax.rsqrt(total_squares[:, None] / full_width + epsilon)
    scaled = values * inverse
    return scaled, inverse, (scaled * gain_cols).astype(jnp.bfloat16)


def local_squares(local_rows):
    values = local_rows.astype(jnp.float32)
    return jnp.sum(values * values, axis=-1)


def layer_forward(local_rows, squares, gain_cols, up_local, full_width):
    scaled, inverse, normed = normed_rows(local_rows, squares, gain_cols, full_width)
    return jnp.dot(normed, up_local, preferred_element_type=jnp.float32)


def layer_back_partials(saved_rows, squares, cotangent, gain_cols, up_local, down_local, full_width):
    scaled, inverse, normed = normed_rows(saved_rows, squares, gain_cols, full_width)
    pre_part = jnp.dot(normed, up_local, preferred_element_type=jnp.float32)
    grad_part = lax.dot_general(
        cotangent, down_local, (((1,), (1,)), ((), ())), preferred_element_type=jnp.float32
    )
    return pre_part, grad_part, scaled, inverse


def pre_gradient(pre_act, act_grad):
    sigmoid_pre = jax.nn.sigmoid(pre_act)
    return (act_grad * sigmoid_pre * (1.0 + pre_act * (1.0 - sigmoid_pre))).astype(jnp.bfloat16)


def back_projection(scaled, gain_cols, norm_grad):
    return jnp.sum(scaled * gain_cols * norm_grad, axis=1)


def back_finish(cotangent, norm_grad, scaled, inverse, gain_cols, full_width, row_total):
    result = cotangent.astype(jnp.float32) + inverse * (
        gain_cols * norm_grad - scaled * row_total[:, None] / full_width
    )
    return result.astype(jnp.bfloat16)


def soft_min(first, second):
    return 0.5 * (
        first + second - jnp.sqrt((first - second) * (first - second) + softness * softness)
    )


def soft_max(first, second):
    return 0.5 * (
        first + second + jnp.sqrt((first - second) * (first - second) + softness * softness)
    )


def soft_relu(difference):
    return 0.5 * (difference + jnp.sqrt(difference * difference + softness * softness))


def box_loss(logits, target_box):
    scaled_box = jax.nn.sigmoid(logits) * 1000.0
    centre_x = scaled_box[:, 0]
    centre_y = scaled_box[:, 1]
    box_width = scaled_box[:, 2]
    box_height = scaled_box[:, 3]
    left_pred = centre_x - 0.5 * box_width
    right_pred = centre_x + 0.5 * box_width
    lower_pred = centre_y - 0.5 * box_height
    upper_pred = centre_y + 0.5 * box_height
    target = target_box.astype(jnp.float32)
    inner_width = soft_relu(soft_min(right_pred, target[:, 2]) - soft_max(left_pred, target[:, 0]))
    inner_height = soft_relu(
        soft_min(upper_pred, target[:, 3]) - soft_max(lower_pred, target[:, 1])
    )
    intersection_area = inner_width * inner_height
    target_area = (target[:, 2] - target[:, 0]) * (target[:, 3] - target[:, 1])
    union_area = box_width * box_height + target_area - intersection_area
    outer_width = soft_max(right_pred, target[:, 2]) - soft_min(left_pred, target[:, 0])
    outer_height = soft_max(upper_pred, target[:, 3]) - soft_min(lower_pred, target[:, 1])
    enclosing = outer_width * outer_height
    return loss_scale * jnp.mean(
        1.0 - intersection_area / union_area + (enclosing - union_area) / enclosing
    )


def head_pool(final_rows, head_gain, head_weight, prompt_length, keep_mask):
    row_count = keep_mask.shape[0]
    positions = jnp.arange(keep_mask.shape[1], dtype=jnp.int32)[None, :]
    starts = prompt_length[:, None]
    weights = (positions == starts - 1).astype(jnp.float32) + (positions >= starts).astype(
        jnp.float32
    ) * keep_mask.astype(jnp.float32)
    counts = jnp.sum(weights, axis=1)
    local_width = final_rows.shape[1]
    tokens = final_rows.astype(jnp.float32).reshape(row_count, keep_mask.shape[1], local_width)
    pooled = (
        jnp.einsum("rt,rtd->rd", weights, tokens, precision=lax.Precision.HIGHEST) / counts[:, None]
    )
    gain_cols = lax.dynamic_slice_in_dim(head_gain, column_start(local_width), local_width, 0)
    logit_part = jnp.dot(pooled * gain_cols, head_weight, precision=lax.Precision.HIGHEST)
    square_part = jnp.sum(pooled * pooled, axis=1, keepdims=True)
    return (weights, counts, pooled, gain_cols), jnp.concatenate([logit_part, square_part], axis=1)


def head_middle(pooled_state, totals, head_weight, head_bias, target_box):
    weights, counts, pooled, gain_cols = pooled_state
    full_width = pooled.shape[1] * tensor_size()
    inverse = lax.rsqrt(totals[:, 4] / full_width + epsilon)
    logits = totals[:, :4] * inverse[:, None] + head_bias

    def loss_of(logit_value):
        return box_loss(logit_value, target_box)

    loss_value, pullback = jax.vjp(loss_of, logits)
    logit_grad = pullback(jnp.ones((), jnp.float32))[0]
    scaled_grad = jnp.dot(logit_grad, head_weight.T, precision=lax.Precision.HIGHEST)
    unit_pooled = pooled * inverse[:, None]
    return (inverse, scaled_grad, unit_pooled), jnp.sum(unit_pooled * gain_cols * scaled_grad, axis=1)


def head_finish(pooled_state, middle_state, row_total, row_shape):
    weights, counts, pooled, gain_cols = pooled_state
    inverse, scaled_grad, unit_pooled = middle_state
    full_width = pooled.shape[1] * tensor_size()
    pooled_grad = inverse[:, None] * (
        gain_cols * scaled_grad - unit_pooled * row_total[:, None] / full_width
    )
    token_grad = (weights / counts[:, None])[:, :, None] * pooled_grad[:, None, :]
    return token_grad.reshape(row_shape).astype(jnp.bfloat16)


def per_device(
    forward_input,
    saved_last,
    saved_first,
    first_cotangent,
    section_entry,
    last_gain,
    last_up,
    last_down,
    first_gain,
    first_up,
    first_down,
    head_gain,
    head_weight,
    head_bias,
    prompt_length,
    keep_mask,
    target_box,
):
    section_index = lax.axis_index("section")
    opening = section_index == 0
    closing = section_index == lax.axis_size("section") - 1
    local_input = forward_input[0]
    width = local_input.shape[1]
    full_width = width * tensor_size()
    last_gain_cols = lax.dynamic_slice_in_dim(last_gain[0], column_start(width), width, 0)
    first_gain_cols = lax.dynamic_slice_in_dim(first_gain[0], column_start(width), width, 0)
    closing_saved = jnp.where(closing, local_input, saved_last[0])
    squares = row_sums(
        jnp.stack(
            [local_squares(local_input), local_squares(saved_first[0]), local_squares(closing_saved)]
        ),
        9,
    )
    squares, up_last, down_last, up_first, down_first = lax.optimization_barrier(
        (squares, last_up[0], last_down[0], first_up[0], first_down[0])
    )
    last_up_local, last_down_local = spread_weights(up_last, down_last)
    first_up_local, first_down_local = spread_weights(up_first, down_first)
    last_pre = layer_forward(local_input, squares[0], last_gain_cols, last_up_local, full_width)
    first_pre, first_grad_part, first_scaled, first_inverse = layer_back_partials(
        saved_first[0], squares[1], first_cotangent[0], first_gain_cols, first_up_local,
        first_down_local, full_width,
    )
    reduced = reduce_columns(jnp.stack([last_pre, first_pre, first_grad_part]), 3, jnp.float32)
    last_act = jax.nn.silu(reduced[0]).astype(jnp.bfloat16)
    first_pre_grad = pre_gradient(reduced[1], reduced[2])
    spread = gather_columns(jnp.stack([last_act, first_pre_grad]), 0)
    last_out = grouped_sum(spread[0], last_down_local, "rows")
    hidden_local = (local_input.astype(jnp.float32) + last_out).astype(jnp.bfloat16)
    first_norm_grad = grouped_sum(spread[1], first_up_local, "cols")
    rows = first_norm_grad.shape[0]
    pooled_state, head_part = head_pool(
        hidden_local, head_gain, head_weight, prompt_length, keep_mask
    )
    first_projection = back_projection(first_scaled, first_gain_cols, first_norm_grad)
    joined = row_sums(jnp.concatenate([first_projection, head_part.reshape(-1)]), 7)
    first_grad = back_finish(
        first_cotangent[0], first_norm_grad, first_scaled, first_inverse, first_gain_cols,
        full_width, joined[:rows],
    )
    arrived_local = shifted(hidden_local, "section", 1)
    returned = shifted(first_grad, "section", -1)
    middle_state, head_row = head_middle(
        pooled_state, joined[rows:].reshape(head_part.shape), head_weight, head_bias, target_box
    )
    entry_local = jnp.where(opening, section_entry, arrived_local)
    late_joined = row_sums(jnp.concatenate([local_squares(entry_local), head_row]), 10)
    entry_squares = late_joined[:rows]
    head_grad = head_finish(pooled_state, middle_state, late_joined[rows:], hidden_local.shape)
    cotangent = jnp.where(closing, head_grad, returned)
    first_pre_late = layer_forward(entry_local, entry_squares, first_gain_cols, first_up_local, full_width)
    last_pre_late, last_grad_part, last_scaled, last_inverse = layer_back_partials(
        closing_saved, squares[2], cotangent, last_gain_cols, last_up_local, last_down_local,
        full_width,
    )
    reduced_late = reduce_columns(
        jnp.stack([first_pre_late, last_pre_late, last_grad_part]), 4, jnp.float32
    )
    first_act = jax.nn.silu(reduced_late[0]).astype(jnp.bfloat16)
    last_pre_grad = pre_gradient(reduced_late[1], reduced_late[2])
    spread_late = gather_columns(jnp.stack([first_act, last_pre_grad]), 1)
    first_out = grouped_sum(spread_late[0], first_down_local, "rows")
    layer_output = (entry_local.astype(jnp.float32) + first_out).astype(jnp.bfloat16)
    last_norm_grad = grouped_sum(spread_late[1], last_up_local, "cols")
    last_total = row_sums(back_projection(last_scaled, last_gain_cols, last_norm_grad), 8)
    input_gradient = back_finish(
        cotangent, last_norm_grad, last_scaled, last_inverse, last_gain_cols, full_width, last_total
    )
    return (layer_output[None], input_gradient[None])


def solution(mesh):
    sections = mesh.shape["section"]
    tensors = mesh.shape["tensor"]
    split = Mesh(mesh.devices.reshape(sections, tensors // 2, 2), ("section", "ty", "tz"))
    rows = P("section", None, TENSOR)
    placed = (
        rows,
        rows,
        rows,
        rows,
        P(None, TENSOR),
        P("section", None),
        rows,
        P("section", TENSOR, None),
        P("section", None),
        rows,
        P("section", TENSOR, None),
        P(),
        P(TENSOR, None),
        P(),
        P(),
        P(),
        P(),
    )
    return jax.shard_map(
        per_device,
        mesh=split,
        in_specs=placed,
        out_specs=(rows, rows),
        check_vma=False,
    )
```
